256 devices in a mesh: ctx: 32 (over x, z_hi, core), tp: 8 (over z_lo, y).
Axes of the slice: x: 4, y: 4, z: 8 (z_hi: 4, z_lo: 2; z = z_hi * 2 + z_lo), core: 2. Of those that a mesh axis runs over, the one named last changes fastest.
Arguments:
- tokens: bfloat16 [32768, 5120], P(('ctx', 'tp')), may hold values from -6 to 6
- queries: bfloat16 [32768, 3072], P('ctx', 'tp'), may hold values from -500 to 500
- w_key: bfloat16 [5120, 3072], P('ctx', 'tp'), may hold values from -0.078125 to 0.078125
- w_value: bfloat16 [5120, 3072], P('ctx', 'tp'), may hold values from -0.078125 to 0.078125
- tile_slot: int32 [128], replicated, may hold values from 0 to 127, as said below
- neighbour_tile: int32 [128, 6], replicated, may hold values from 0 to 127, as said below
- slab_start: int32 [128, 6], replicated, may hold values from 0 to 192
- slab_length: int32 [128, 6], replicated, may hold values from 0 to 64, as said below
- window_low: int32 [128, 6], replicated, may hold values from 0 to 127, as said below
- window_high: int32 [128, 6], replicated, may hold values from 129 to 256
Outputs:
- attended: bfloat16 [32768, 3072], P('ctx', 'tp')
The draws below stay inside these ranges and needn't reach their ends.
Inputs may be any that keep to these rules, and one draw needn't show every extreme that they name: `tile_slot`: the slots form a permutation, and tile t has a slot in the block of 4 slots starting at (t // 4) * 4. `neighbour_tile`: call b = t // 4 the block of tile t; blocks b and b + 1 modulo 128 // 4 are adjacent. The first clip is the tiles of blocks 128 // 16 to 23, the second clip the other tiles. Each entry names a tile of the same clip whose block is the own one or adjacent to it; at most 2 entries of a tile name tiles of the previous block, and at most 2 of the next; entries naming the own block name other tiles than the own one. `slab_length`: zero leaves the entry unused. window_low is below window_high of the same entry.
All inputs are finite; a program needn't handle non-finite values.
Results may differ from the reference program's by a relative error of at most 0.0065.
The reference program's roundings to bfloat16 on the way (of `key`, `value` and `probability`) count: a program that leaves them out, or rounds other values in their place, can miss the bound.
Values may be sent and summed in bfloat16 or wider, within the bound.
No kernel may reach another device: no remote copies, remote signals or barrier semaphores. Data moves between devices by JAX's collectives and lax.ppermute only.
A program may use at most 64 MiB of HBM per device.

```python
import math
import jax
import jax.numpy as jnp
from jax import lax

D = 5120
HEADS = 24
HD = 128
TILE = 256
NB = 6
SLAB = 64
TPD = 4
TILES = 128
ROWS = 32768


def linked_tables(key):
    subkeys = jax.random.split(jax.random.fold_in(key, 7), 10)
    device_count = TILES // TPD
    half_count = device_count // 2
    quarter = device_count // 4
    tile_index = jnp.arange(TILES, dtype=jnp.int32)
    device = tile_index // TPD
    position = tile_index % TPD
    shifted = (device - quarter) % device_count
    clip_first = shifted // half_count * half_count
    clip_last = clip_first + half_count - 1
    chosen = jax.random.randint(subkeys[0], (device_count,), 0, TPD)
    forced = (position == chosen[device])[:, None]
    column = jnp.arange(NB, dtype=jnp.int32)[None, :]
    raw_side = jax.random.randint(subkeys[1], (TILES, NB), 0, 2)
    direction = jnp.where(column < 2, -raw_side, jnp.where(column < 4, raw_side, 0))
    direction = jnp.where(forced, jnp.where(column < 2, -1, jnp.where(column < 4, 1, 0)), direction)
    target_shifted = shifted[:, None] + direction
    outside = (target_shifted < clip_first[:, None]) | (target_shifted > clip_last[:, None])
    direction = jnp.where(outside, 0, direction)
    random_pos = jax.random.randint(subkeys[2], (TILES, NB), 0, TPD)
    local_step = jax.random.randint(subkeys[3], (TILES, NB), 1, TPD)
    target_pos = jnp.where(direction == 0, (position[:, None] + local_step) % TPD, random_pos)
    target_device = (device[:, None] + direction) % device_count
    neighbour = target_device * TPD + target_pos
    length = jax.random.randint(subkeys[4], (TILES, NB), 1, SLAB + 1)
    unused = jax.random.randint(subkeys[5], (TILES, NB), 0, 4) == 0
    length = jnp.where(unused, 0, length)
    length = jnp.where(forced, jnp.where(column == 4, 0, SLAB), length)
    slab_first = jax.random.randint(subkeys[6], (TILES, NB), 0, TILE - SLAB + 1)
    slab_first = jnp.where(forced, jnp.where(column < 2, 0, TILE - SLAB), slab_first)
    low_bound = jax.random.randint(subkeys[7], (TILES, NB), 0, TILE // 2)
    high_bound = jax.random.randint(subkeys[8], (TILES, NB), TILE // 2 + 1, TILE + 1)
    low_bound = jnp.where(forced, jnp.where(column < 5, 0, TILE // 2 - 1), low_bound)
    high_bound = jnp.where(forced, jnp.where(column < 5, TILE, TILE // 2 + 1), high_bound)
    order_score = jax.random.randint(subkeys[9], (device_count, TPD), 0, 1 << 20) * TPD + jnp.arange(TPD, dtype=jnp.int32)[None, :]
    within = jnp.argsort(order_score, axis=1).astype(jnp.int32)
    slots = device * TPD + within[device, position]
    return (slots.astype(jnp.int32), neighbour.astype(jnp.int32), slab_first.astype(jnp.int32), length.astype(jnp.int32), low_bound.astype(jnp.int32), high_bound.astype(jnp.int32))


def draw_tile_slot(key, part):
    return linked_tables(key)[0]


def draw_neighbour_tile(key, part):
    return linked_tables(key)[1]


def draw_slab_start(key, part):
    return linked_tables(key)[2]


def draw_slab_length(key, part):
    return linked_tables(key)[3]


def draw_window_low(key, part):
    return linked_tables(key)[4]


def draw_window_high(key, part):
    return linked_tables(key)[5]


def draw_queries(key, part):
    normal = jnp.clip(jax.random.normal(key, (ROWS, HEADS * HD), jnp.float32), -5.0, 5.0)
    return normal.astype(jnp.bfloat16)


def shard_levels(key, extent, shards, low, top_value):
    def one(axis_at, shards_of):
        draws = jax.random.uniform(jax.random.fold_in(jax.random.fold_in(key, 6), axis_at), (shards_of,), jnp.float32, low / len(shards), top_value / len(shards))
        return jnp.repeat(jnp.exp(draws), extent[axis_at] // shards_of).reshape((-1,) + (1,) * (len(extent) - axis_at - 1))

    gain = one(*shards[0])
    for cut in shards[1:]:
        gain = gain * one(*cut)
    return gain


def centred(stream_key, extent, scale, reach, shards=(), held_as=jnp.bfloat16):
    factor_of = shard_levels(stream_key, extent, shards, -0.22, 0.18) if shards else 1.0
    drawn = jax.random.normal(stream_key, extent, jnp.float32) * scale * factor_of
    return jnp.minimum(jnp.maximum(drawn, -reach), reach).astype(held_as)


def setup_inputs(seed: int = 0) -> dict:
    streams_of = jax.random.split(jax.random.key(seed), 11)
    return {
        "tokens": centred(streams_of[0], (ROWS, D), 1.0, 6.0, ((0, 256),)),
        "queries": draw_queries(jax.random.fold_in(streams_of[10], 71), 0),
        "w_key": centred(streams_of[2], (D, HEADS * HD), D ** -0.5, 0.078125, ((0, 32), (1, 8))),
        "w_value": centred(streams_of[3], (D, HEADS * HD), D ** -0.5, 0.078125, ((0, 32), (1, 8))),
        "tile_slot": draw_tile_slot(jax.random.fold_in(streams_of[10], 71), 0),
        "neighbour_tile": draw_neighbour_tile(jax.random.fold_in(streams_of[10], 71), 0),
        "slab_start": draw_slab_start(jax.random.fold_in(streams_of[10], 71), 0),
        "slab_length": draw_slab_length(jax.random.fold_in(streams_of[10], 71), 0),
        "window_low": draw_window_low(jax.random.fold_in(streams_of[10], 71), 0),
        "window_high": draw_window_high(jax.random.fold_in(streams_of[10], 71), 0),
    }


def attend_tile(query_tile, key_rows, value_rows, allowed, head_count):
    query_heads = query_tile.astype(jnp.float32).reshape(TILE, head_count, HD)
    key_heads = key_rows.astype(jnp.float32).reshape(-1, head_count, HD)
    value_heads = value_rows.astype(jnp.float32).reshape(-1, head_count, HD)
    scores = jnp.einsum('rhd,shd->hrs', query_heads, key_heads) * (1.0 / math.sqrt(HD))
    scores = jnp.where(allowed[None, :, :], scores, -jnp.inf)
    row_top = lax.optimization_barrier(jnp.max(scores, axis=-1, keepdims=True))
    weights = jnp.exp(scores - row_top)
    row_total = lax.optimization_barrier(jnp.sum(weights, axis=-1, keepdims=True))
    probability = lax.optimization_barrier(weights.astype(jnp.bfloat16))
    weighted = jnp.einsum('hrs,shd->rhd', probability.astype(jnp.float32), value_heads)
    result = weighted / jnp.transpose(row_total, (1, 0, 2))
    return result.reshape(TILE, head_count * HD).astype(jnp.bfloat16)

def reference(tokens, queries, w_key, w_value, tile_slot, neighbour_tile, slab_start, slab_length, window_low, window_high):
    key = jnp.dot(tokens, w_key, preferred_element_type=jnp.float32).astype(jnp.bfloat16)
    value = jnp.dot(tokens, w_value, preferred_element_type=jnp.float32).astype(jnp.bfloat16)
    head_count = w_key.shape[1] // HD
    tile_count = tile_slot.shape[0]
    slot_tile = jnp.argsort(tile_slot).astype(jnp.int32)
    offsets = jnp.arange(SLAB, dtype=jnp.int32)
    own_rows = jnp.arange(TILE, dtype=jnp.int32)

    def one_slot(slot_id):
        tile_id = slot_tile[slot_id]
        sources = tile_slot[neighbour_tile[tile_id]].astype(jnp.int32)
        firsts = sources * TILE + slab_start[tile_id].astype(jnp.int32)
        slab_rows = (firsts[:, None] + offsets[None, :]).reshape(-1)
        all_rows = jnp.concatenate([slot_id * TILE + own_rows, slab_rows]).astype(jnp.int32)
        key_rows = jnp.take(key, all_rows, axis=0)
        value_rows = jnp.take(value, all_rows, axis=0)
        in_window = (own_rows[:, None] >= window_low[tile_id][None, :]) & (own_rows[:, None] < window_high[tile_id][None, :])
        valid_slab = offsets[None, :] < slab_length[tile_id][:, None]
        allowed_slab = (in_window[:, :, None] & valid_slab[None, :, :]).reshape(TILE, NB * SLAB)
        allowed = jnp.concatenate([jnp.ones((TILE, TILE), dtype=bool), allowed_slab], axis=1)
        query_tile = lax.dynamic_slice_in_dim(queries, slot_id * TILE, TILE, 0)
        return attend_tile(query_tile, key_rows, value_rows, allowed, head_count)
    blocks = lax.map(one_slot, jnp.arange(tile_count, dtype=jnp.int32))
    return blocks.reshape(tile_count * TILE, -1)
```

```python
import math

import jax
import jax.numpy as jnp
from jax import lax
from jax.experimental import pallas as pl
from jax.experimental.pallas import tpu as pltpu
from jax.sharding import PartitionSpec as P

HD = 128
TILE = 256
NB = 6
SLAB = 64
TPD = 4
WIN = 80
NX, NZH, NC, NZL, NY = 4, 4, 2, 2, 4
AXES = ("ctx", "tp")
BF16 = jnp.bfloat16
F32 = jnp.float32


def _index(x, zh, c, zl, y):
    return (((x % NX) * NZH + zh % NZH) * NC + c % NC) * (NZL * NY) + zl % NZL * NY + y % NY


def _moves(dx=0, dzh=0, dc=0, dzl=0, dy=0):
    pairs = []
    for x in range(NX):
        for zh in range(NZH):
            for c in range(NC):
                for zl in range(NZL):
                    for y in range(NY):
                        pairs.append(
                            (
                                _index(x, zh, c, zl, y),
                                _index(x + dx, zh + dzh, c + dc, zl + dzl, y + dy),
                            )
                        )
    return pairs


def send(a, **step):
    return lax.ppermute(a, AXES, _moves(**step))


def after(a, *earlier):
    return lax.optimization_barrier((a, *earlier))[0]


X_REL = (0, -1, 1, 2)
ZH_REL = (0, -1, 1, 2)


def _weight_copies(pieces):
    out = []
    for flip in range(2):
        own, left, right, far_a, far_b = pieces[flip * 5 : flip * 5 + 5]
        for q, ref in ((0, own), (1, left), (2, right)):
            for i in range(4):
                for kv in range(2):
                    out.append((ref, i * 320 + kv * 160, q, ZH_REL[i], flip, kv))
        for ref, at in ((far_a, 0), (far_b, 2)):
            for i in range(2):
                for kv in range(2):
                    out.append((ref, i * 320 + kv * 160, 3, ZH_REL[at + i], flip, kv))
    return out


def _project(pos, toks, tok_rows, pieces, t_buf, w_buf, acc, t_sem, w_sem, fs):
    x, zh, c = pos[0], pos[1], pos[2]
    quarter = fs * NZH * NC
    waits = [[] for _ in range(4)]
    copies = _weight_copies(pieces)
    for q in range(4):
        n = 0
        for ref, row, at, zrel, flip, kv in copies:
            if at != q:
                continue
            place = ((zh + zrel + NZH) % NZH * NC + (c + flip) % NC) * fs
            cp = pltpu.make_async_copy(
                ref.at[pl.ds(row, fs), :],
                w_buf.at[q, pl.ds(pl.multiple_of(place, 32), fs), pl.ds(kv * 384, 384)],
                w_sem.at[q, n],
            )
            cp.start()
            waits[q].append(cp)
            n += 1
        col = pl.multiple_of((x + X_REL[q] + NX) % NX * quarter, 128)
        r0 = 0
        for i, (tok, rows) in enumerate(zip(toks, tok_rows)):
            cp = pltpu.make_async_copy(
                tok.at[:, pl.ds(col, quarter)],
                t_buf.at[q, pl.ds(r0, rows), :],
                t_sem.at[q, i],
            )
            cp.start()
            waits[q].append(cp)
            r0 += rows
    for q in range(4):
        for cp in waits[q]:
            cp.wait()
        part = jnp.dot(t_buf[q], w_buf[q], preferred_element_type=F32)
        if q == 0:
            acc[...] = part
        else:
            acc[...] += part


def _scratch(rows, ntok, fs):
    quarter = fs * NZH * NC
    return [
        pltpu.VMEM((4, rows, quarter), BF16),
        pltpu.VMEM((4, quarter, 768), BF16),
        pltpu.VMEM((rows, 768), F32),
        pltpu.SemaphoreType.DMA((4, ntok)),
        pltpu.SemaphoreType.DMA((4, 16)),
    ]


ANY = pl.BlockSpec(memory_space=pl.ANY)
SM = pl.BlockSpec(memory_space=pltpu.SMEM)
VM = pl.BlockSpec(memory_space=pltpu.VMEM)
VMEM_LIMIT = 48 * 1024 * 1024


def project(pos, toks, pieces, fs):
    rows = [t.shape[0] for t in toks]
    total = sum(rows)
    n = len(toks)

    def body(*refs):
        pos_ref = refs[0]
        tok_refs = refs[1 : 1 + n]
        piece_refs = refs[1 + n : 11 + n]
        out, t_buf, w_buf, acc, t_sem, w_sem = refs[11 + n :]
        _project(pos_ref, tok_refs, rows, piece_refs, t_buf, w_buf, acc, t_sem, w_sem, fs)
        out[...] = acc[...].astype(BF16)

    return pl.pallas_call(
        body,
        out_shape=jax.ShapeDtypeStruct((total, 768), BF16),
        in_specs=[SM] + [ANY] * (n + 10),
        out_specs=VM,
        scratch_shapes=_scratch(total, n, fs),
        compiler_params=pltpu.CompilerParams(vmem_limit_bytes=VMEM_LIMIT),
    )(pos, *toks, *pieces)


def _tile_at(slot_ref, block, p):
    tile = block * TPD
    for i in range(1, TPD):
        tile = jnp.where(slot_ref[0, block * TPD + i] == block * TPD + p, block * TPD + i, tile)
    return tile


def _aligned(start):
    return jnp.minimum(start // 16 * 16, TILE - WIN)


def project_last(pos, toks, pieces, done, done_places, places, tables, fs):
    rows = [t.shape[0] for t in toks]
    total = sum(rows)
    n = len(toks)
    nd = len(done)
    ncopy = sum(len(p) for p in done_places)

    def body(*refs):
        pos_ref = refs[0]
        tok_refs = refs[1 : 1 + n]
        piece_refs = refs[1 + n : 11 + n]
        done_refs = refs[11 + n : 11 + n + nd]
        slot, neighbour, first = refs[11 + n + nd : 14 + n + nd]
        full, to_next, to_prev = refs[14 + n + nd : 17 + n + nd]
        t_buf, w_buf, acc, t_sem, w_sem, d_sem = refs[17 + n + nd :]
        block, zl, y, blocks = pos_ref[3], pos_ref[4], pos_ref[5], pos_ref[6]

        def row_of(place):
            dzl, dy, half = place
            r = ((zl + dzl) % NZL * NY + (y + dy + NY) % NY) * 128 + half * 64
            return pl.multiple_of(r, 64)

        waits = []
        for ref, plan in zip(done_refs, done_places):
            r0 = 0
            for place, count in plan:
                cp = pltpu.make_async_copy(
                    ref.at[pl.ds(r0, count), :],
                    full.at[pl.ds(row_of(place), count), :],
                    d_sem.at[len(waits)],
                )
                cp.start()
                waits.append(cp)
                r0 += count
        _project(pos_ref, tok_refs, rows, piece_refs, t_buf, w_buf, acc, t_sem, w_sem, fs)
        r0 = 0
        for place, count in places:
            full[pl.ds(row_of(place), count), :] = acc[pl.ds(r0, count), :].astype(BF16)
            r0 += count
        for cp in waits:
            cp.wait()
        lane = lax.broadcasted_iota(jnp.int32, (SLAB, WIN), 1)
        sub = lax.broadcasted_iota(jnp.int32, (SLAB, WIN), 0)
        for out, step in ((to_next, 1), (to_prev, -1)):
            target = (block + step + blocks) % blocks
            for p in range(TPD):
                tile = _tile_at(slot, target, p)
                seen = jnp.int32(0)
                starts = [jnp.int32(0), jnp.int32(0)]
                for j in range(NB):
                    other = neighbour[j, tile]
                    hit = other // TPD == block
                    row = slot[0, other] % TPD * TILE
                    s = first[j, tile]
                    for o in range(2):
                        take = jnp.logical_and(hit, seen == o)
                        starts[o] = jnp.where(take, row + s, starts[o])
                    seen = seen + hit.astype(jnp.int32)
                for o in range(2):
                    row = starts[o] // TILE * TILE
                    s = starts[o] - row
                    al = _aligned(s)
                    window = full[pl.ds(pl.multiple_of(row + al, 16), WIN), :]
                    pick = (lane == sub + (s - al)).astype(F32).astype(BF16)
                    out[pl.ds((p * 2 + o) * SLAB, SLAB), :] = jnp.dot(
                        pick, window, preferred_element_type=F32
                    ).astype(BF16)

    return pl.pallas_call(
        body,
        out_shape=[
            jax.ShapeDtypeStruct((TPD * TILE, 768), BF16),
            jax.ShapeDtypeStruct((TPD * 2 * SLAB, 768), BF16),
            jax.ShapeDtypeStruct((TPD * 2 * SLAB, 768), BF16),
        ],
        in_specs=[SM] + [ANY] * (n + 10 + nd) + [SM] * 3,
        out_specs=[VM, VM, VM],
        scratch_shapes=_scratch(total, n, fs) + [pltpu.SemaphoreType.DMA((ncopy,))],
        compiler_params=pltpu.CompilerParams(vmem_limit_bytes=VMEM_LIMIT),
    )(pos, *toks, *pieces, *done, *tables)


CAND = 768
HALO = TPD * 2 * SLAB


def attend(pos, queries, full, from_prev, from_next, tables):
    scale = 1.0 / math.sqrt(HD)

    def body(pos_ref, q_ref, full_ref, prev_ref, next_ref, slot, neighbour, first, length,
             low, high, out, rows_buf, cand, sems):
        p = pl.program_id(0)
        block, blocks = pos_ref[3], pos_ref[6]

        @pl.when(p == 0)
        def _():
            parts = ((prev_ref, 0, HALO), (full_ref, HALO, TPD * TILE),
                     (next_ref, HALO + TPD * TILE, HALO))
            waits = []
            for i, (ref, at, count) in enumerate(parts):
                cp = pltpu.make_async_copy(ref, rows_buf.at[pl.ds(at, count), :], sems.at[i])
                cp.start()
                waits.append(cp)
            rows_buf[pl.ds(2 * HALO + TPD * TILE, 16), :] = jnp.zeros((16, 768), BF16)
            cand[pl.ds(TILE + NB * WIN, CAND - TILE - NB * WIN), :] = jnp.zeros(
                (CAND - TILE - NB * WIN, 768), BF16
            )
            for cp in waits:
                cp.wait()

        tile = _tile_at(slot, block, p)
        own = pl.multiple_of(HALO + p * TILE, 128)
        cand[pl.ds(0, TILE), :] = rows_buf[pl.ds(own, TILE), :]
        col = lax.broadcasted_iota(jnp.int32, (8, CAND), 1)
        lows = jnp.where(col < TILE, 0, TILE)
        highs = jnp.where(col < TILE, TILE, 0)
        seen_prev = jnp.int32(0)
        seen_next = jnp.int32(0)
        for j in range(NB):
            other = neighbour[j, tile]
            at = other // TPD
            is_prev = at == (block + blocks - 1) % blocks
            is_next = at == (block + 1) % blocks
            s = first[j, tile]
            al = _aligned(s)
            begin = HALO + slot[0, other] % TPD * TILE + al
            begin = jnp.where(is_prev, (p * 2 + seen_prev) * SLAB, begin)
            begin = jnp.where(
                is_next, HALO + TPD * TILE + (p * 2 + seen_next) * SLAB, begin
            )
            rem = jnp.where(jnp.logical_or(is_prev, is_next), 0, s - al)
            seen_prev = seen_prev + is_prev.astype(jnp.int32)
            seen_next = seen_next + is_next.astype(jnp.int32)
            c0 = TILE + j * WIN
            cand[pl.ds(c0, WIN), :] = rows_buf[pl.ds(pl.multiple_of(begin, 16), WIN), :]
            valid = jnp.logical_and(col >= c0 + rem, col < c0 + rem + length[j, tile])
            lows = jnp.where(valid, low[j, tile], lows)
            highs = jnp.where(valid, high[j, tile], highs)
        row = lax.broadcasted_iota(jnp.int32, (TILE, CAND), 0)
        allowed = jnp.logical_and(row >= lows[0:1, :], row < highs[0:1, :])
        for h in range(3):
            q = q_ref[:, h * HD : (h + 1) * HD]
            k = cand[:, h * HD : (h + 1) * HD]
            v = cand[:, 384 + h * HD : 384 + (h + 1) * HD]
            scores = lax.dot_general(
                q, k, (((1,), (1,)), ((), ())), preferred_element_type=F32
            ) * scale
            scores = jnp.where(allowed, scores, -jnp.inf)
            top = jnp.max(scores, axis=-1, keepdims=True)
            weights = jnp.exp(scores - top)
            total = jnp.sum(weights, axis=-1, keepdims=True)
            mixed = jnp.dot(weights.astype(BF16), v, preferred_element_type=F32)
            out[:, h * HD : (h + 1) * HD] = (mixed / total).astype(BF16)

    return pl.pallas_call(
        body,
        grid=(TPD,),
        out_shape=jax.ShapeDtypeStruct(queries.shape, BF16),
        in_specs=[SM, pl.BlockSpec((TILE, 384), lambda p: (p, 0)), ANY, ANY, ANY] + [SM] * 6,
        out_specs=pl.BlockSpec((TILE, 384), lambda p: (p, 0)),
        scratch_shapes=[
            pltpu.VMEM((2 * HALO + TPD * TILE + 16, 768), BF16),
            pltpu.VMEM((CAND, 768), BF16),
            pltpu.SemaphoreType.DMA((3,)),
        ],
        compiler_params=pltpu.CompilerParams(vmem_limit_bytes=VMEM_LIMIT),
    )(pos, queries, full, from_prev, from_next, *tables)


def per_device(
    tokens,
    queries,
    w_key,
    w_value,
    tile_slot,
    neighbour_tile,
    slab_start,
    slab_length,
    window_low,
    window_high,
):
    fs = w_key.shape[0]
    ctx = lax.axis_index("ctx")
    tp = lax.axis_index("tp")
    pos = jnp.stack(
        [ctx // 8, ctx // 2 % 4, ctx % 2, ctx, tp // 4, tp % 4, jnp.int32(lax.axis_size("ctx"))]
    ).astype(jnp.int32)
    tables = (
        tile_slot.reshape(1, -1),
        neighbour_tile.T,
        slab_start.T,
        slab_length.T,
        window_low.T,
        window_high.T,
    )

    w = jnp.concatenate([w_key, w_value], axis=0)
    a = send(w, dzh=1)
    b = send(w, dzh=-1)
    ya = send(tokens, dy=1)
    yb = send(tokens, dy=-1)
    ck = send(a[:fs], dzh=1)
    cv = send(b[fs:], dzh=-1)
    zp = send(after(tokens, a, b), dzl=1)
    own = jnp.concatenate([w, a, b, ck, cv], axis=0)
    half = own.shape[0] // 2
    left = send(own, dx=1)
    right = send(own, dx=-1)
    yo_top = send(ya[:64], dy=1)
    yo_bottom = send(yb[64:], dy=-1)
    far_a = send(left[:half], dx=1)
    far_b = send(right[half:], dx=-1)
    mine = (own, left, right, far_a, far_b)
    pieces = mine + tuple(send(p, dc=1) for p in mine)
    zt, zb = zp[:64], zp[64:]
    t1 = (send(zt, dy=1), send(zt, dy=-1), send(yo_top, dzl=1))
    t2 = (send(zb, dy=1), send(zb, dy=-1), send(yo_bottom, dzl=1))

    kv1 = project(pos, (tokens, ya, yb, yo_top, yo_bottom, zp), pieces, fs)
    kv2 = project(pos, t1, pieces, fs)
    plan1 = (
        ((0, 0, 0), 128),
        ((0, -1, 0), 128),
        ((0, 1, 0), 128),
        ((0, 2, 0), 64),
        ((0, 2, 1), 64),
        ((1, 0, 0), 128),
    )
    plan2 = (((1, -1, 0), 64), ((1, 1, 0), 64), ((1, 2, 0), 64))
    plan3 = (((1, -1, 1), 64), ((1, 1, 1), 64), ((1, 2, 1), 64))
    full, to_next, to_prev = project_last(
        pos, t2, pieces, (kv1, kv2), (plan1, plan2), plan3, tables[:3], fs
    )
    peers = lax.axis_size("ctx")
    up = [(i, (i + 1) % peers) for i in range(peers)]
    from_prev = lax.ppermute(to_next, "ctx", up)
    from_next = lax.ppermute(to_prev, "ctx", [(j, i) for i, j in up])
    return attend(pos, queries, full, from_prev, from_next, tables)


def solution(mesh):
    in_specs = (
        P(("ctx", "tp"), None),
        P("ctx", "tp"),
        P("ctx", "tp"),
        P("ctx", "tp"),
        P(),
        P(),
        P(),
        P(),
        P(),
        P(),
    )
    out_specs = P("ctx", "tp")
    return jax.shard_map(
        per_device, mesh=mesh, in_specs=in_specs, out_specs=out_specs, check_vma=False
    )
```

```python
import math

import jax
import jax.numpy as jnp
from jax import lax
from jax.experimental import pallas as pl
from jax.experimental.pallas import tpu as pltpu
from jax.sharding import PartitionSpec as P


HD = 128
TILE = 256
NB = 6
SLAB = 64
TPD = 4
HALO = TPD * 2 * SLAB
WIN = 80
NX, NZH, NC, NZL, NY = 4, 4, 2, 2, 4
AXES = ("ctx", "tp")
BF16 = jnp.bfloat16
F32 = jnp.float32


def _index(x, zh, c, zl, y):
    return (((x % NX) * NZH + zh % NZH) * NC + c % NC) * (NZL * NY) + zl % NZL * NY + y % NY


def _moves(dx=0, dzh=0, dc=0, dzl=0, dy=0, sx=0, sz=0):
    pairs = []
    for x in range(NX):
        for zh in range(NZH):
            for c in range(NC):
                for zl in range(NZL):
                    for y in range(NY):
                        pairs.append(
                            (
                                _index(x, zh, c, zl, y),
                                _index(
                                    x + dx + sx * (1 - 2 * c),
                                    zh + dzh + sz * (1 - 2 * c),
                                    c + dc,
                                    zl + dzl,
                                    y + dy,
                                ),
                            )
                        )
    return pairs


def _far_moves():
    blocks = NX * NZH * NC
    tps = NZL * NY
    return [
        (b * tps + t, (b - 1 + 2 * (b % 2)) % blocks * tps + t)
        for b in range(blocks)
        for t in range(tps)
    ]


def send(a, **step):
    return lax.ppermute(a, AXES, _moves(**step))


PAIR = ((0, False, 0), (0, False, 1))
NEAR = ((1, True, 0), (1, True, 1), (2, False, 0))
BOTH = NEAR + ((-1, True, 1), (-1, True, 0), (2, False, 1))


ANY = pl.BlockSpec(memory_space=pl.ANY)
SM = pl.BlockSpec(memory_space=pltpu.SMEM)
VM = pl.BlockSpec(memory_space=pltpu.VMEM)
MIB = 1024 * 1024


def join(*parts):
    rows = [p.shape[0] for p in parts]

    def body(*refs):
        out, sems = refs[-2:]
        copies = []
        for i, ref in enumerate(refs[:-2]):
            copies.append(
                pltpu.make_async_copy(ref, out.at[pl.ds(sum(rows[:i]), rows[i]), :], sems.at[i])
            )
        for cp in copies:
            cp.start()
        for cp in copies:
            cp.wait()

    return pl.pallas_call(
        body,
        out_shape=jax.ShapeDtypeStruct((sum(rows), parts[0].shape[1]), parts[0].dtype),
        in_specs=[ANY] * len(parts),
        out_specs=ANY,
        scratch_shapes=[pltpu.SemaphoreType.DMA((len(parts),))],
        compiler_params=pltpu.CompilerParams(vmem_limit_bytes=MIB),
    )(*parts)


def project(pos, toks, tok_at, rows, pieces, fs):
    nt, np_ = len(toks), len(pieces)
    features = fs * NX * NZH * NC
    quarter = features // NX

    def body(*refs):
        pos_ref = refs[0]
        tok_refs = refs[1 : 1 + nt]
        piece_refs = refs[1 + nt : 1 + nt + np_]
        out, w_out, t_buf, w_buf, acc, t_sem, w_sem, o_sem = refs[1 + nt + np_ :]
        x, zh, c = pos_ref[0], pos_ref[1], pos_ref[2]
        waits = []
        for ref, (_, xrel, signed, flip, plan) in zip(piece_refs, pieces):
            core = (c + flip) % NC
            sign = 2 * core - 1
            xs = (x + (sign * xrel if signed else xrel) + NX) % NX
            for i, (zrel, zsigned, other) in enumerate(plan):
                zs = (zh + (sign * zrel if zsigned else zrel) + NZH) % NZH
                place = pl.multiple_of(((xs * NZH + zs) * NC + (core + other) % NC) * fs, 32)
                for kv in range(2):
                    cp = pltpu.make_async_copy(
                        ref.at[pl.ds((2 * i + kv) * fs, fs), :],
                        w_buf.at[pl.ds(place, fs), pl.ds(kv * 384, 384)],
                        w_sem.at[len(waits)],
                    )
                    cp.start()
                    waits.append(cp)
        for i, (ref, (r0, c0)) in enumerate(zip(tok_refs, tok_at)):
            cp = pltpu.make_async_copy(
                ref,
                t_buf.at[pl.ds(r0, ref.shape[0]), pl.ds(c0, ref.shape[1])],
                t_sem.at[i],
            )
            cp.start()
            waits.append(cp)
        for cp in waits:
            cp.wait()
        back = pltpu.make_async_copy(w_buf, w_out, o_sem)
        back.start()
        for q in range(NX):
            part = jnp.dot(
                t_buf[:, q * quarter : (q + 1) * quarter],
                w_buf[q * quarter : (q + 1) * quarter, :],
                preferred_element_type=F32,
            )
            if q == 0:
                acc[...] = part
            elif q < NX - 1:
                acc[...] += part
            else:
                out[...] = (acc[...] + part).astype(BF16)
        back.wait()

    n_copies = 2 * sum(len(p[4]) for p in pieces)
    return pl.pallas_call(
        body,
        out_shape=[
            jax.ShapeDtypeStruct((rows, 768), BF16),
            jax.ShapeDtypeStruct((features, 768), BF16),
        ],
        in_specs=[SM] + [ANY] * (nt + np_),
        out_specs=[VM, ANY],
        scratch_shapes=[
            pltpu.VMEM((rows, features), BF16),
            pltpu.VMEM((features, 768), BF16),
            pltpu.VMEM((rows, 768), F32),
            pltpu.SemaphoreType.DMA((nt,)),
            pltpu.SemaphoreType.DMA((n_copies,)),
            pltpu.SemaphoreType.DMA,
        ],
        compiler_params=pltpu.CompilerParams(vmem_limit_bytes=30 * MIB),
    )(pos, *toks, *[p[0] for p in pieces])


def _half_product(toks, w, row0, t_buf, w_buf, t_sem, w_sem):
    n = toks[0].shape[0]
    half = toks[0].shape[1]
    step = half // 2
    waits = []
    for i, ref in enumerate(toks):
        waits.append(pltpu.make_async_copy(ref, t_buf.at[pl.ds(i * n, n), :], t_sem.at[i]))
    loads = [
        pltpu.make_async_copy(
            w.at[pl.ds(row0 + i * step, step), :], w_buf.at[pl.ds(i * step, step), :], w_sem.at[i]
        )
        for i in range(2)
    ]
    for cp in loads[:1] + waits + loads[1:]:
        cp.start()

    def product(acc):
        for cp in waits:
            cp.wait()
        for i in range(2):
            loads[i].wait()
            acc[...] += jnp.dot(
                t_buf[:, i * step : (i + 1) * step],
                w_buf[i * step : (i + 1) * step, :],
                preferred_element_type=F32,
            )

    return product


def _half_scratch(rows, half):
    return [
        pltpu.VMEM((rows, half), BF16),
        pltpu.VMEM((half, 768), BF16),
        pltpu.SemaphoreType.DMA((3,)),
        pltpu.SemaphoreType.DMA((2,)),
    ]


def project_half(toks, w):
    rows = sum(t.shape[0] for t in toks)
    half = toks[0].shape[1]

    def body(t0, t1, t2, w_ref, acc, t_buf, w_buf, t_sem, w_sem):
        product = _half_product((t0, t1, t2), w_ref, 0, t_buf, w_buf, t_sem, w_sem)
        acc[...] = jnp.zeros_like(acc)
        product(acc)

    return pl.pallas_call(
        body,
        out_shape=jax.ShapeDtypeStruct((rows, 768), F32),
        in_specs=[ANY] * 4,
        out_specs=VM,
        scratch_shapes=_half_scratch(rows, half),
        compiler_params=pltpu.CompilerParams(vmem_limit_bytes=16 * MIB),
    )(*toks, w)


def _tile_at(slot_ref, block, p):
    tile = block * TPD
    for i in range(1, TPD):
        tile = jnp.where(slot_ref[0, block * TPD + i] == block * TPD + p, block * TPD + i, tile)
    return tile


def _aligned(start):
    return jnp.minimum(start // 16 * 16, TILE - WIN)


def project_last(pos, toks, w, acc_in, done, done_places, places, tables):
    rows = sum(t.shape[0] for t in toks)
    half = toks[0].shape[1]
    n = toks[0].shape[0]

    def body(pos_ref, t0, t1, t2, w_ref, acc_ref, done_ref, slot, neighbour, first,
             full, to_near, to_far, t_buf, w_buf, t_sem, w_sem, acc, wide):
        block, zl, y, blocks = pos_ref[3], pos_ref[4], pos_ref[5], pos_ref[6]
        product = _half_product((t0, t1, t2), w_ref, half, t_buf, w_buf, t_sem, w_sem)

        def row_of(place):
            dzl, dy = place
            return pl.multiple_of(((zl + dzl) % NZL * NY + (y + dy + NY) % NY) * n, n)

        for i, place in enumerate(done_places):
            part = done_ref[i * n : (i + 1) * n, :]
            full[pl.ds(row_of(place), n), :] = part
            wide[pl.ds(row_of(place), n), :] = part.astype(F32)
        acc[...] = acc_ref[...]
        product(acc)
        for i, place in enumerate(places):
            part = acc[i * n : (i + 1) * n, :].astype(BF16)
            full[pl.ds(row_of(place), n), :] = part
            wide[pl.ds(row_of(place), n), :] = part.astype(F32)
        up = 1 - 2 * pos_ref[2]
        for out, step in ((to_near, up), (to_far, -up)):
            target = (block + step + blocks) % blocks

            def pick(p, carry, out=out, target=target):
                tile = _tile_at(slot, target, p)
                seen = jnp.int32(0)
                starts = [jnp.int32(0), jnp.int32(0)]
                for j in range(NB):
                    other = neighbour[j, tile]
                    hit = other // TPD == block
                    row = slot[0, other] % TPD * TILE + first[j, tile]
                    for o in range(2):
                        take = jnp.logical_and(hit, seen == o)
                        starts[o] = jnp.where(take, row, starts[o])
                    seen = seen + hit.astype(jnp.int32)
                for o in range(2):
                    al = pl.multiple_of(starts[o] // 8 * 8, 8)
                    rem = starts[o] - al
                    window = pltpu.roll(
                        wide[pl.ds(al, SLAB + 8), :], (SLAB + 8 - rem) % (SLAB + 8), 0
                    )
                    at = pl.multiple_of((p * 2 + o) * SLAB, SLAB)
                    out[pl.ds(at, SLAB), :] = window[:SLAB].astype(BF16)
                return carry

            lax.fori_loop(0, TPD, pick, 0)

    return pl.pallas_call(
        body,
        out_shape=[
            jax.ShapeDtypeStruct((TPD * TILE, 768), BF16),
            jax.ShapeDtypeStruct((HALO, 768), BF16),
            jax.ShapeDtypeStruct((HALO, 768), BF16),
        ],
        in_specs=[SM] + [ANY] * 4 + [VM, VM] + [SM] * 3,
        out_specs=[VM, VM, VM],
        scratch_shapes=_half_scratch(rows, half)
        + [pltpu.VMEM((rows, 768), F32), pltpu.VMEM((TPD * TILE + 8, 768), F32)],
        compiler_params=pltpu.CompilerParams(vmem_limit_bytes=24 * MIB),
    )(pos, *toks, w, acc_in, done, *tables)


CAND = 768


def attend(pos, queries, full, from_near, from_far, tables):
    scale = 1.0 / math.sqrt(HD)

    def body(pos_ref, q_ref, full_ref, near_ref, far_ref, slot, neighbour, first, length,
             low, high, out, cand):
        p = pl.program_id(0)
        block, blocks = pos_ref[3], pos_ref[6]

        @pl.when(p == 0)
        def _():
            cand[pl.ds(TILE + NB * WIN, CAND - TILE - NB * WIN), :] = jnp.zeros(
                (CAND - TILE - NB * WIN, 768), BF16
            )
            for j in range(NB):
                cand[pl.ds(TILE + j * WIN + SLAB, WIN - SLAB), :] = jnp.zeros(
                    (WIN - SLAB, 768), BF16
                )

        tile = _tile_at(slot, block, p)
        own = pl.multiple_of(p * TILE, TILE)
        cand[pl.ds(0, TILE), :] = full_ref[pl.ds(own, TILE), :]
        col = lax.broadcasted_iota(jnp.int32, (8, CAND), 1)
        lows = jnp.where(col < TILE, 0, TILE)
        highs = jnp.where(col < TILE, TILE, 0)
        up = 1 - 2 * pos_ref[2]
        near_block = (block + up + blocks) % blocks
        far_block = (block - up + blocks) % blocks
        seen_near = jnp.int32(0)
        seen_far = jnp.int32(0)
        for j in range(NB):
            other = neighbour[j, tile]
            at = other // TPD
            is_near = at == near_block
            is_far = at == far_block
            s = first[j, tile]
            al = _aligned(s)
            c0 = TILE + j * WIN
            begin = slot[0, other] % TPD * TILE + al

            @pl.when(is_near)
            def _(c0=c0, seen_near=seen_near):
                at = pl.multiple_of((p * 2 + seen_near) * SLAB, SLAB)
                cand[pl.ds(c0, SLAB), :] = near_ref[pl.ds(at, SLAB), :]

            @pl.when(is_far)
            def _(c0=c0, seen_far=seen_far):
                at = pl.multiple_of((p * 2 + seen_far) * SLAB, SLAB)
                cand[pl.ds(c0, SLAB), :] = far_ref[pl.ds(at, SLAB), :]

            away = jnp.logical_or(is_near, is_far)

            @pl.when(jnp.logical_not(away))
            def _(c0=c0, begin=begin):
                cand[pl.ds(c0, WIN), :] = full_ref[pl.ds(pl.multiple_of(begin, 16), WIN), :]

            rem = jnp.where(away, 0, s - al)
            seen_near = seen_near + is_near.astype(jnp.int32)
            seen_far = seen_far + is_far.astype(jnp.int32)
            valid = jnp.logical_and(col >= c0 + rem, col < c0 + rem + length[j, tile])
            lows = jnp.where(valid, low[j, tile], lows)
            highs = jnp.where(valid, high[j, tile], highs)
        row = lax.broadcasted_iota(jnp.int32, (TILE, CAND), 0)
        allowed = jnp.logical_and(row >= lows[0:1, :], row < highs[0:1, :])
        for h in range(3):
            q = q_ref[:, h * HD : (h + 1) * HD]
            k = cand[:, h * HD : (h + 1) * HD]
            v = cand[:, 384 + h * HD : 384 + (h + 1) * HD]
            scores = lax.dot_general(
                q, k, (((1,), (1,)), ((), ())), preferred_element_type=F32
            ) * scale
            scores = jnp.where(allowed, scores, -jnp.inf)
            top = jnp.max(scores, axis=-1, keepdims=True)
            weights = jnp.exp(scores - top)
            total = jnp.sum(weights, axis=-1, keepdims=True)
            mixed = jnp.dot(weights.astype(BF16), v, preferred_element_type=F32)
            out[:, h * HD : (h + 1) * HD] = (mixed / total).astype(BF16)

    return pl.pallas_call(
        body,
        grid=(TPD,),
        out_shape=jax.ShapeDtypeStruct(queries.shape, BF16),
        in_specs=[SM, pl.BlockSpec((TILE, 384), lambda p: (p, 0)), VM, VM, VM] + [SM] * 6,
        out_specs=pl.BlockSpec((TILE, 384), lambda p: (p, 0)),
        scratch_shapes=[pltpu.VMEM((CAND, 768), BF16)],
        compiler_params=pltpu.CompilerParams(vmem_limit_bytes=24 * MIB),
    )(pos, queries, full, from_near, from_far, *tables)


def per_device(
    tokens,
    queries,
    w_key,
    w_value,
    tile_slot,
    neighbour_tile,
    slab_start,
    slab_length,
    window_low,
    window_high,
):
    fs = w_key.shape[0]
    ctx = lax.axis_index("ctx")
    tp = lax.axis_index("tp")
    pos = jnp.stack(
        [ctx >> 3, (ctx >> 1) & 3, ctx & 1, ctx, tp >> 2, tp & 3, jnp.int32(lax.axis_size("ctx"))]
    ).astype(jnp.int32)
    tables = (
        tile_slot.reshape(1, -1),
        neighbour_tile.T,
        slab_start.T,
        slab_length.T,
        window_low.T,
        window_high.T,
    )

    h = tokens.shape[1] // 2
    w = join(w_key, w_value)
    pair = join(w, send(w, dc=1))
    ya = send(tokens, dy=1)
    z1 = send(pair, sz=1)
    yb = send(tokens, dy=-1)
    xa1 = send(pair, sx=1)
    tl, tr = tokens[:, :h], tokens[:, h:]
    xa2 = send(xa1[: 2 * fs], sx=1)
    z2 = send(z1[: 2 * fs], sz=1)
    z_l = send(tl, dzl=1)
    z_r = send(tr, dzl=1)
    near = join(z1, z2)
    both = join(near, send(near, dc=1))
    xb1 = send(both, sx=1)
    yo_l = send(ya[:, :h], dy=1)
    yo_r = send(yb[:, h:], dy=-1)
    ua_l = send(z_l, dy=1)
    ub_l = send(z_l, dy=-1)
    xb2 = send(xb1[: 6 * fs], sx=1)
    uo_l = send(yo_l, dzl=1)
    uo_r = send(yo_r, dzl=1)
    ua_r = send(z_r, dy=1)
    ub_r = send(z_r, dy=-1)
    pieces = [(pair, 0, False, 0, PAIR), (both, 0, False, 0, BOTH)]
    for p, xrel, signed, plan in (
        (xa1, 1, True, PAIR), (xa2, 2, False, PAIR[:1]), (xb1, 1, True, BOTH), (xb2, 2, False, NEAR)
    ):
        pieces += [(p, xrel, signed, 0, plan), (send(p, dc=1), xrel, signed, 1, plan)]

    n = tokens.shape[0]
    toks = (tokens, ya, yb, yo_l, yo_r, z_l, z_r)
    at = ((0, 0), (n, 0), (2 * n, 0), (3 * n, 0), (3 * n, h), (4 * n, 0), (4 * n, h))
    kv1, w_all = project(pos, toks, at, 5 * n, pieces, fs)
    part = project_half((ua_l, ub_l, uo_l), w_all)
    full, to_near, to_far = project_last(
        pos,
        (ua_r, ub_r, uo_r),
        w_all,
        part,
        kv1,
        ((0, 0), (0, -1), (0, 1), (0, 2), (1, 0)),
        ((1, -1), (1, 1), (1, 2)),
        tables[:3],
    )
    from_far = lax.ppermute(to_far, AXES, _far_moves())
    from_near = lax.ppermute(to_near, AXES, _moves(dc=1))
    return attend(pos, queries, full, from_near, from_far, tables)


def solution(mesh):
    in_specs = (
        P(("ctx", "tp"), None),
        P("ctx", "tp"),
        P("ctx", "tp"),
        P("ctx", "tp"),
        P(),
        P(),
        P(),
        P(),
        P(),
        P(),
    )
    out_specs = P("ctx", "tp")
    return jax.shard_map(
        per_device, mesh=mesh, in_specs=in_specs, out_specs=out_specs, check_vma=False
    )
```

```python
import math

import jax
import jax.numpy as jnp
from jax import lax
from jax.experimental import pallas as pl
from jax.experimental.pallas import tpu as pltpu
from jax.sharding import PartitionSpec as P


HD = 128
TILE = 256
NB = 6
SLAB = 64
TPD = 4
HALO = TPD * 2 * SLAB
WIN = 80
NX, NZH, NC, NZL, NY = 4, 4, 2, 2, 4
AXES = ("ctx", "tp")
BF16 = jnp.bfloat16
F32 = jnp.float32


def _index(x, zh, c, zl, y):
    return (((x % NX) * NZH + zh % NZH) * NC + c % NC) * (NZL * NY) + zl % NZL * NY + y % NY


def _moves(dx=0, dzh=0, dc=0, dzl=0, dy=0, sx=0, sz=0):
    pairs = []
    for x in range(NX):
        for zh in range(NZH):
            for c in range(NC):
                for zl in range(NZL):
                    for y in range(NY):
                        pairs.append(
                            (
                                _index(x, zh, c, zl, y),
                                _index(
                                    x + dx + sx * (1 - 2 * c),
                                    zh + dzh + sz * (1 - 2 * c),
                                    c + dc,
                                    zl + dzl,
                                    y + dy,
                                ),
                            )
                        )
    return pairs


def _far_moves():
    blocks = NX * NZH * NC
    tps = NZL * NY
    return [
        (b * tps + t, (b - 1 + 2 * (b % 2)) % blocks * tps + t)
        for b in range(blocks)
        for t in range(tps)
    ]


def send(a, **step):
    return lax.ppermute(a, AXES, _far_moves() if "far" in step else _moves(**step))


SAME = ((0, False, 0),)
OTHER = ((0, False, 1),)
NEAR = ((1, True, 0), (1, True, 1), (2, False, 0))
FAR = ((-1, True, 1), (-1, True, 0), (2, False, 1))


ANY = pl.BlockSpec(memory_space=pl.ANY)
HBM = pl.BlockSpec(memory_space=pltpu.HBM)
SM = pl.BlockSpec(memory_space=pltpu.SMEM)
VM = pl.BlockSpec(memory_space=pltpu.VMEM)
MIB = 1024 * 1024


def join(*parts, space=None):
    rows = [p.shape[0] for p in parts]

    def body(*refs):
        out, sems = refs[-2:]
        copies = []
        for i, ref in enumerate(refs[:-2]):
            copies.append(
                pltpu.make_async_copy(ref, out.at[pl.ds(sum(rows[:i]), rows[i]), :], sems.at[i])
            )
        for cp in copies:
            cp.start()
        for cp in copies:
            cp.wait()

    return pl.pallas_call(
        body,
        out_shape=jax.ShapeDtypeStruct((sum(rows), parts[0].shape[1]), parts[0].dtype),
        in_specs=[space or ANY] * len(parts),
        out_specs=ANY,
        scratch_shapes=[pltpu.SemaphoreType.DMA((len(parts),))],
        compiler_params=pltpu.CompilerParams(vmem_limit_bytes=MIB),
    )(*parts)


def project(pos, toks, tok_at, rows, pieces, fs):
    nt, np_ = len(toks), len(pieces)
    features = fs * NX * NZH * NC
    quarter = features // NX

    def body(*refs):
        pos_ref = refs[0]
        tok_refs = refs[1 : 1 + nt]
        piece_refs = refs[1 + nt : 1 + nt + np_]
        out, w_out, t_buf, w_buf, acc, t_sem, w_sem, o_sem = refs[1 + nt + np_ :]
        x, zh, c = pos_ref[0], pos_ref[1], pos_ref[2]
        waits = []
        for ref, (_, xrel, signed, flip, plan) in zip(piece_refs, pieces):
            core = (c + flip) % NC
            sign = 2 * core - 1
            xs = (x + (sign * xrel if signed else xrel) + NX) % NX
            for i, (zrel, zsigned, other) in enumerate(plan):
                zs = (zh + (sign * zrel if zsigned else zrel) + NZH) % NZH
                place = pl.multiple_of(((xs * NZH + zs) * NC + (core + other) % NC) * fs, 32)
                for kv in range(2):
                    cp = pltpu.make_async_copy(
                        ref.at[pl.ds((2 * i + kv) * fs, fs), :],
                        w_buf.at[pl.ds(place, fs), pl.ds(kv * 384, 384)],
                        w_sem.at[len(waits)],
                    )
                    cp.start()
                    waits.append(cp)
        for i, (ref, (r0, c0)) in enumerate(zip(tok_refs, tok_at)):
            cp = pltpu.make_async_copy(
                ref,
                t_buf.at[pl.ds(r0, ref.shape[0]), pl.ds(c0, ref.shape[1])],
                t_sem.at[i],
            )
            cp.start()
            waits.append(cp)
        for cp in waits:
            cp.wait()
        back = pltpu.make_async_copy(w_buf, w_out, o_sem)
        back.start()
        for q in range(NX):
            part = jnp.dot(
                t_buf[:, q * quarter : (q + 1) * quarter],
                w_buf[q * quarter : (q + 1) * quarter, :],
                preferred_element_type=F32,
            )
            if q == 0:
                acc[...] = part
            elif q < NX - 1:
                acc[...] += part
            else:
                out[...] = (acc[...] + part).astype(BF16)
        back.wait()

    n_copies = 2 * sum(len(p[4]) for p in pieces)
    return pl.pallas_call(
        body,
        out_shape=[
            jax.ShapeDtypeStruct((rows, 768), BF16),
            jax.ShapeDtypeStruct((features, 768), BF16),
        ],
        in_specs=[SM] + [HBM] * (nt + np_),
        out_specs=[VM, ANY],
        scratch_shapes=[
            pltpu.VMEM((rows, features), BF16),
            pltpu.VMEM((features, 768), BF16),
            pltpu.VMEM((rows, 768), F32),
            pltpu.SemaphoreType.DMA((nt,)),
            pltpu.SemaphoreType.DMA((n_copies,)),
            pltpu.SemaphoreType.DMA,
        ],
        compiler_params=pltpu.CompilerParams(vmem_limit_bytes=60 * MIB),
    )(pos, *toks, *[p[0] for p in pieces])


def _half_product(toks, w, row0, t_buf, w_buf, t_sem, w_sem):
    n = toks[0].shape[0]
    half = toks[0].shape[1]
    step = half // 2
    waits = []
    for i, ref in enumerate(toks):
        waits.append(pltpu.make_async_copy(ref, t_buf.at[pl.ds(i * n, n), :], t_sem.at[i]))
    loads = [
        pltpu.make_async_copy(
            w.at[pl.ds(row0 + i * step, step), :], w_buf.at[pl.ds(i * step, step), :], w_sem.at[i]
        )
        for i in range(2)
    ]
    for cp in loads[:1] + waits + loads[1:]:
        cp.start()

    def product(acc):
        for cp in waits:
            cp.wait()
        for i in range(2):
            loads[i].wait()
            acc[...] += jnp.dot(
                t_buf[:, i * step : (i + 1) * step],
                w_buf[i * step : (i + 1) * step, :],
                preferred_element_type=F32,
            )

    return product


def _half_scratch(rows, half):
    return [
        pltpu.VMEM((rows, half), BF16),
        pltpu.VMEM((half, 768), BF16),
        pltpu.SemaphoreType.DMA((3,)),
        pltpu.SemaphoreType.DMA((2,)),
    ]


def project_half(toks, w):
    rows = sum(t.shape[0] for t in toks)
    half = toks[0].shape[1]

    def body(t0, t1, t2, w_ref, acc, t_buf, w_buf, t_sem, w_sem):
        product = _half_product((t0, t1, t2), w_ref, 0, t_buf, w_buf, t_sem, w_sem)
        acc[...] = jnp.zeros_like(acc)
        product(acc)

    return pl.pallas_call(
        body,
        out_shape=jax.ShapeDtypeStruct((rows, 768), F32),
        in_specs=[ANY] * 4,
        out_specs=VM,
        scratch_shapes=_half_scratch(rows, half),
        compiler_params=pltpu.CompilerParams(vmem_limit_bytes=60 * MIB),
    )(*toks, w)


def _tile_at(slot_ref, block, p):
    tile = block * TPD
    for i in range(1, TPD):
        tile = jnp.where(slot_ref[0, block * TPD + i] == block * TPD + p, block * TPD + i, tile)
    return tile


def _aligned(start):
    return jnp.minimum(start // 16 * 16, TILE - WIN)


def project_last(pos, toks, w, acc_in, done, done_places, places, tables):
    rows = sum(t.shape[0] for t in toks)
    half = toks[0].shape[1]
    n = toks[0].shape[0]

    def body(pos_ref, t0, t1, t2, w_ref, acc_ref, done_ref, slot, neighbour, first,
             full, near_k, near_v, far_k, far_v, t_buf, w_buf, t_sem, w_sem, acc, wide):
        block, zl, y, blocks = pos_ref[3], pos_ref[4], pos_ref[5], pos_ref[6]
        product = _half_product((t0, t1, t2), w_ref, half, t_buf, w_buf, t_sem, w_sem)

        def row_of(place):
            dzl, dy = place
            return pl.multiple_of(((zl + dzl) % NZL * NY + (y + dy + NY) % NY) * n, n)

        for i, place in enumerate(done_places):
            part = done_ref[i * n : (i + 1) * n, :]
            full[pl.ds(row_of(place), n), :] = part
            wide[pl.ds(row_of(place), n), :] = part.astype(F32)
        acc[...] = acc_ref[...]
        product(acc)
        for i, place in enumerate(places):
            part = acc[i * n : (i + 1) * n, :].astype(BF16)
            full[pl.ds(row_of(place), n), :] = part
            wide[pl.ds(row_of(place), n), :] = part.astype(F32)
        up = 1 - 2 * pos_ref[2]
        for keys, values, step in ((far_k, far_v, -up), (near_k, near_v, up)):
            target = (block + step + blocks) % blocks

            def pick(p, carry, keys=keys, values=values, target=target):
                tile = _tile_at(slot, target, p)
                seen = jnp.int32(0)
                starts = [jnp.int32(0), jnp.int32(0)]
                for j in range(NB):
                    other = neighbour[j, tile]
                    hit = other // TPD == block
                    row = slot[0, other] % TPD * TILE + first[j, tile]
                    for o in range(2):
                        take = jnp.logical_and(hit, seen == o)
                        starts[o] = jnp.where(take, row, starts[o])
                    seen = seen + hit.astype(jnp.int32)
                for o in range(2):
                    al = pl.multiple_of(starts[o] // 8 * 8, 8)
                    rem = starts[o] - al
                    window = pltpu.roll(
                        wide[pl.ds(al, SLAB + 8), :], (SLAB + 8 - rem) % (SLAB + 8), 0
                    )
                    at = pl.multiple_of((p * 2 + o) * SLAB, SLAB)
                    keys[pl.ds(at, SLAB), :] = window[:SLAB, :384].astype(BF16)
                    values[pl.ds(at, SLAB), :] = window[:SLAB, 384:].astype(BF16)
                return carry

            lax.fori_loop(0, TPD, pick, 0)

    return pl.pallas_call(
        body,
        out_shape=[jax.ShapeDtypeStruct((TPD * TILE, 768), BF16)]
        + [jax.ShapeDtypeStruct((HALO, 384), BF16)] * 4,
        in_specs=[SM] + [ANY] * 4 + [VM, VM] + [SM] * 3,
        out_specs=[VM] * 5,
        scratch_shapes=_half_scratch(rows, half)
        + [pltpu.VMEM((rows, 768), F32), pltpu.VMEM((TPD * TILE + 8, 768), F32)],
        compiler_params=pltpu.CompilerParams(vmem_limit_bytes=24 * MIB),
    )(pos, *toks, w, acc_in, done, *tables)


CAND = 768


def _clear_rest(cand):
    cand[pl.ds(TILE + NB * WIN, CAND - TILE - NB * WIN), :] = jnp.zeros(
        (CAND - TILE - NB * WIN, 384), BF16
    )
    for j in range(NB):
        cand[pl.ds(TILE + j * WIN + SLAB, WIN - SLAB), :] = jnp.zeros((WIN - SLAB, 384), BF16)


def _collect(p, pos_ref, slot, neighbour, first, full_ref, near_ref, far_ref, cand, side):
    block, blocks = pos_ref[3], pos_ref[6]
    cols = slice(side * 384, side * 384 + 384)
    tile = _tile_at(slot, block, p)
    own = pl.multiple_of(p * TILE, TILE)
    cand[pl.ds(0, TILE), :] = full_ref[pl.ds(own, TILE), cols]
    up = 1 - 2 * pos_ref[2]
    near_block = (block + up + blocks) % blocks
    far_block = (block - up + blocks) % blocks
    seen_near = jnp.int32(0)
    seen_far = jnp.int32(0)
    places = []
    for j in range(NB):
        other = neighbour[j, tile]
        at = other // TPD
        is_near = at == near_block
        is_far = at == far_block
        s = first[j, tile]
        al = _aligned(s)
        c0 = TILE + j * WIN
        begin = slot[0, other] % TPD * TILE + al
        away = jnp.logical_or(is_near, is_far)

        @pl.when(is_near)
        def _(c0=c0, seen=seen_near):
            row = pl.multiple_of((p * 2 + seen) * SLAB, SLAB)
            cand[pl.ds(c0, SLAB), :] = near_ref[pl.ds(row, SLAB), :]

        @pl.when(is_far)
        def _(c0=c0, seen=seen_far):
            row = pl.multiple_of((p * 2 + seen) * SLAB, SLAB)
            cand[pl.ds(c0, SLAB), :] = far_ref[pl.ds(row, SLAB), :]

        @pl.when(jnp.logical_not(away))
        def _(c0=c0, begin=begin):
            cand[pl.ds(c0, WIN), :] = full_ref[pl.ds(pl.multiple_of(begin, 16), WIN), cols]

        places.append(c0 + jnp.where(away, 0, s - al))
        seen_near = seen_near + is_near.astype(jnp.int32)
        seen_far = seen_far + is_far.astype(jnp.int32)
    return tile, places


def weigh(pos, queries, full, near_k, far_k, tables):
    scale = 1.0 / math.sqrt(HD)

    def body(pos_ref, q_ref, full_ref, near_ref, far_ref, slot, neighbour, first, length,
             low, high, prob, total, cand):
        p = pl.program_id(0)

        @pl.when(p == 0)
        def _():
            _clear_rest(cand)

        tile, places = _collect(
            p, pos_ref, slot, neighbour, first, full_ref, near_ref, far_ref, cand, 0
        )
        col = lax.broadcasted_iota(jnp.int32, (8, CAND), 1)
        lows = jnp.where(col < TILE, 0, TILE)
        highs = jnp.where(col < TILE, TILE, 0)
        for j in range(NB):
            valid = jnp.logical_and(col >= places[j], col < places[j] + length[j, tile])
            lows = jnp.where(valid, low[j, tile], lows)
            highs = jnp.where(valid, high[j, tile], highs)
        row = lax.broadcasted_iota(jnp.int32, (TILE, CAND), 0)
        allowed = jnp.logical_and(row >= lows[0:1, :], row < highs[0:1, :])
        for h in range(3):
            cols = slice(h * HD, h * HD + HD)
            scores = lax.dot_general(
                q_ref[:, cols],
                cand[:, cols],
                (((1,), (1,)), ((), ())),
                preferred_element_type=F32,
            ) * scale
            scores = jnp.where(allowed, scores, -jnp.inf)
            top = jnp.max(scores, axis=-1, keepdims=True)
            weights = jnp.exp(scores - top)
            total[:, cols] = jnp.broadcast_to(
                jnp.sum(weights, axis=-1, keepdims=True), (TILE, HD)
            )
            prob[0, h] = weights.astype(BF16)

    return pl.pallas_call(
        body,
        grid=(TPD,),
        out_shape=[
            jax.ShapeDtypeStruct((TPD, 3, TILE, CAND), BF16),
            jax.ShapeDtypeStruct((TPD * TILE, 384), F32),
        ],
        in_specs=[SM, pl.BlockSpec((TILE, 384), lambda p: (p, 0)), VM, VM, VM] + [SM] * 6,
        out_specs=[
            pl.BlockSpec((1, 3, TILE, CAND), lambda p: (p, 0, 0, 0)),
            pl.BlockSpec((TILE, 384), lambda p: (p, 0)),
        ],
        scratch_shapes=[pltpu.VMEM((CAND, 384), BF16)],
        compiler_params=pltpu.CompilerParams(vmem_limit_bytes=24 * MIB),
    )(pos, queries, full, near_k, far_k, *tables)


def mix(pos, prob, total, full, near_v, far_v, tables):
    def body(pos_ref, prob_ref, total_ref, full_ref, near_ref, far_ref, slot, neighbour, first,
             out, cand):
        p = pl.program_id(0)

        @pl.when(p == 0)
        def _():
            _clear_rest(cand)

        _collect(p, pos_ref, slot, neighbour, first, full_ref, near_ref, far_ref, cand, 1)
        for h in range(3):
            cols = slice(h * HD, h * HD + HD)
            mixed = jnp.dot(prob_ref[0, h], cand[:, cols], preferred_element_type=F32)
            out[:, cols] = (mixed / total_ref[:, cols]).astype(BF16)

    return pl.pallas_call(
        body,
        grid=(TPD,),
        out_shape=jax.ShapeDtypeStruct((TPD * TILE, 384), BF16),
        in_specs=[
            SM,
            pl.BlockSpec((1, 3, TILE, CAND), lambda p: (p, 0, 0, 0)),
            pl.BlockSpec((TILE, 384), lambda p: (p, 0)),
            VM,
            VM,
            VM,
        ]
        + [SM] * 3,
        out_specs=pl.BlockSpec((TILE, 384), lambda p: (p, 0)),
        scratch_shapes=[pltpu.VMEM((CAND, 384), BF16)],
        compiler_params=pltpu.CompilerParams(vmem_limit_bytes=24 * MIB),
    )(pos, prob, total, full, near_v, far_v, *tables)


def per_device(
    tokens,
    queries,
    w_key,
    w_value,
    tile_slot,
    neighbour_tile,
    slab_start,
    slab_length,
    window_low,
    window_high,
):
    fs = w_key.shape[0]
    ctx = lax.axis_index("ctx")
    tp = lax.axis_index("tp")
    pos = jnp.stack(
        [ctx >> 3, (ctx >> 1) & 3, ctx & 1, ctx, tp >> 2, tp & 3, jnp.int32(lax.axis_size("ctx"))]
    ).astype(jnp.int32)
    tables = (
        tile_slot.reshape(1, -1),
        neighbour_tile.T,
        slab_start.T,
        slab_length.T,
        window_low.T,
        window_high.T,
    )

    h = tokens.shape[1] // 2
    w = join(w_key, w_value, space=HBM)
    wc = send(w, dc=1)
    ya = send(tokens, dy=1)
    z1w = send(w, sz=1)
    yb = send(tokens, dy=-1)
    z1c = send(wc, sz=1)
    xw1 = send(w, sx=1)
    xc1 = send(wc, sx=1)
    z2 = send(z1w, sz=1)
    xw2 = send(xw1, sx=1)
    tl, tr = tokens[:, :h], tokens[:, h:]
    z_l = send(tl, dzl=1)
    near = join(z1w, z1c, z2)
    xn1 = send(near, sx=1)
    far = send(near, dc=1)
    z_r = send(tr, dzl=1)
    xf1 = send(far, sx=1)
    yo_l = send(ya[:, :h], dy=1)
    yo_r = send(yb[:, h:], dy=-1)
    xn2 = send(xn1, sx=1)
    ua_l = send(z_l, dy=1)
    ub_l = send(z_l, dy=-1)
    uo_l = send(yo_l, dzl=1)
    uo_r = send(yo_r, dzl=1)
    ua_r = send(z_r, dy=1)
    ub_r = send(z_r, dy=-1)
    pieces = [
        (w, 0, False, 0, SAME),
        (wc, 0, False, 0, OTHER),
        (near, 0, False, 0, NEAR),
        (far, 0, False, 0, FAR),
    ]
    for p, xrel, signed, plan in (
        (xw1, 1, True, SAME),
        (xc1, 1, True, OTHER),
        (xw2, 2, False, SAME),
        (xn1, 1, True, NEAR),
        (xf1, 1, True, FAR),
        (xn2, 2, False, NEAR),
    ):
        pieces += [(p, xrel, signed, 0, plan), (send(p, dc=1), xrel, signed, 1, plan)]

    n = tokens.shape[0]
    toks = (tokens, ya, yb, yo_l, yo_r, z_l, z_r)
    at = ((0, 0), (n, 0), (2 * n, 0), (3 * n, 0), (3 * n, h), (4 * n, 0), (4 * n, h))
    kv1, w_all = project(pos, toks, at, 5 * n, pieces, fs)
    part = project_half((ua_l, ub_l, uo_l), w_all)
    full, *slabs = project_last(
        pos,
        (ua_r, ub_r, uo_r),
        w_all,
        part,
        kv1,
        ((0, 0), (0, -1), (0, 1), (0, 2), (1, 0)),
        ((1, -1), (1, 1), (1, 2)),
        tables[:3],
    )
    near_k, near_v, far_k, far_v = slabs
    far_k = send(far_k, far=1)
    near_k = send(near_k, dc=1)
    far_v = send(far_v, far=1)
    near_v = send(near_v, dc=1)
    prob, total = weigh(pos, queries, full, near_k, far_k, tables)
    return mix(pos, prob, total, full, near_v, far_v, tables[:3])


def solution(mesh):
    in_specs = (
        P(("ctx", "tp"), None),
        P("ctx", "tp"),
        P("ctx", "tp"),
        P("ctx", "tp"),
        P(),
        P(),
        P(),
        P(),
        P(),
        P(),
    )
    out_specs = P("ctx", "tp")
    return jax.shard_map(
        per_device, mesh=mesh, in_specs=in_specs, out_specs=out_specs, check_vma=False
    )
```

```python
import math

import jax
import jax.numpy as jnp
from jax import lax
from jax.experimental import pallas as pl
from jax.experimental.pallas import tpu as pltpu
from jax.sharding import PartitionSpec as P


HD = 128
TILE = 256
NB = 6
SLAB = 64
TPD = 4
HALO = TPD * 2 * SLAB
WIN = 80
NX, NZH, NC, NZL, NY = 4, 4, 2, 2, 4
AXES = ("ctx", "tp")
BF16 = jnp.bfloat16
F32 = jnp.float32


def _index(x, zh, c, zl, y):
    return (((x % NX) * NZH + zh % NZH) * NC + c % NC) * (NZL * NY) + zl % NZL * NY + y % NY


def _moves(dx=0, dzh=0, dc=0, dzl=0, dy=0, sx=0, sz=0):
    pairs = []
    for x in range(NX):
        for zh in range(NZH):
            for c in range(NC):
                for zl in range(NZL):
                    for y in range(NY):
                        pairs.append(
                            (
                                _index(x, zh, c, zl, y),
                                _index(
                                    x + dx + sx * (1 - 2 * c),
                                    zh + dzh + sz * (1 - 2 * c),
                                    c + dc,
                                    zl + dzl,
                                    y + dy,
                                ),
                            )
                        )
    return pairs


def _far_moves():
    blocks = NX * NZH * NC
    tps = NZL * NY
    return [
        (b * tps + t, (b - 1 + 2 * (b % 2)) % blocks * tps + t)
        for b in range(blocks)
        for t in range(tps)
    ]


def send(a, **step):
    return lax.ppermute(a, AXES, _far_moves() if "far" in step else _moves(**step))


SAME = ((0, False, 0),)
OTHER = ((0, False, 1),)
NEAR = ((1, True, 0), (1, True, 1), (2, False, 0))
FAR = ((-1, True, 1), (-1, True, 0), (2, False, 1))


ANY = pl.BlockSpec(memory_space=pl.ANY)
HBM = pl.BlockSpec(memory_space=pltpu.HBM)
SM = pl.BlockSpec(memory_space=pltpu.SMEM)
VM = pl.BlockSpec(memory_space=pltpu.VMEM)
MIB = 1024 * 1024


def join(*parts, space=None):
    rows = [p.shape[0] for p in parts]

    def body(*refs):
        out, sems = refs[-2:]
        copies = []
        for i, ref in enumerate(refs[:-2]):
            copies.append(
                pltpu.make_async_copy(ref, out.at[pl.ds(sum(rows[:i]), rows[i]), :], sems.at[i])
            )
        for cp in copies:
            cp.start()
        for cp in copies:
            cp.wait()

    return pl.pallas_call(
        body,
        out_shape=jax.ShapeDtypeStruct((sum(rows), parts[0].shape[1]), parts[0].dtype),
        in_specs=[space or ANY] * len(parts),
        out_specs=ANY,
        scratch_shapes=[pltpu.SemaphoreType.DMA((len(parts),))],
        compiler_params=pltpu.CompilerParams(vmem_limit_bytes=MIB),
    )(*parts)


def project(pos, toks, tok_at, rows, pieces, fs):
    nt, np_ = len(toks), len(pieces)
    features = fs * NX * NZH * NC
    quarter = features // NX

    def body(*refs):
        pos_ref = refs[0]
        tok_refs = refs[1 : 1 + nt]
        piece_refs = refs[1 + nt : 1 + nt + np_]
        out, w_out, t_buf, w_buf, acc, t_sem, w_sem, o_sem = refs[1 + nt + np_ :]
        x, zh, c = pos_ref[0], pos_ref[1], pos_ref[2]
        waits = []
        for ref, (_, xrel, signed, flip, plan) in zip(piece_refs, pieces):
            core = (c + flip) % NC
            sign = 2 * core - 1
            xs = (x + (sign * xrel if signed else xrel) + NX) % NX
            for i, (zrel, zsigned, other) in enumerate(plan):
                zs = (zh + (sign * zrel if zsigned else zrel) + NZH) % NZH
                place = pl.multiple_of(((xs * NZH + zs) * NC + (core + other) % NC) * fs, 32)
                for kv in range(2):
                    cp = pltpu.make_async_copy(
                        ref.at[pl.ds((2 * i + kv) * fs, fs), :],
                        w_buf.at[pl.ds(place, fs), pl.ds(kv * 384, 384)],
                        w_sem.at[len(waits)],
                    )
                    cp.start()
                    waits.append(cp)
        for i, (ref, (r0, c0)) in enumerate(zip(tok_refs, tok_at)):
            cp = pltpu.make_async_copy(
                ref,
                t_buf.at[pl.ds(r0, ref.shape[0]), pl.ds(c0, ref.shape[1])],
                t_sem.at[i],
            )
            cp.start()
            waits.append(cp)
        for cp in waits:
            cp.wait()
        back = pltpu.make_async_copy(w_buf, w_out, o_sem)
        back.start()
        for q in range(NX):
            part = jnp.dot(
                t_buf[:, q * quarter : (q + 1) * quarter],
                w_buf[q * quarter : (q + 1) * quarter, :],
                preferred_element_type=F32,
            )
            if q == 0:
                acc[...] = part
            elif q < NX - 1:
                acc[...] += part
            else:
                out[...] = (acc[...] + part).astype(BF16)
        back.wait()

    n_copies = 2 * sum(len(p[4]) for p in pieces)
    return pl.pallas_call(
        body,
        out_shape=[
            jax.ShapeDtypeStruct((rows, 768), BF16),
            jax.ShapeDtypeStruct((features, 768), BF16),
        ],
        in_specs=[SM] + [HBM] * (nt + np_),
        out_specs=[VM, ANY],
        scratch_shapes=[
            pltpu.VMEM((rows, features), BF16),
            pltpu.VMEM((features, 768), BF16),
            pltpu.VMEM((rows, 768), F32),
            pltpu.SemaphoreType.DMA((nt,)),
            pltpu.SemaphoreType.DMA((n_copies,)),
            pltpu.SemaphoreType.DMA,
        ],
        compiler_params=pltpu.CompilerParams(vmem_limit_bytes=60 * MIB),
    )(pos, *toks, *[p[0] for p in pieces])


def _half_product(toks, w, row0, cols, t_buf, w_buf, t_sem, w_sem):
    n = toks[0].shape[0]
    half = toks[0].shape[1]
    step = half // 2
    waits = []
    for i, ref in enumerate(toks):
        waits.append(pltpu.make_async_copy(ref, t_buf.at[pl.ds(i * n, n), :], t_sem.at[i]))
    loads = [
        pltpu.make_async_copy(
            w.at[pl.ds(row0 + i * step, step), pl.ds(*cols)],
            w_buf.at[pl.ds(i * step, step), :],
            w_sem.at[i],
        )
        for i in range(2)
    ]
    for cp in loads[:1] + waits + loads[1:]:
        cp.start()

    def product(acc):
        for cp in waits:
            cp.wait()
        for i in range(2):
            loads[i].wait()
            acc[...] += jnp.dot(
                t_buf[:, i * step : (i + 1) * step],
                w_buf[i * step : (i + 1) * step, :],
                preferred_element_type=F32,
            )

    return product


def _half_scratch(rows, half, width):
    return [
        pltpu.VMEM((rows, half), BF16),
        pltpu.VMEM((half, width), BF16),
        pltpu.SemaphoreType.DMA((3,)),
        pltpu.SemaphoreType.DMA((2,)),
    ]


def project_half(toks, w):
    rows = sum(t.shape[0] for t in toks)
    half = toks[0].shape[1]

    def body(t0, t1, t2, w_ref, acc, t_buf, w_buf, t_sem, w_sem):
        product = _half_product((t0, t1, t2), w_ref, 0, (0, 768), t_buf, w_buf, t_sem, w_sem)
        acc[...] = jnp.zeros_like(acc)
        product(acc)

    return pl.pallas_call(
        body,
        out_shape=jax.ShapeDtypeStruct((rows, 768), F32),
        in_specs=[ANY] * 4,
        out_specs=VM,
        scratch_shapes=_half_scratch(rows, half, 768),
        compiler_params=pltpu.CompilerParams(vmem_limit_bytes=57 * MIB),
    )(*toks, w)


def _tile_at(slot_ref, block, p):
    tile = block * TPD
    for i in range(1, TPD):
        tile = jnp.where(slot_ref[0, block * TPD + i] == block * TPD + p, block * TPD + i, tile)
    return tile


def _aligned(start):
    return jnp.minimum(start // 16 * 16, TILE - WIN)


def project_last(side, pos, toks, w, acc_in, done, done_places, places, tables):
    rows = sum(t.shape[0] for t in toks)
    half = toks[0].shape[1]
    n = toks[0].shape[0]

    def body(pos_ref, t0, t1, t2, w_ref, acc_ref, done_ref, slot, neighbour, first,
             full, near, far, t_buf, w_buf, t_sem, w_sem, acc, wide, a_sem):
        block, zl, y, blocks = pos_ref[3], pos_ref[4], pos_ref[5], pos_ref[6]
        cols = (side * 384, 384)
        begin = pltpu.make_async_copy(acc_ref.at[:, pl.ds(*cols)], acc, a_sem)
        begin.start()
        product = _half_product((t0, t1, t2), w_ref, half, cols, t_buf, w_buf, t_sem, w_sem)

        def row_of(place):
            dzl, dy = place
            return pl.multiple_of(((zl + dzl) % NZL * NY + (y + dy + NY) % NY) * n, n)

        for i, place in enumerate(done_places):
            part = done_ref[i * n : (i + 1) * n, side * 384 : side * 384 + 384]
            full[pl.ds(row_of(place), n), :] = part
            wide[pl.ds(row_of(place), n), :] = part.astype(F32)
        begin.wait()
        product(acc)
        for i, place in enumerate(places):
            part = acc[i * n : (i + 1) * n, :].astype(BF16)
            full[pl.ds(row_of(place), n), :] = part
            wide[pl.ds(row_of(place), n), :] = part.astype(F32)
        up = 1 - 2 * pos_ref[2]
        for out, step in ((far, -up), (near, up)):
            target = (block + step + blocks) % blocks

            def pick(p, carry, out=out, target=target):
                tile = _tile_at(slot, target, p)
                seen = jnp.int32(0)
                starts = [jnp.int32(0), jnp.int32(0)]
                for j in range(NB):
                    other = neighbour[j, tile]
                    hit = other // TPD == block
                    row = slot[0, other] % TPD * TILE + first[j, tile]
                    for o in range(2):
                        take = jnp.logical_and(hit, seen == o)
                        starts[o] = jnp.where(take, row, starts[o])
                    seen = seen + hit.astype(jnp.int32)
                for o in range(2):
                    al = pl.multiple_of(starts[o] // 8 * 8, 8)
                    rem = starts[o] - al
                    window = pltpu.roll(
                        wide[pl.ds(al, SLAB + 8), :], (SLAB + 8 - rem) % (SLAB + 8), 0
                    )
                    at = pl.multiple_of((p * 2 + o) * SLAB, SLAB)
                    out[pl.ds(at, SLAB), :] = window[:SLAB].astype(BF16)
                return carry

            lax.fori_loop(0, TPD, pick, 0)

    return pl.pallas_call(
        body,
        out_shape=[jax.ShapeDtypeStruct((TPD * TILE, 384), BF16)]
        + [jax.ShapeDtypeStruct((HALO, 384), BF16)] * 2,
        in_specs=[SM] + [ANY] * 5 + [VM] + [SM] * 3,
        out_specs=[VM] * 3,
        scratch_shapes=_half_scratch(rows, half, 384)
        + [pltpu.VMEM((rows, 384), F32), pltpu.VMEM((TPD * TILE + 8, 384), F32)]
        + [pltpu.SemaphoreType.DMA],
        compiler_params=pltpu.CompilerParams(vmem_limit_bytes=48 * MIB),
    )(pos, *toks, w, acc_in, done, *tables)


CAND = 768


def _clear_rest(cand):
    cand[pl.ds(TILE + NB * WIN, CAND - TILE - NB * WIN), :] = jnp.zeros(
        (CAND - TILE - NB * WIN, 384), BF16
    )
    for j in range(NB):
        cand[pl.ds(TILE + j * WIN + SLAB, WIN - SLAB), :] = jnp.zeros((WIN - SLAB, 384), BF16)


def _collect(p, pos_ref, slot, neighbour, first, full_ref, near_ref, far_ref, cand):
    block, blocks = pos_ref[3], pos_ref[6]
    tile = _tile_at(slot, block, p)
    own = pl.multiple_of(p * TILE, TILE)
    cand[pl.ds(0, TILE), :] = full_ref[pl.ds(own, TILE), :]
    up = 1 - 2 * pos_ref[2]
    near_block = (block + up + blocks) % blocks
    far_block = (block - up + blocks) % blocks
    seen_near = jnp.int32(0)
    seen_far = jnp.int32(0)
    places = []
    for j in range(NB):
        other = neighbour[j, tile]
        at = other // TPD
        is_near = at == near_block
        is_far = at == far_block
        s = first[j, tile]
        al = _aligned(s)
        c0 = TILE + j * WIN
        begin = slot[0, other] % TPD * TILE + al
        away = jnp.logical_or(is_near, is_far)

        @pl.when(is_near)
        def _(c0=c0, seen=seen_near):
            row = pl.multiple_of((p * 2 + seen) * SLAB, SLAB)
            cand[pl.ds(c0, SLAB), :] = near_ref[pl.ds(row, SLAB), :]

        @pl.when(is_far)
        def _(c0=c0, seen=seen_far):
            row = pl.multiple_of((p * 2 + seen) * SLAB, SLAB)
            cand[pl.ds(c0, SLAB), :] = far_ref[pl.ds(row, SLAB), :]

        @pl.when(jnp.logical_not(away))
        def _(c0=c0, begin=begin):
            cand[pl.ds(c0, WIN), :] = full_ref[pl.ds(pl.multiple_of(begin, 16), WIN), :]

        places.append(c0 + jnp.where(away, 0, s - al))
        seen_near = seen_near + is_near.astype(jnp.int32)
        seen_far = seen_far + is_far.astype(jnp.int32)
    return tile, places


def weigh(pos, queries, full, near_k, far_k, tables):
    scale = 1.0 / math.sqrt(HD)

    def body(pos_ref, q_ref, full_ref, near_ref, far_ref, slot, neighbour, first, length,
             low, high, prob, total, cand):
        p = pl.program_id(0)

        @pl.when(p == 0)
        def _():
            _clear_rest(cand)

        tile, places = _collect(
            p, pos_ref, slot, neighbour, first, full_ref, near_ref, far_ref, cand
        )
        col = lax.broadcasted_iota(jnp.int32, (8, CAND), 1)
        lows = jnp.where(col < TILE, 0, TILE)
        highs = jnp.where(col < TILE, TILE, 0)
        for j in range(NB):
            valid = jnp.logical_and(col >= places[j], col < places[j] + length[j, tile])
            lows = jnp.where(valid, low[j, tile], lows)
            highs = jnp.where(valid, high[j, tile], highs)
        row = lax.broadcasted_iota(jnp.int32, (TILE, CAND), 0)
        allowed = jnp.logical_and(row >= lows[0:1, :], row < highs[0:1, :])
        for h in range(3):
            cols = slice(h * HD, h * HD + HD)
            scores = lax.dot_general(
                q_ref[:, cols],
                cand[:, cols],
                (((1,), (1,)), ((), ())),
                preferred_element_type=F32,
            ) * scale
            scores = jnp.where(allowed, scores, -jnp.inf)
            top = jnp.max(scores, axis=-1, keepdims=True)
            weights = jnp.exp(scores - top)
            total[:, cols] = jnp.broadcast_to(
                jnp.sum(weights, axis=-1, keepdims=True), (TILE, HD)
            )
            prob[0, h] = weights.astype(BF16)

    return pl.pallas_call(
        body,
        grid=(TPD,),
        out_shape=[
            jax.ShapeDtypeStruct((TPD, 3, TILE, CAND), BF16),
            jax.ShapeDtypeStruct((TPD * TILE, 384), F32),
        ],
        in_specs=[SM, pl.BlockSpec((TILE, 384), lambda p: (p, 0)), VM, VM, VM] + [SM] * 6,
        out_specs=[
            pl.BlockSpec((1, 3, TILE, CAND), lambda p: (p, 0, 0, 0)),
            pl.BlockSpec((TILE, 384), lambda p: (p, 0)),
        ],
        scratch_shapes=[pltpu.VMEM((CAND, 384), BF16)],
        compiler_params=pltpu.CompilerParams(vmem_limit_bytes=24 * MIB),
    )(pos, queries, full, near_k, far_k, *tables)


def mix(pos, prob, total, full, near_v, far_v, tables):
    def body(pos_ref, prob_ref, total_ref, full_ref, near_ref, far_ref, slot, neighbour, first,
             out, cand):
        p = pl.program_id(0)

        @pl.when(p == 0)
        def _():
            _clear_rest(cand)

        _collect(p, pos_ref, slot, neighbour, first, full_ref, near_ref, far_ref, cand)
        for h in range(3):
            cols = slice(h * HD, h * HD + HD)
            mixed = jnp.dot(prob_ref[0, h], cand[:, cols], preferred_element_type=F32)
            out[:, cols] = (mixed / total_ref[:, cols]).astype(BF16)

    return pl.pallas_call(
        body,
        grid=(TPD,),
        out_shape=jax.ShapeDtypeStruct((TPD * TILE, 384), BF16),
        in_specs=[
            SM,
            pl.BlockSpec((1, 3, TILE, CAND), lambda p: (p, 0, 0, 0)),
            pl.BlockSpec((TILE, 384), lambda p: (p, 0)),
            VM,
            VM,
            VM,
        ]
        + [SM] * 3,
        out_specs=pl.BlockSpec((TILE, 384), lambda p: (p, 0)),
        scratch_shapes=[pltpu.VMEM((CAND, 384), BF16)],
        compiler_params=pltpu.CompilerParams(vmem_limit_bytes=24 * MIB),
    )(pos, prob, total, full, near_v, far_v, *tables)


def per_device(
    tokens,
    queries,
    w_key,
    w_value,
    tile_slot,
    neighbour_tile,
    slab_start,
    slab_length,
    window_low,
    window_high,
):
    fs = w_key.shape[0]
    ctx = lax.axis_index("ctx")
    tp = lax.axis_index("tp")
    pos = jnp.stack(
        [ctx >> 3, (ctx >> 1) & 3, ctx & 1, ctx, tp >> 2, tp & 3, jnp.int32(lax.axis_size("ctx"))]
    ).astype(jnp.int32)
    tables = (
        tile_slot.reshape(1, -1),
        neighbour_tile.T,
        slab_start.T,
        slab_length.T,
        window_low.T,
        window_high.T,
    )

    h = tokens.shape[1] // 2
    w = join(w_key, w_value, space=HBM)
    wc = send(w, dc=1)
    ya = send(tokens, dy=1)
    z1w = send(w, sz=1)
    yb = send(tokens, dy=-1)
    z1c = send(wc, sz=1)
    xw1 = send(w, sx=1)
    xc1 = send(wc, sx=1)
    z2 = send(z1w, sz=1)
    xw2 = send(xw1, sx=1)
    tl, tr = tokens[:, :h], tokens[:, h:]
    z_l = send(tl, dzl=1)
    near = join(z1w, z1c, z2)
    xn1 = send(near, sx=1)
    far = send(near, dc=1)
    z_r = send(tr, dzl=1)
    xf1 = send(far, sx=1)
    yo_l = send(ya[:, :h], dy=1)
    yo_r = send(yb[:, h:], dy=-1)
    xn2 = send(xn1, sx=1)
    ua_l = send(z_l, dy=1)
    ub_l = send(z_l, dy=-1)
    uo_l = send(yo_l, dzl=1)
    uo_r = send(yo_r, dzl=1)
    ua_r = send(z_r, dy=1)
    ub_r = send(z_r, dy=-1)
    pieces = [
        (w, 0, False, 0, SAME),
        (wc, 0, False, 0, OTHER),
        (near, 0, False, 0, NEAR),
        (far, 0, False, 0, FAR),
    ]
    for p, xrel, signed, plan in (
        (xw1, 1, True, SAME),
        (xc1, 1, True, OTHER),
        (xw2, 2, False, SAME),
        (xn1, 1, True, NEAR),
        (xf1, 1, True, FAR),
        (xn2, 2, False, NEAR),
    ):
        pieces += [(p, xrel, signed, 0, plan), (send(p, dc=1), xrel, signed, 1, plan)]

    n = tokens.shape[0]
    toks = (tokens, ya, yb, yo_l, yo_r, z_l, z_r)
    at = ((0, 0), (n, 0), (2 * n, 0), (3 * n, 0), (3 * n, h), (4 * n, 0), (4 * n, h))
    kv1, w_all = project(pos, toks, at, 5 * n, pieces, fs)
    part = project_half((ua_l, ub_l, uo_l), w_all)
    last = (
        kv1,
        ((0, 0), (0, -1), (0, 1), (0, 2), (1, 0)),
        ((1, -1), (1, 1), (1, 2)),
        tables[:3],
    )
    rest = (ua_r, ub_r, uo_r)
    keys, near_k, far_k = project_last(0, pos, rest, w_all, part, *last)
    part = lax.optimization_barrier((part, far_k))[0]
    far_k = send(far_k, far=1)
    near_k = send(near_k, dc=1)
    values, near_v, far_v = project_last(1, pos, rest, w_all, part, *last)
    far_v = send(far_v, far=1)
    near_v = send(near_v, dc=1)
    prob, total = weigh(pos, queries, keys, near_k, far_k, tables)
    return mix(pos, prob, total, values, near_v, far_v, tables[:3])


def solution(mesh):
    in_specs = (
        P(("ctx", "tp"), None),
        P("ctx", "tp"),
        P("ctx", "tp"),
        P("ctx", "tp"),
        P(),
        P(),
        P(),
        P(),
        P(),
        P(),
    )
    out_specs = P("ctx", "tp")
    return jax.shard_map(
        per_device, mesh=mesh, in_specs=in_specs, out_specs=out_specs, check_vma=False
    )
```

```python
import math

import jax
import jax.numpy as jnp
from jax import lax
from jax.experimental import pallas as pl
from jax.experimental.pallas import tpu as pltpu
from jax.sharding import PartitionSpec as P


HD = 128
TILE = 256
NB = 6
SLAB = 64
TPD = 4
HALO = TPD * 2 * SLAB
WIN = 80
NX, NZH, NC, NZL, NY = 4, 4, 2, 2, 4
AXES = ("ctx", "tp")
BF16 = jnp.bfloat16
F32 = jnp.float32


def _index(x, zh, c, zl, y):
    return (((x % NX) * NZH + zh % NZH) * NC + c % NC) * (NZL * NY) + zl % NZL * NY + y % NY


def _moves(dx=0, dzh=0, dc=0, dzl=0, dy=0, sx=0, sz=0):
    pairs = []
    for x in range(NX):
        for zh in range(NZH):
            for c in range(NC):
                for zl in range(NZL):
                    for y in range(NY):
                        pairs.append(
                            (
                                _index(x, zh, c, zl, y),
                                _index(
                                    x + dx + sx * (1 - 2 * c),
                                    zh + dzh + sz * (1 - 2 * c),
                                    c + dc,
                                    zl + dzl,
                                    y + dy,
                                ),
                            )
                        )
    return pairs


def _far_moves():
    blocks = NX * NZH * NC
    tps = NZL * NY
    return [
        (b * tps + t, (b - 1 + 2 * (b % 2)) % blocks * tps + t)
        for b in range(blocks)
        for t in range(tps)
    ]


def send(a, **step):
    return lax.ppermute(a, AXES, _far_moves() if "far" in step else _moves(**step))


SAME = ((0, False, 0),)
OTHER = ((0, False, 1),)
NEAR = ((1, True, 0), (1, True, 1), (2, False, 0))
FAR = ((-1, True, 1), (-1, True, 0), (2, False, 1))


ANY = pl.BlockSpec(memory_space=pl.ANY)
HBM = pl.BlockSpec(memory_space=pltpu.HBM)
SM = pl.BlockSpec(memory_space=pltpu.SMEM)
VM = pl.BlockSpec(memory_space=pltpu.VMEM)
MIB = 1024 * 1024


def join(*parts, space=None):
    rows = [p.shape[0] for p in parts]

    def body(*refs):
        out, sems = refs[-2:]
        copies = []
        for i, ref in enumerate(refs[:-2]):
            copies.append(
                pltpu.make_async_copy(ref, out.at[pl.ds(sum(rows[:i]), rows[i]), :], sems.at[i])
            )
        for cp in copies:
            cp.start()
        for cp in copies:
            cp.wait()

    return pl.pallas_call(
        body,
        out_shape=jax.ShapeDtypeStruct((sum(rows), parts[0].shape[1]), parts[0].dtype),
        in_specs=[space or ANY] * len(parts),
        out_specs=ANY,
        scratch_shapes=[pltpu.SemaphoreType.DMA((len(parts),))],
        compiler_params=pltpu.CompilerParams(vmem_limit_bytes=MIB),
    )(*parts)


def project(pos, toks, tok_at, rows, pieces, fs):
    nt, np_ = len(toks), len(pieces)
    features = fs * NX * NZH * NC
    quarter = features // NX

    def body(*refs):
        pos_ref = refs[0]
        tok_refs = refs[1 : 1 + nt]
        piece_refs = refs[1 + nt : 1 + nt + np_]
        out, w_out, t_buf, w_buf, acc, t_sem, w_sem, o_sem = refs[1 + nt + np_ :]
        x, zh, c = pos_ref[0], pos_ref[1], pos_ref[2]
        steps = (0, 2 * c - 1, 1 - 2 * c, 2)
        at = [(x + step + NX) % NX for step in steps]
        waits = [[] for _ in steps]
        count = 0
        for group in range(NX):
            for ref, (_, xrel, signed, flip, plan) in zip(piece_refs, pieces):
                if (1 + flip if signed else xrel // 2 * 3) != group:
                    continue
                core = (c + flip) % NC
                sign = 2 * core - 1
                for i, (zrel, zsigned, other) in enumerate(plan):
                    zs = (zh + (sign * zrel if zsigned else zrel) + NZH) % NZH
                    place = pl.multiple_of((zs * NC + (core + other) % NC) * fs, 32)
                    for kv in range(2):
                        cp = pltpu.make_async_copy(
                            ref.at[pl.ds((2 * i + kv) * fs, fs), :],
                            w_buf.at[at[group], pl.ds(place, fs), pl.ds(kv * 384, 384)],
                            w_sem.at[count],
                        )
                        cp.start()
                        waits[group].append(cp)
                        count += 1
            if group == 0:
                for i, (ref, (r0, c0)) in enumerate(zip(tok_refs, tok_at)):
                    for k in range(ref.shape[1] // quarter):
                        cp = pltpu.make_async_copy(
                            ref.at[:, pl.ds(k * quarter, quarter)],
                            t_buf.at[c0 // quarter + k, pl.ds(r0, ref.shape[0]), :],
                            t_sem.at[i, k],
                        )
                        cp.start()
                        waits[0].append(cp)
        backs = []
        for q in range(NX):
            for cp in waits[q]:
                cp.wait()
            back = pltpu.make_async_copy(w_buf.at[at[q]], w_out.at[at[q]], o_sem.at[q])
            back.start()
            backs.append(back)
            part = jnp.dot(t_buf[at[q]], w_buf[at[q]], preferred_element_type=F32)
            if q == 0:
                acc[...] = part
            elif q < NX - 1:
                acc[...] += part
            else:
                out[...] = (acc[...] + part).astype(BF16)
        for back in backs:
            back.wait()

    n_copies = 2 * sum(len(p[4]) for p in pieces)
    return pl.pallas_call(
        body,
        out_shape=[
            jax.ShapeDtypeStruct((rows, 768), BF16),
            jax.ShapeDtypeStruct((NX, quarter, 768), BF16),
        ],
        in_specs=[SM] + [HBM] * (nt + np_),
        out_specs=[VM, ANY],
        scratch_shapes=[
            pltpu.VMEM((NX, rows, quarter), BF16),
            pltpu.VMEM((NX, quarter, 768), BF16),
            pltpu.VMEM((rows, 768), F32),
            pltpu.SemaphoreType.DMA((nt, NX)),
            pltpu.SemaphoreType.DMA((n_copies,)),
            pltpu.SemaphoreType.DMA((NX,)),
        ],
        compiler_params=pltpu.CompilerParams(vmem_limit_bytes=36 * MIB),
    )(pos, *toks, *[p[0] for p in pieces])


def _half_product(toks, w, row0, cols, t_buf, w_buf, t_sem, w_sem):
    n = toks[0].shape[0]
    half = toks[0].shape[1]
    step = half // 2
    waits = []
    for i, ref in enumerate(toks):
        waits.append(pltpu.make_async_copy(ref, t_buf.at[pl.ds(i * n, n), :], t_sem.at[i]))
    loads = [
        pltpu.make_async_copy(
            w.at[pl.ds(row0 + i * step, step), pl.ds(*cols)],
            w_buf.at[pl.ds(i * step, step), :],
            w_sem.at[i],
        )
        for i in range(2)
    ]
    for cp in loads[:1] + waits + loads[1:]:
        cp.start()

    def product(acc):
        for cp in waits:
            cp.wait()
        for i in range(2):
            loads[i].wait()
            acc[...] += jnp.dot(
                t_buf[:, i * step : (i + 1) * step],
                w_buf[i * step : (i + 1) * step, :],
                preferred_element_type=F32,
            )

    return product


def _half_scratch(rows, half, width):
    return [
        pltpu.VMEM((rows, half), BF16),
        pltpu.VMEM((half, width), BF16),
        pltpu.SemaphoreType.DMA((3,)),
        pltpu.SemaphoreType.DMA((2,)),
    ]


def project_half(toks, w):
    rows = sum(t.shape[0] for t in toks)
    half = toks[0].shape[1]

    def body(t0, t1, t2, w_ref, acc, t_buf, w_buf, t_sem, w_sem):
        product = _half_product((t0, t1, t2), w_ref, 0, (0, 768), t_buf, w_buf, t_sem, w_sem)
        acc[...] = jnp.zeros_like(acc)
        product(acc)

    return pl.pallas_call(
        body,
        out_shape=jax.ShapeDtypeStruct((rows, 768), F32),
        in_specs=[ANY] * 4,
        out_specs=VM,
        scratch_shapes=_half_scratch(rows, half, 768),
        compiler_params=pltpu.CompilerParams(vmem_limit_bytes=48 * MIB),
    )(*toks, w)


def _tile_at(slot_ref, block, p):
    tile = block * TPD
    for i in range(1, TPD):
        tile = jnp.where(slot_ref[0, block * TPD + i] == block * TPD + p, block * TPD + i, tile)
    return tile


def _aligned(start):
    return jnp.minimum(start // 16 * 16, TILE - WIN)


def project_last(side, pos, toks, w, acc_in, done, done_places, places, tables):
    rows = sum(t.shape[0] for t in toks)
    half = toks[0].shape[1]
    n = toks[0].shape[0]

    def body(pos_ref, t0, t1, t2, w_ref, acc_ref, done_ref, slot, neighbour, first,
             full, near, far, t_buf, w_buf, t_sem, w_sem, acc, wide, a_sem):
        block, zl, y, blocks = pos_ref[3], pos_ref[4], pos_ref[5], pos_ref[6]
        cols = (side * 384, 384)
        begin = pltpu.make_async_copy(acc_ref.at[:, pl.ds(*cols)], acc, a_sem)
        begin.start()
        product = _half_product((t0, t1, t2), w_ref, half, cols, t_buf, w_buf, t_sem, w_sem)

        def row_of(place):
            dzl, dy = place
            return pl.multiple_of(((zl + dzl) % NZL * NY + (y + dy + NY) % NY) * n, n)

        for i, place in enumerate(done_places):
            part = done_ref[i * n : (i + 1) * n, side * 384 : side * 384 + 384]
            full[pl.ds(row_of(place), n), :] = part
            wide[pl.ds(row_of(place), n), :] = part.astype(F32)
        begin.wait()
        product(acc)
        for i, place in enumerate(places):
            part = acc[i * n : (i + 1) * n, :].astype(BF16)
            full[pl.ds(row_of(place), n), :] = part
            wide[pl.ds(row_of(place), n), :] = part.astype(F32)
        up = 1 - 2 * pos_ref[2]
        for out, step in ((far, -up), (near, up)):
            target = (block + step + blocks) % blocks

            def pick(p, carry, out=out, target=target):
                tile = _tile_at(slot, target, p)
                seen = jnp.int32(0)
                starts = [jnp.int32(0), jnp.int32(0)]
                for j in range(NB):
                    other = neighbour[j, tile]
                    hit = other // TPD == block
                    row = slot[0, other] % TPD * TILE + first[j, tile]
                    for o in range(2):
                        take = jnp.logical_and(hit, seen == o)
                        starts[o] = jnp.where(take, row, starts[o])
                    seen = seen + hit.astype(jnp.int32)
                for o in range(2):
                    al = pl.multiple_of(starts[o] // 8 * 8, 8)
                    rem = starts[o] - al
                    window = pltpu.roll(
                        wide[pl.ds(al, SLAB + 8), :], (SLAB + 8 - rem) % (SLAB + 8), 0
                    )
                    at = pl.multiple_of((p * 2 + o) * SLAB, SLAB)
                    out[pl.ds(at, SLAB), :] = window[:SLAB].astype(BF16)
                return carry

            lax.fori_loop(0, TPD, pick, 0)

    return pl.pallas_call(
        body,
        out_shape=[jax.ShapeDtypeStruct((TPD * TILE, 384), BF16)]
        + [jax.ShapeDtypeStruct((HALO, 384), BF16)] * 2,
        in_specs=[SM] + [ANY] * 5 + [VM] + [SM] * 3,
        out_specs=[VM] * 3,
        scratch_shapes=_half_scratch(rows, half, 384)
        + [pltpu.VMEM((rows, 384), F32), pltpu.VMEM((TPD * TILE + 8, 384), F32)]
        + [pltpu.SemaphoreType.DMA],
        compiler_params=pltpu.CompilerParams(vmem_limit_bytes=48 * MIB),
    )(pos, *toks, w, acc_in, done, *tables)


CAND = 768


def _clear_rest(cand):
    cand[pl.ds(TILE + NB * WIN, CAND - TILE - NB * WIN), :] = jnp.zeros(
        (CAND - TILE - NB * WIN, 384), BF16
    )
    for j in range(NB):
        cand[pl.ds(TILE + j * WIN + SLAB, WIN - SLAB), :] = jnp.zeros((WIN - SLAB, 384), BF16)


def _collect(p, pos_ref, slot, neighbour, first, full_ref, near_ref, far_ref, cand):
    block, blocks = pos_ref[3], pos_ref[6]
    tile = _tile_at(slot, block, p)
    own = pl.multiple_of(p * TILE, TILE)
    cand[pl.ds(0, TILE), :] = full_ref[pl.ds(own, TILE), :]
    up = 1 - 2 * pos_ref[2]
    near_block = (block + up + blocks) % blocks
    far_block = (block - up + blocks) % blocks
    seen_near = jnp.int32(0)
    seen_far = jnp.int32(0)
    places = []
    for j in range(NB):
        other = neighbour[j, tile]
        at = other // TPD
        is_near = at == near_block
        is_far = at == far_block
        s = first[j, tile]
        al = _aligned(s)
        c0 = TILE + j * WIN
        begin = slot[0, other] % TPD * TILE + al
        away = jnp.logical_or(is_near, is_far)

        @pl.when(is_near)
        def _(c0=c0, seen=seen_near):
            row = pl.multiple_of((p * 2 + seen) * SLAB, SLAB)
            cand[pl.ds(c0, SLAB), :] = near_ref[pl.ds(row, SLAB), :]

        @pl.when(is_far)
        def _(c0=c0, seen=seen_far):
            row = pl.multiple_of((p * 2 + seen) * SLAB, SLAB)
            cand[pl.ds(c0, SLAB), :] = far_ref[pl.ds(row, SLAB), :]

        @pl.when(jnp.logical_not(away))
        def _(c0=c0, begin=begin):
            cand[pl.ds(c0, WIN), :] = full_ref[pl.ds(pl.multiple_of(begin, 16), WIN), :]

        places.append(c0 + jnp.where(away, 0, s - al))
        seen_near = seen_near + is_near.astype(jnp.int32)
        seen_far = seen_far + is_far.astype(jnp.int32)
    return tile, places


def weigh(pos, queries, full, near_k, far_k, tables):
    scale = 1.0 / math.sqrt(HD)

    def body(pos_ref, q_ref, full_ref, near_ref, far_ref, slot, neighbour, first, length,
             low, high, prob, total, cand):
        p = pl.program_id(0)

        @pl.when(p == 0)
        def _():
            _clear_rest(cand)

        tile, places = _collect(
            p, pos_ref, slot, neighbour, first, full_ref, near_ref, far_ref, cand
        )
        col = lax.broadcasted_iota(jnp.int32, (8, CAND), 1)
        lows = jnp.where(col < TILE, 0, TILE)
        highs = jnp.where(col < TILE, TILE, 0)
        for j in range(NB):
            valid = jnp.logical_and(col >= places[j], col < places[j] + length[j, tile])
            lows = jnp.where(valid, low[j, tile], lows)
            highs = jnp.where(valid, high[j, tile], highs)
        row = lax.broadcasted_iota(jnp.int32, (TILE, CAND), 0)
        allowed = jnp.logical_and(row >= lows[0:1, :], row < highs[0:1, :])
        for h in range(3):
            cols = slice(h * HD, h * HD + HD)
            scores = lax.dot_general(
                q_ref[:, cols],
                cand[:, cols],
                (((1,), (1,)), ((), ())),
                preferred_element_type=F32,
            ) * scale
            scores = jnp.where(allowed, scores, -jnp.inf)
            top = jnp.max(scores, axis=-1, keepdims=True)
            weights = jnp.exp(scores - top)
            total[:, cols] = jnp.broadcast_to(
                jnp.sum(weights, axis=-1, keepdims=True), (TILE, HD)
            )
            prob[0, h] = weights.astype(BF16)

    return pl.pallas_call(
        body,
        grid=(TPD,),
        out_shape=[
            jax.ShapeDtypeStruct((TPD, 3, TILE, CAND), BF16),
            jax.ShapeDtypeStruct((TPD * TILE, 384), F32),
        ],
        in_specs=[SM, pl.BlockSpec((TILE, 384), lambda p: (p, 0)), VM, VM, VM] + [SM] * 6,
        out_specs=[
            pl.BlockSpec((1, 3, TILE, CAND), lambda p: (p, 0, 0, 0)),
            pl.BlockSpec((TILE, 384), lambda p: (p, 0)),
        ],
        scratch_shapes=[pltpu.VMEM((CAND, 384), BF16)],
        compiler_params=pltpu.CompilerParams(vmem_limit_bytes=24 * MIB),
    )(pos, queries, full, near_k, far_k, *tables)


def mix(pos, prob, total, full, near_v, far_v, tables):
    def body(pos_ref, prob_ref, total_ref, full_ref, near_ref, far_ref, slot, neighbour, first,
             out, cand):
        p = pl.program_id(0)

        @pl.when(p == 0)
        def _():
            _clear_rest(cand)

        _collect(p, pos_ref, slot, neighbour, first, full_ref, near_ref, far_ref, cand)
        for h in range(3):
            cols = slice(h * HD, h * HD + HD)
            mixed = jnp.dot(prob_ref[0, h], cand[:, cols], preferred_element_type=F32)
            out[:, cols] = (mixed / total_ref[:, cols]).astype(BF16)

    return pl.pallas_call(
        body,
        grid=(TPD,),
        out_shape=jax.ShapeDtypeStruct((TPD * TILE, 384), BF16),
        in_specs=[
            SM,
            pl.BlockSpec((1, 3, TILE, CAND), lambda p: (p, 0, 0, 0)),
            pl.BlockSpec((TILE, 384), lambda p: (p, 0)),
            VM,
            VM,
            VM,
        ]
        + [SM] * 3,
        out_specs=pl.BlockSpec((TILE, 384), lambda p: (p, 0)),
        scratch_shapes=[pltpu.VMEM((CAND, 384), BF16)],
        compiler_params=pltpu.CompilerParams(vmem_limit_bytes=24 * MIB),
    )(pos, prob, total, full, near_v, far_v, *tables)


def per_device(
    tokens,
    queries,
    w_key,
    w_value,
    tile_slot,
    neighbour_tile,
    slab_start,
    slab_length,
    window_low,
    window_high,
):
    fs = w_key.shape[0]
    ctx = lax.axis_index("ctx")
    tp = lax.axis_index("tp")
    pos = jnp.stack(
        [ctx >> 3, (ctx >> 1) & 3, ctx & 1, ctx, tp >> 2, tp & 3, jnp.int32(lax.axis_size("ctx"))]
    ).astype(jnp.int32)
    tables = (
        tile_slot.reshape(1, -1),
        neighbour_tile.T,
        slab_start.T,
        slab_length.T,
        window_low.T,
        window_high.T,
    )

    h = tokens.shape[1] // 2
    w = join(w_key, w_value, space=HBM)
    wc = send(w, dc=1)
    ya = send(tokens, dy=1)
    z1w = send(w, sz=1)
    yb = send(tokens, dy=-1)
    z1c = send(wc, sz=1)
    xw1 = send(w, sx=1)
    xc1 = send(wc, sx=1)
    z2 = send(z1w, sz=1)
    xw1, pos = lax.optimization_barrier((xw1, pos))
    xw2 = send(xw1, sx=1)
    tl, tr = tokens[:, :h], tokens[:, h:]
    z_l = send(tl, dzl=1)
    near = join(z1w, z1c, z2)
    xn1 = send(near, sx=1)
    far = send(near, dc=1)
    z_r = send(tr, dzl=1)
    xf1 = send(far, sx=1)
    yo_l = send(ya[:, :h], dy=1)
    yo_r = send(yb[:, h:], dy=-1)
    xn2 = send(xn1, sx=1)
    ua_l = send(z_l, dy=1)
    ub_l = send(z_l, dy=-1)
    uo_l = send(yo_l, dzl=1)
    uo_r = send(yo_r, dzl=1)
    ua_r = send(z_r, dy=1)
    ub_r = send(z_r, dy=-1)
    pieces = [
        (w, 0, False, 0, SAME),
        (wc, 0, False, 0, OTHER),
        (near, 0, False, 0, NEAR),
        (far, 0, False, 0, FAR),
    ]
    for p, xrel, signed, plan in (
        (xw1, 1, True, SAME),
        (xc1, 1, True, OTHER),
        (xw2, 2, False, SAME),
        (xn1, 1, True, NEAR),
        (xf1, 1, True, FAR),
        (xn2, 2, False, NEAR),
    ):
        pieces += [(p, xrel, signed, 0, plan), (send(p, dc=1), xrel, signed, 1, plan)]

    n = tokens.shape[0]
    toks = (tokens, ya, yb, yo_l, yo_r, z_l, z_r)
    at = ((0, 0), (n, 0), (2 * n, 0), (3 * n, 0), (3 * n, h), (4 * n, 0), (4 * n, h))
    kv1, w_all = project(pos, toks, at, 5 * n, pieces, fs)
    w_all = w_all.reshape(tokens.shape[1], 768)
    part = project_half((ua_l, ub_l, uo_l), w_all)
    last = (
        kv1,
        ((0, 0), (0, -1), (0, 1), (0, 2), (1, 0)),
        ((1, -1), (1, 1), (1, 2)),
        tables[:3],
    )
    rest = (ua_r, ub_r, uo_r)
    keys, near_k, far_k = project_last(0, pos, rest, w_all, part, *last)
    part = lax.optimization_barrier((part, far_k))[0]
    far_k = send(far_k, far=1)
    near_k = send(near_k, dc=1)
    values, near_v, far_v = project_last(1, pos, rest, w_all, part, *last)
    far_v = send(far_v, far=1)
    near_v = send(near_v, dc=1)
    prob, total = weigh(pos, queries, keys, near_k, far_k, tables)
    return mix(pos, prob, total, values, near_v, far_v, tables[:3])


def solution(mesh):
    in_specs = (
        P(("ctx", "tp"), None),
        P("ctx", "tp"),
        P("ctx", "tp"),
        P("ctx", "tp"),
        P(),
        P(),
        P(),
        P(),
        P(),
        P(),
    )
    out_specs = P("ctx", "tp")
    return jax.shard_map(
        per_device, mesh=mesh, in_specs=in_specs, out_specs=out_specs, check_vma=False
    )
```

```python
import math

import jax
import jax.numpy as jnp
from jax import lax
from jax.experimental import pallas as pl
from jax.experimental.pallas import tpu as pltpu
from jax.sharding import PartitionSpec as P


HD = 128
TILE = 256
NB = 6
SLAB = 64
TPD = 4
HALO = TPD * 2 * SLAB
WIN = 80
NX, NZH, NC, NZL, NY = 4, 4, 2, 2, 4
AXES = ("ctx", "tp")
BF16 = jnp.bfloat16
F32 = jnp.float32


def _index(x, zh, c, zl, y):
    return (((x % NX) * NZH + zh % NZH) * NC + c % NC) * (NZL * NY) + zl % NZL * NY + y % NY


def _moves(dx=0, dzh=0, dc=0, dzl=0, dy=0, sx=0, sz=0):
    pairs = []
    for x in range(NX):
        for zh in range(NZH):
            for c in range(NC):
                for zl in range(NZL):
                    for y in range(NY):
                        pairs.append(
                            (
                                _index(x, zh, c, zl, y),
                                _index(
                                    x + dx + sx * (1 - 2 * c),
                                    zh + dzh + sz * (1 - 2 * c),
                                    c + dc,
                                    zl + dzl,
                                    y + dy,
                                ),
                            )
                        )
    return pairs


def _far_moves():
    blocks = NX * NZH * NC
    tps = NZL * NY
    return [
        (b * tps + t, (b - 1 + 2 * (b % 2)) % blocks * tps + t)
        for b in range(blocks)
        for t in range(tps)
    ]


def send(a, **step):
    return lax.ppermute(a, AXES, _far_moves() if "far" in step else _moves(**step))


SAME = ((0, False, 0),)
OTHER = ((0, False, 1),)
NEAR = ((1, True, 0), (1, True, 1), (2, False, 0))
FAR = ((-1, True, 1), (-1, True, 0), (2, False, 1))


ANY = pl.BlockSpec(memory_space=pl.ANY)
HBM = pl.BlockSpec(memory_space=pltpu.HBM)
SM = pl.BlockSpec(memory_space=pltpu.SMEM)
VM = pl.BlockSpec(memory_space=pltpu.VMEM)
MIB = 1024 * 1024


def join(*parts, space=None):
    rows = [p.shape[0] for p in parts]

    def body(*refs):
        out, sems = refs[-2:]
        copies = []
        for i, ref in enumerate(refs[:-2]):
            copies.append(
                pltpu.make_async_copy(ref, out.at[pl.ds(sum(rows[:i]), rows[i]), :], sems.at[i])
            )
        for cp in copies:
            cp.start()
        for cp in copies:
            cp.wait()

    return pl.pallas_call(
        body,
        out_shape=jax.ShapeDtypeStruct((sum(rows), parts[0].shape[1]), parts[0].dtype),
        in_specs=[space or ANY] * len(parts),
        out_specs=ANY,
        scratch_shapes=[pltpu.SemaphoreType.DMA((len(parts),))],
        compiler_params=pltpu.CompilerParams(vmem_limit_bytes=MIB),
    )(*parts)


def project(pos, toks, tok_at, rows, pieces, fs):
    nt, np_ = len(toks), len(pieces)
    features = fs * NX * NZH * NC
    quarter = features // NX

    def body(*refs):
        pos_ref = refs[0]
        tok_refs = refs[1 : 1 + nt]
        piece_refs = refs[1 + nt : 1 + nt + np_]
        out, w_out, t_buf, w_buf, acc, t_sem, w_sem, o_sem = refs[1 + nt + np_ :]
        x, zh, c = pos_ref[0], pos_ref[1], pos_ref[2]
        steps = (0, 2 * c - 1, 1 - 2 * c, 2)
        at = [(x + step + NX) % NX for step in steps]
        waits = [[] for _ in steps]
        count = 0
        for group in range(NX):
            for ref, (_, xrel, signed, flip, plan) in zip(piece_refs, pieces):
                if (1 + flip if signed else xrel // 2 * 3) != group:
                    continue
                core = (c + flip) % NC
                sign = 2 * core - 1
                for i, (zrel, zsigned, other) in enumerate(plan):
                    zs = (zh + (sign * zrel if zsigned else zrel) + NZH) % NZH
                    place = pl.multiple_of((zs * NC + (core + other) % NC) * fs, 32)
                    for kv in range(2):
                        cp = pltpu.make_async_copy(
                            ref.at[pl.ds((2 * i + kv) * fs, fs), :],
                            w_buf.at[at[group], pl.ds(place, fs), pl.ds(kv * 384, 384)],
                            w_sem.at[count],
                        )
                        cp.start()
                        waits[group].append(cp)
                        count += 1
            if group == 0:
                for i, (ref, (r0, c0)) in enumerate(zip(tok_refs, tok_at)):
                    for k in range(ref.shape[1] // quarter):
                        cp = pltpu.make_async_copy(
                            ref.at[:, pl.ds(k * quarter, quarter)],
                            t_buf.at[c0 // quarter + k, pl.ds(r0, ref.shape[0]), :],
                            t_sem.at[i, k],
                        )
                        cp.start()
                        waits[0].append(cp)
        backs = []
        for q in range(NX):
            for cp in waits[q]:
                cp.wait()
            back = pltpu.make_async_copy(w_buf.at[at[q]], w_out.at[at[q]], o_sem.at[q])
            back.start()
            backs.append(back)
            part = jnp.dot(t_buf[at[q]], w_buf[at[q]], preferred_element_type=F32)
            if q == 0:
                acc[...] = part
            elif q < NX - 1:
                acc[...] += part
            else:
                out[...] = (acc[...] + part).astype(BF16)
        for back in backs:
            back.wait()

    n_copies = 2 * sum(len(p[4]) for p in pieces)
    return pl.pallas_call(
        body,
        out_shape=[
            jax.ShapeDtypeStruct((rows, 768), BF16),
            jax.ShapeDtypeStruct((NX, quarter, 768), BF16),
        ],
        in_specs=[SM] + [HBM] * (nt + np_),
        out_specs=[VM, ANY],
        scratch_shapes=[
            pltpu.VMEM((NX, rows, quarter), BF16),
            pltpu.VMEM((NX, quarter, 768), BF16),
            pltpu.VMEM((rows, 768), F32),
            pltpu.SemaphoreType.DMA((nt, NX)),
            pltpu.SemaphoreType.DMA((n_copies,)),
            pltpu.SemaphoreType.DMA((NX,)),
        ],
        compiler_params=pltpu.CompilerParams(vmem_limit_bytes=36 * MIB),
    )(pos, *toks, *[p[0] for p in pieces])


CHUNKS = 4


def _half_product(toks, w, row0, cols, t_buf, w_buf, t_sem, w_sem):
    n = toks[0].shape[0]
    step = toks[0].shape[1] // CHUNKS

    def copies(k):
        at = k * step if isinstance(k, int) else pl.multiple_of(k * step, 128)
        yield pltpu.make_async_copy(
            w.at[pl.ds(row0 + at, step), pl.ds(*cols)], w_buf.at[k], w_sem.at[k]
        )
        for i, ref in enumerate(toks):
            yield pltpu.make_async_copy(
                ref.at[:, pl.ds(at, step)], t_buf.at[k, pl.ds(i * n, n), :], t_sem.at[k, i]
            )

    for k in range(CHUNKS):
        for cp in copies(k):
            cp.start()

    def product(acc):
        def one(k, carry):
            for cp in copies(k):
                cp.wait()
            acc[...] += jnp.dot(t_buf[k], w_buf[k], preferred_element_type=F32)
            return carry

        lax.fori_loop(0, CHUNKS, one, 0)

    return product


def _half_scratch(rows, half, width, ntok):
    return [
        pltpu.VMEM((CHUNKS, rows, half // CHUNKS), BF16),
        pltpu.VMEM((CHUNKS, half // CHUNKS, width), BF16),
        pltpu.SemaphoreType.DMA((CHUNKS, ntok)),
        pltpu.SemaphoreType.DMA((CHUNKS,)),
    ]


def project_half(toks, w):
    rows = sum(t.shape[0] for t in toks)
    half = toks[0].shape[1]

    def body(t0, t1, t2, w_ref, acc, t_buf, w_buf, t_sem, w_sem):
        product = _half_product((t0, t1, t2), w_ref, 0, (0, 768), t_buf, w_buf, t_sem, w_sem)
        acc[...] = jnp.zeros_like(acc)
        product(acc)

    return pl.pallas_call(
        body,
        out_shape=jax.ShapeDtypeStruct((rows, 768), F32),
        in_specs=[ANY] * 4,
        out_specs=VM,
        scratch_shapes=_half_scratch(rows, half, 768, 3),
        compiler_params=pltpu.CompilerParams(vmem_limit_bytes=48 * MIB),
    )(*toks, w)


def project_rest(toks, w, acc_in):
    rows = sum(t.shape[0] for t in toks)
    half = toks[0].shape[1]

    def body(t0, t1, w_ref, acc_ref, out, t_buf, w_buf, t_sem, w_sem, acc, a_sem):
        begin = pltpu.make_async_copy(acc_ref.at[pl.ds(0, rows), :], acc, a_sem)
        begin.start()
        product = _half_product((t0, t1), w_ref, half, (0, 768), t_buf, w_buf, t_sem, w_sem)
        begin.wait()
        product(acc)
        out[...] = acc[...].astype(BF16)

    return pl.pallas_call(
        body,
        out_shape=jax.ShapeDtypeStruct((rows, 768), BF16),
        in_specs=[ANY] * 4,
        out_specs=VM,
        scratch_shapes=_half_scratch(rows, half, 768, 2)
        + [pltpu.VMEM((rows, 768), F32), pltpu.SemaphoreType.DMA],
        compiler_params=pltpu.CompilerParams(vmem_limit_bytes=48 * MIB),
    )(*toks, w, acc_in)


def _tile_at(slot_ref, block, p):
    tile = block * TPD
    for i in range(1, TPD):
        tile = jnp.where(slot_ref[0, block * TPD + i] == block * TPD + p, block * TPD + i, tile)
    return tile


def _aligned(start):
    return jnp.minimum(start // 16 * 16, TILE - WIN)


def project_last(side, pos, tok, w, acc_in, done, done_places, place, tables):
    n, half = tok.shape
    row0 = acc_in.shape[0] - n

    def body(pos_ref, t0, w_ref, acc_ref, done_a, done_b, slot, neighbour, first,
             full, near, far, t_buf, w_buf, t_sem, w_sem, acc, wide, a_sem):
        block, zl, y, blocks = pos_ref[3], pos_ref[4], pos_ref[5], pos_ref[6]
        cols = (side * 384, 384)
        begin = pltpu.make_async_copy(acc_ref.at[pl.ds(row0, n), pl.ds(*cols)], acc, a_sem)
        begin.start()
        product = _half_product((t0,), w_ref, half, cols, t_buf, w_buf, t_sem, w_sem)

        def row_of(place):
            dzl, dy = place
            return pl.multiple_of(((zl + dzl) % NZL * NY + (y + dy + NY) % NY) * n, n)

        for ref, at in zip((done_a, done_b), done_places):
            for i, where in enumerate(at):
                part = ref[i * n : (i + 1) * n, side * 384 : side * 384 + 384]
                full[pl.ds(row_of(where), n), :] = part
                wide[pl.ds(row_of(where), n), :] = part.astype(F32)
        begin.wait()
        product(acc)
        part = acc[...].astype(BF16)
        full[pl.ds(row_of(place), n), :] = part
        wide[pl.ds(row_of(place), n), :] = part.astype(F32)
        up = 1 - 2 * pos_ref[2]
        for out, step in ((far, -up), (near, up)):
            target = (block + step + blocks) % blocks

            def pick(p, carry, out=out, target=target):
                tile = _tile_at(slot, target, p)
                seen = jnp.int32(0)
                starts = [jnp.int32(0), jnp.int32(0)]
                for j in range(NB):
                    other = neighbour[j, tile]
                    hit = other // TPD == block
                    row = slot[0, other] % TPD * TILE + first[j, tile]
                    for o in range(2):
                        take = jnp.logical_and(hit, seen == o)
                        starts[o] = jnp.where(take, row, starts[o])
                    seen = seen + hit.astype(jnp.int32)
                for o in range(2):
                    al = pl.multiple_of(starts[o] // 8 * 8, 8)
                    rem = starts[o] - al
                    window = pltpu.roll(
                        wide[pl.ds(al, SLAB + 8), :], (SLAB + 8 - rem) % (SLAB + 8), 0
                    )
                    at = pl.multiple_of((p * 2 + o) * SLAB, SLAB)
                    out[pl.ds(at, SLAB), :] = window[:SLAB].astype(BF16)
                return carry

            lax.fori_loop(0, TPD, pick, 0)

    return pl.pallas_call(
        body,
        out_shape=[jax.ShapeDtypeStruct((TPD * TILE, 384), BF16)]
        + [jax.ShapeDtypeStruct((HALO, 384), BF16)] * 2,
        in_specs=[SM] + [ANY] * 3 + [VM] * 2 + [SM] * 3,
        out_specs=[VM] * 3,
        scratch_shapes=_half_scratch(n, half, 384, 1)
        + [pltpu.VMEM((n, 384), F32), pltpu.VMEM((TPD * TILE + 8, 384), F32)]
        + [pltpu.SemaphoreType.DMA],
        compiler_params=pltpu.CompilerParams(vmem_limit_bytes=48 * MIB),
    )(pos, tok, w, acc_in, *done, *tables)


CAND = 768


def _clear_rest(cand):
    cand[pl.ds(TILE + NB * WIN, CAND - TILE - NB * WIN), :] = jnp.zeros(
        (CAND - TILE - NB * WIN, 384), BF16
    )
    for j in range(NB):
        cand[pl.ds(TILE + j * WIN + SLAB, WIN - SLAB), :] = jnp.zeros((WIN - SLAB, 384), BF16)


def _collect(p, pos_ref, slot, neighbour, first, full_ref, near_ref, far_ref, cand):
    block, blocks = pos_ref[3], pos_ref[6]
    tile = _tile_at(slot, block, p)
    own = pl.multiple_of(p * TILE, TILE)
    cand[pl.ds(0, TILE), :] = full_ref[pl.ds(own, TILE), :]
    up = 1 - 2 * pos_ref[2]
    near_block = (block + up + blocks) % blocks
    far_block = (block - up + blocks) % blocks
    seen_near = jnp.int32(0)
    seen_far = jnp.int32(0)
    places = []
    for j in range(NB):
        other = neighbour[j, tile]
        at = other // TPD
        is_near = at == near_block
        is_far = at == far_block
        s = first[j, tile]
        al = _aligned(s)
        c0 = TILE + j * WIN
        begin = slot[0, other] % TPD * TILE + al
        away = jnp.logical_or(is_near, is_far)

        @pl.when(is_near)
        def _(c0=c0, seen=seen_near):
            row = pl.multiple_of((p * 2 + seen) * SLAB, SLAB)
            cand[pl.ds(c0, SLAB), :] = near_ref[pl.ds(row, SLAB), :]

        @pl.when(is_far)
        def _(c0=c0, seen=seen_far):
            row = pl.multiple_of((p * 2 + seen) * SLAB, SLAB)
            cand[pl.ds(c0, SLAB), :] = far_ref[pl.ds(row, SLAB), :]

        @pl.when(jnp.logical_not(away))
        def _(c0=c0, begin=begin):
            cand[pl.ds(c0, WIN), :] = full_ref[pl.ds(pl.multiple_of(begin, 16), WIN), :]

        places.append(c0 + jnp.where(away, 0, s - al))
        seen_near = seen_near + is_near.astype(jnp.int32)
        seen_far = seen_far + is_far.astype(jnp.int32)
    return tile, places


def weigh(pos, queries, full, near_k, far_k, tables):
    scale = 1.0 / math.sqrt(HD)

    def body(pos_ref, q_ref, full_ref, near_ref, far_ref, slot, neighbour, first, length,
             low, high, prob, total, cand):
        p = pl.program_id(0)

        @pl.when(p == 0)
        def _():
            _clear_rest(cand)

        tile, places = _collect(
            p, pos_ref, slot, neighbour, first, full_ref, near_ref, far_ref, cand
        )
        col = lax.broadcasted_iota(jnp.int32, (8, CAND), 1)
        lows = jnp.where(col < TILE, 0, TILE)
        highs = jnp.where(col < TILE, TILE, 0)
        for j in range(NB):
            valid = jnp.logical_and(col >= places[j], col < places[j] + length[j, tile])
            lows = jnp.where(valid, low[j, tile], lows)
            highs = jnp.where(valid, high[j, tile], highs)
        row = lax.broadcasted_iota(jnp.int32, (TILE, CAND - TILE), 0)
        allowed = jnp.logical_and(row >= lows[0:1, TILE:], row < highs[0:1, TILE:])
        for h in range(3):
            cols = slice(h * HD, h * HD + HD)
            scores = lax.dot_general(
                q_ref[:, cols],
                cand[:, cols],
                (((1,), (1,)), ((), ())),
                preferred_element_type=F32,
            ) * scale
            own = scores[:, :TILE]
            slabs = jnp.where(allowed, scores[:, TILE:], -jnp.inf)
            top = jnp.maximum(
                jnp.max(own, axis=-1, keepdims=True), jnp.max(slabs, axis=-1, keepdims=True)
            )
            own = jnp.exp(own - top)
            slabs = jnp.exp(slabs - top)
            total[:, cols] = jnp.broadcast_to(
                jnp.sum(own, axis=-1, keepdims=True) + jnp.sum(slabs, axis=-1, keepdims=True),
                (TILE, HD),
            )
            prob[0, h, :, :TILE] = own.astype(BF16)
            prob[0, h, :, TILE:] = slabs.astype(BF16)

    return pl.pallas_call(
        body,
        grid=(TPD,),
        out_shape=[
            jax.ShapeDtypeStruct((TPD, 3, TILE, CAND), BF16),
            jax.ShapeDtypeStruct((TPD * TILE, 384), F32),
        ],
        in_specs=[SM, pl.BlockSpec((TILE, 384), lambda p: (p, 0)), VM, VM, VM] + [SM] * 6,
        out_specs=[
            pl.BlockSpec((1, 3, TILE, CAND), lambda p: (p, 0, 0, 0)),
            pl.BlockSpec((TILE, 384), lambda p: (p, 0)),
        ],
        scratch_shapes=[pltpu.VMEM((CAND, 384), BF16)],
        compiler_params=pltpu.CompilerParams(vmem_limit_bytes=24 * MIB),
    )(pos, queries, full, near_k, far_k, *tables)


def mix(pos, prob, total, full, near_v, far_v, tables):
    def body(pos_ref, prob_ref, total_ref, full_ref, near_ref, far_ref, slot, neighbour, first,
             out, cand):
        p = pl.program_id(0)

        @pl.when(p == 0)
        def _():
            _clear_rest(cand)

        _collect(p, pos_ref, slot, neighbour, first, full_ref, near_ref, far_ref, cand)
        for h in range(3):
            cols = slice(h * HD, h * HD + HD)
            mixed = jnp.dot(prob_ref[0, h], cand[:, cols], preferred_element_type=F32)
            out[:, cols] = (mixed / total_ref[:, cols]).astype(BF16)

    return pl.pallas_call(
        body,
        grid=(TPD,),
        out_shape=jax.ShapeDtypeStruct((TPD * TILE, 384), BF16),
        in_specs=[
            SM,
            pl.BlockSpec((1, 3, TILE, CAND), lambda p: (p, 0, 0, 0)),
            pl.BlockSpec((TILE, 384), lambda p: (p, 0)),
            VM,
            VM,
            VM,
        ]
        + [SM] * 3,
        out_specs=pl.BlockSpec((TILE, 384), lambda p: (p, 0)),
        scratch_shapes=[pltpu.VMEM((CAND, 384), BF16)],
        compiler_params=pltpu.CompilerParams(vmem_limit_bytes=24 * MIB),
    )(pos, prob, total, full, near_v, far_v, *tables)


def per_device(
    tokens,
    queries,
    w_key,
    w_value,
    tile_slot,
    neighbour_tile,
    slab_start,
    slab_length,
    window_low,
    window_high,
):
    fs = w_key.shape[0]
    ctx = lax.axis_index("ctx")
    tp = lax.axis_index("tp")
    pos = jnp.stack(
        [ctx >> 3, (ctx >> 1) & 3, ctx & 1, ctx, tp >> 2, tp & 3, jnp.int32(lax.axis_size("ctx"))]
    ).astype(jnp.int32)
    tables = (
        tile_slot.reshape(1, -1),
        neighbour_tile.T,
        slab_start.T,
        slab_length.T,
        window_low.T,
        window_high.T,
    )

    h = tokens.shape[1] // 2
    w = join(w_key, w_value, space=HBM)
    wc = send(w, dc=1)
    ya = send(tokens, dy=1)
    z1w = send(w, sz=1)
    yb = send(tokens, dy=-1)
    z1c = send(wc, sz=1)
    xw1 = send(w, sx=1)
    xc1 = send(wc, sx=1)
    z2 = send(z1w, sz=1)
    xw1, pos = lax.optimization_barrier((xw1, pos))
    xw2 = send(xw1, sx=1)
    tl, tr = tokens[:, :h], tokens[:, h:]
    z_l = send(tl, dzl=1)
    near = join(z1w, z1c, z2)
    xn1 = send(near, sx=1)
    far = send(near, dc=1)
    z_r = send(tr, dzl=1)
    xf1 = send(far, sx=1)
    yo_l = send(ya[:, :h], dy=1)
    yo_r = send(yb[:, h:], dy=-1)
    xn2 = send(xn1, sx=1)
    ua_l = send(z_l, dy=1)
    ub_l = send(z_l, dy=-1)
    uo_l = send(yo_l, dzl=1)
    uo_r = send(yo_r, dzl=1)
    ua_r = send(z_r, dy=1)
    ub_r = send(z_r, dy=-1)
    pieces = [
        (w, 0, False, 0, SAME),
        (wc, 0, False, 0, OTHER),
        (near, 0, False, 0, NEAR),
        (far, 0, False, 0, FAR),
    ]
    for p, xrel, signed, plan in (
        (xw1, 1, True, SAME),
        (xc1, 1, True, OTHER),
        (xw2, 2, False, SAME),
        (xn1, 1, True, NEAR),
        (xf1, 1, True, FAR),
        (xn2, 2, False, NEAR),
    ):
        pieces += [(p, xrel, signed, 0, plan), (send(p, dc=1), xrel, signed, 1, plan)]

    n = tokens.shape[0]
    toks = (tokens, ya, yb, yo_l, yo_r, z_l, z_r)
    at = ((0, 0), (n, 0), (2 * n, 0), (3 * n, 0), (3 * n, h), (4 * n, 0), (4 * n, h))
    kv1, w_all = project(pos, toks, at, 5 * n, pieces, fs)
    w_all = w_all.reshape(tokens.shape[1], 768)
    part = project_half((ua_l, ub_l, uo_l), w_all)
    kv2 = project_rest((ua_r, ub_r), w_all, part)
    last = (
        (kv1, kv2),
        (((0, 0), (0, -1), (0, 1), (0, 2), (1, 0)), ((1, -1), (1, 1))),
        (1, 2),
        tables[:3],
    )
    keys, near_k, far_k = project_last(0, pos, uo_r, w_all, part, *last)
    part = lax.optimization_barrier((part, far_k))[0]
    far_k = send(far_k, far=1)
    near_k = send(near_k, dc=1)
    values, near_v, far_v = project_last(1, pos, uo_r, w_all, part, *last)
    far_v = send(far_v, far=1)
    near_v = send(near_v, dc=1)
    prob, total = weigh(pos, queries, keys, near_k, far_k, tables)
    return mix(pos, prob, total, values, near_v, far_v, tables[:3])


def solution(mesh):
    in_specs = (
        P(("ctx", "tp"), None),
        P("ctx", "tp"),
        P("ctx", "tp"),
        P("ctx", "tp"),
        P(),
        P(),
        P(),
        P(),
        P(),
        P(),
    )
    out_specs = P("ctx", "tp")
    return jax.shard_map(
        per_device, mesh=mesh, in_specs=in_specs, out_specs=out_specs, check_vma=False
    )
```

```python
import math

import jax
import jax.numpy as jnp
from jax import lax
from jax.experimental import pallas as pl
from jax.experimental.pallas import tpu as pltpu
from jax.sharding import PartitionSpec as P


HD = 128
TILE = 256
NB = 6
SLAB = 64
TPD = 4
HALO = TPD * 2 * SLAB
WIN = 80
NX, NZH, NC, NZL, NY = 4, 4, 2, 2, 4
AXES = ("ctx", "tp")
BF16 = jnp.bfloat16
F32 = jnp.float32


def _index(x, zh, c, zl, y):
    return (((x % NX) * NZH + zh % NZH) * NC + c % NC) * (NZL * NY) + zl % NZL * NY + y % NY


def _moves(dx=0, dzh=0, dc=0, dzl=0, dy=0, sx=0, sz=0):
    pairs = []
    for x in range(NX):
        for zh in range(NZH):
            for c in range(NC):
                for zl in range(NZL):
                    for y in range(NY):
                        pairs.append(
                            (
                                _index(x, zh, c, zl, y),
                                _index(
                                    x + dx + sx * (1 - 2 * c),
                                    zh + dzh + sz * (1 - 2 * c),
                                    c + dc,
                                    zl + dzl,
                                    y + dy,
                                ),
                            )
                        )
    return pairs


def _far_moves():
    blocks = NX * NZH * NC
    tps = NZL * NY
    return [
        (b * tps + t, (b - 1 + 2 * (b % 2)) % blocks * tps + t)
        for b in range(blocks)
        for t in range(tps)
    ]


def send(a, **step):
    return lax.ppermute(a, AXES, _far_moves() if "far" in step else _moves(**step))


SAME = ((0, False, 0),)
OTHER = ((0, False, 1),)
NEAR = ((1, True, 0), (1, True, 1), (2, False, 0))
FAR = ((-1, True, 1), (-1, True, 0), (2, False, 1))


ANY = pl.BlockSpec(memory_space=pl.ANY)
HBM = pl.BlockSpec(memory_space=pltpu.HBM)
SM = pl.BlockSpec(memory_space=pltpu.SMEM)
VM = pl.BlockSpec(memory_space=pltpu.VMEM)
MIB = 1024 * 1024


def join(*parts, space=None):
    rows = [p.shape[0] for p in parts]

    def body(*refs):
        out, sems = refs[-2:]
        copies = []
        for i, ref in enumerate(refs[:-2]):
            copies.append(
                pltpu.make_async_copy(ref, out.at[pl.ds(sum(rows[:i]), rows[i]), :], sems.at[i])
            )
        for cp in copies:
            cp.start()
        for cp in copies:
            cp.wait()

    return pl.pallas_call(
        body,
        out_shape=jax.ShapeDtypeStruct((sum(rows), parts[0].shape[1]), parts[0].dtype),
        in_specs=[space or ANY] * len(parts),
        out_specs=ANY,
        scratch_shapes=[pltpu.SemaphoreType.DMA((len(parts),))],
        compiler_params=pltpu.CompilerParams(vmem_limit_bytes=MIB),
    )(*parts)


def project(pos, toks, tok_at, rows, pieces, fs):
    nt, np_ = len(toks), len(pieces)
    features = fs * NX * NZH * NC
    quarter = features // NX

    def body(*refs):
        pos_ref = refs[0]
        tok_refs = refs[1 : 1 + nt]
        piece_refs = refs[1 + nt : 1 + nt + np_]
        out, w_out, t_buf, w_buf, acc, t_sem, w_sem, o_sem = refs[1 + nt + np_ :]
        x, zh, c = pos_ref[0], pos_ref[1], pos_ref[2]
        steps = (0, 2 * c - 1, 1 - 2 * c, 2)
        at = [(x + step + NX) % NX for step in steps]
        waits = [[] for _ in steps]
        count = 0
        for group in range(NX):
            for ref, (_, xrel, signed, flip, plan) in zip(piece_refs, pieces):
                if (1 + flip if signed else xrel // 2 * 3) != group:
                    continue
                core = (c + flip) % NC
                sign = 2 * core - 1
                for i, (zrel, zsigned, other) in enumerate(plan):
                    zs = (zh + (sign * zrel if zsigned else zrel) + NZH) % NZH
                    place = pl.multiple_of((zs * NC + (core + other) % NC) * fs, 32)
                    for kv in range(2):
                        cp = pltpu.make_async_copy(
                            ref.at[pl.ds((2 * i + kv) * fs, fs), :],
                            w_buf.at[at[group], pl.ds(place, fs), pl.ds(kv * 384, 384)],
                            w_sem.at[count],
                        )
                        cp.start()
                        waits[group].append(cp)
                        count += 1
            if group == 0:
                for i, (ref, (r0, c0)) in enumerate(zip(tok_refs, tok_at)):
                    for k in range(ref.shape[1] // quarter):
                        cp = pltpu.make_async_copy(
                            ref.at[:, pl.ds(k * quarter, quarter)],
                            t_buf.at[c0 // quarter + k, pl.ds(r0, ref.shape[0]), :],
                            t_sem.at[i, k],
                        )
                        cp.start()
                        waits[0].append(cp)
        backs = []
        for q in range(NX):
            for cp in waits[q]:
                cp.wait()
            back = pltpu.make_async_copy(w_buf.at[at[q]], w_out.at[at[q]], o_sem.at[q])
            back.start()
            backs.append(back)
            part = jnp.dot(t_buf[at[q]], w_buf[at[q]], preferred_element_type=F32)
            if q == 0:
                acc[...] = part
            elif q < NX - 1:
                acc[...] += part
            else:
                out[...] = (acc[...] + part).astype(BF16)
        for back in backs:
            back.wait()

    n_copies = 2 * sum(len(p[4]) for p in pieces)
    return pl.pallas_call(
        body,
        out_shape=[
            jax.ShapeDtypeStruct((rows, 768), BF16),
            jax.ShapeDtypeStruct((NX, quarter, 768), BF16),
        ],
        in_specs=[SM] + [HBM] * (nt + np_),
        out_specs=[VM, ANY],
        scratch_shapes=[
            pltpu.VMEM((NX, rows, quarter), BF16),
            pltpu.VMEM((NX, quarter, 768), BF16),
            pltpu.VMEM((rows, 768), F32),
            pltpu.SemaphoreType.DMA((nt, NX)),
            pltpu.SemaphoreType.DMA((n_copies,)),
            pltpu.SemaphoreType.DMA((NX,)),
        ],
        compiler_params=pltpu.CompilerParams(vmem_limit_bytes=36 * MIB),
    )(pos, *toks, *[p[0] for p in pieces])


CHUNKS = 4


def _half_product(toks, w, row0, cols, t_buf, w_buf, t_sem, w_sem):
    n = toks[0].shape[0]
    step = toks[0].shape[1] // CHUNKS

    def copies(k):
        at = k * step if isinstance(k, int) else pl.multiple_of(k * step, 128)
        yield pltpu.make_async_copy(
            w.at[pl.ds(row0 + at, step), pl.ds(*cols)], w_buf.at[k], w_sem.at[k]
        )
        for i, ref in enumerate(toks):
            yield pltpu.make_async_copy(
                ref.at[:, pl.ds(at, step)], t_buf.at[k, pl.ds(i * n, n), :], t_sem.at[k, i]
            )

    for k in range(CHUNKS):
        for cp in copies(k):
            cp.start()

    def product(acc):
        def one(k, carry):
            for cp in copies(k):
                cp.wait()
            acc[...] += jnp.dot(t_buf[k], w_buf[k], preferred_element_type=F32)
            return carry

        lax.fori_loop(0, CHUNKS, one, 0)

    return product


def _half_scratch(rows, half, width, ntok):
    return [
        pltpu.VMEM((CHUNKS, rows, half // CHUNKS), BF16),
        pltpu.VMEM((CHUNKS, half // CHUNKS, width), BF16),
        pltpu.SemaphoreType.DMA((CHUNKS, ntok)),
        pltpu.SemaphoreType.DMA((CHUNKS,)),
    ]


def project_half(toks, w):
    rows = sum(t.shape[0] for t in toks)
    half = toks[0].shape[1]

    def body(t0, t1, t2, w_ref, acc, t_buf, w_buf, t_sem, w_sem):
        product = _half_product((t0, t1, t2), w_ref, 0, (0, 768), t_buf, w_buf, t_sem, w_sem)
        acc[...] = jnp.zeros_like(acc)
        product(acc)

    return pl.pallas_call(
        body,
        out_shape=jax.ShapeDtypeStruct((rows, 768), F32),
        in_specs=[ANY] * 4,
        out_specs=VM,
        scratch_shapes=_half_scratch(rows, half, 768, 3),
        compiler_params=pltpu.CompilerParams(vmem_limit_bytes=48 * MIB),
    )(*toks, w)


def _tile_at(slot_ref, block, p):
    tile = block * TPD
    for i in range(1, TPD):
        tile = jnp.where(slot_ref[0, block * TPD + i] == block * TPD + p, block * TPD + i, tile)
    return tile


def _aligned(start):
    return jnp.minimum(start // 16 * 16, TILE - WIN)


def project_last(side, pos, toks, w, acc_in, done, done_places, places, tables):
    n, half = toks[0].shape
    rows = n * len(toks)

    def body(pos_ref, t0, t1, t2, w_ref, acc_ref, done_ref, slot, neighbour, first,
             full, near, far, t_buf, w_buf, t_sem, w_sem, acc, wide, a_sem):
        block, zl, y, blocks = pos_ref[3], pos_ref[4], pos_ref[5], pos_ref[6]
        cols = (side * 384, 384)
        begin = pltpu.make_async_copy(acc_ref.at[:, pl.ds(*cols)], acc, a_sem)
        begin.start()
        product = _half_product((t0, t1, t2), w_ref, half, cols, t_buf, w_buf, t_sem, w_sem)

        def row_of(place):
            dzl, dy = place
            return pl.multiple_of(((zl + dzl) % NZL * NY + (y + dy + NY) % NY) * n, n)

        for i, place in enumerate(done_places):
            part = done_ref[i * n : (i + 1) * n, side * 384 : side * 384 + 384]
            full[pl.ds(row_of(place), n), :] = part
            wide[pl.ds(row_of(place), n), :] = part.astype(F32)
        begin.wait()
        product(acc)
        for i, place in enumerate(places):
            part = acc[i * n : (i + 1) * n, :].astype(BF16)
            full[pl.ds(row_of(place), n), :] = part
            wide[pl.ds(row_of(place), n), :] = part.astype(F32)
        up = 1 - 2 * pos_ref[2]
        for out, step in ((far, -up), (near, up)):
            target = (block + step + blocks) % blocks

            def pick(p, carry, out=out, target=target):
                tile = _tile_at(slot, target, p)
                seen = jnp.int32(0)
                starts = [jnp.int32(0), jnp.int32(0)]
                for j in range(NB):
                    other = neighbour[j, tile]
                    hit = other // TPD == block
                    row = slot[0, other] % TPD * TILE + first[j, tile]
                    for o in range(2):
                        take = jnp.logical_and(hit, seen == o)
                        starts[o] = jnp.where(take, row, starts[o])
                    seen = seen + hit.astype(jnp.int32)
                for o in range(2):
                    al = pl.multiple_of(starts[o] // 8 * 8, 8)
                    rem = starts[o] - al
                    window = pltpu.roll(
                        wide[pl.ds(al, SLAB + 8), :], (SLAB + 8 - rem) % (SLAB + 8), 0
                    )
                    at = pl.multiple_of((p * 2 + o) * SLAB, SLAB)
                    out[pl.ds(at, SLAB), :] = window[:SLAB].astype(BF16)
                return carry

            lax.fori_loop(0, TPD, pick, 0)

    return pl.pallas_call(
        body,
        out_shape=[jax.ShapeDtypeStruct((TPD * TILE, 384), BF16)]
        + [jax.ShapeDtypeStruct((HALO, 384), BF16)] * 2,
        in_specs=[SM] + [ANY] * 5 + [VM] + [SM] * 3,
        out_specs=[VM] * 3,
        scratch_shapes=_half_scratch(rows, half, 384, 3)
        + [pltpu.VMEM((rows, 384), F32), pltpu.VMEM((TPD * TILE + 8, 384), F32)]
        + [pltpu.SemaphoreType.DMA],
        compiler_params=pltpu.CompilerParams(vmem_limit_bytes=48 * MIB),
    )(pos, *toks, w, acc_in, done, *tables)


CAND = 768


def _clear_rest(cand):
    cand[pl.ds(TILE + NB * WIN, CAND - TILE - NB * WIN), :] = jnp.zeros(
        (CAND - TILE - NB * WIN, 384), BF16
    )
    for j in range(NB):
        cand[pl.ds(TILE + j * WIN + SLAB, WIN - SLAB), :] = jnp.zeros((WIN - SLAB, 384), BF16)


def _collect(p, pos_ref, slot, neighbour, first, full_ref, near_ref, far_ref, cand):
    block, blocks = pos_ref[3], pos_ref[6]
    tile = _tile_at(slot, block, p)
    own = pl.multiple_of(p * TILE, TILE)
    cand[pl.ds(0, TILE), :] = full_ref[pl.ds(own, TILE), :]
    up = 1 - 2 * pos_ref[2]
    near_block = (block + up + blocks) % blocks
    far_block = (block - up + blocks) % blocks
    seen_near = jnp.int32(0)
    seen_far = jnp.int32(0)
    places = []
    for j in range(NB):
        other = neighbour[j, tile]
        at = other // TPD
        is_near = at == near_block
        is_far = at == far_block
        s = first[j, tile]
        al = _aligned(s)
        c0 = TILE + j * WIN
        begin = slot[0, other] % TPD * TILE + al
        away = jnp.logical_or(is_near, is_far)

        @pl.when(is_near)
        def _(c0=c0, seen=seen_near):
            row = pl.multiple_of((p * 2 + seen) * SLAB, SLAB)
            cand[pl.ds(c0, SLAB), :] = near_ref[pl.ds(row, SLAB), :]

        @pl.when(is_far)
        def _(c0=c0, seen=seen_far):
            row = pl.multiple_of((p * 2 + seen) * SLAB, SLAB)
            cand[pl.ds(c0, SLAB), :] = far_ref[pl.ds(row, SLAB), :]

        @pl.when(jnp.logical_not(away))
        def _(c0=c0, begin=begin):
            cand[pl.ds(c0, WIN), :] = full_ref[pl.ds(pl.multiple_of(begin, 16), WIN), :]

        places.append(c0 + jnp.where(away, 0, s - al))
        seen_near = seen_near + is_near.astype(jnp.int32)
        seen_far = seen_far + is_far.astype(jnp.int32)
    return tile, places


def weigh(pos, queries, full, near_k, far_k, tables):
    scale = 1.0 / math.sqrt(HD)

    def body(pos_ref, q_ref, full_ref, near_ref, far_ref, slot, neighbour, first, length,
             low, high, prob, total, cand):
        p = pl.program_id(0)

        @pl.when(p == 0)
        def _():
            _clear_rest(cand)

        tile, places = _collect(
            p, pos_ref, slot, neighbour, first, full_ref, near_ref, far_ref, cand
        )
        col = lax.broadcasted_iota(jnp.int32, (8, CAND), 1)
        lows = jnp.where(col < TILE, 0, TILE)
        highs = jnp.where(col < TILE, TILE, 0)
        for j in range(NB):
            valid = jnp.logical_and(col >= places[j], col < places[j] + length[j, tile])
            lows = jnp.where(valid, low[j, tile], lows)
            highs = jnp.where(valid, high[j, tile], highs)
        row = lax.broadcasted_iota(jnp.int32, (TILE, CAND - TILE), 0)
        allowed = jnp.logical_and(row >= lows[0:1, TILE:], row < highs[0:1, TILE:])
        for h in range(3):
            cols = slice(h * HD, h * HD + HD)
            scores = lax.dot_general(
                q_ref[:, cols],
                cand[:, cols],
                (((1,), (1,)), ((), ())),
                preferred_element_type=F32,
            ) * scale
            own = scores[:, :TILE]
            slabs = jnp.where(allowed, scores[:, TILE:], -jnp.inf)
            top = jnp.maximum(
                jnp.max(own, axis=-1, keepdims=True), jnp.max(slabs, axis=-1, keepdims=True)
            )
            own = jnp.exp(own - top)
            slabs = jnp.exp(slabs - top)
            total[:, cols] = jnp.broadcast_to(
                jnp.sum(own, axis=-1, keepdims=True) + jnp.sum(slabs, axis=-1, keepdims=True),
                (TILE, HD),
            )
            prob[0, h, :, :TILE] = own.astype(BF16)
            prob[0, h, :, TILE:] = slabs.astype(BF16)

    return pl.pallas_call(
        body,
        grid=(TPD,),
        out_shape=[
            jax.ShapeDtypeStruct((TPD, 3, TILE, CAND), BF16),
            jax.ShapeDtypeStruct((TPD * TILE, 384), F32),
        ],
        in_specs=[SM, pl.BlockSpec((TILE, 384), lambda p: (p, 0)), VM, VM, VM] + [SM] * 6,
        out_specs=[
            pl.BlockSpec((1, 3, TILE, CAND), lambda p: (p, 0, 0, 0)),
            pl.BlockSpec((TILE, 384), lambda p: (p, 0)),
        ],
        scratch_shapes=[pltpu.VMEM((CAND, 384), BF16)],
        compiler_params=pltpu.CompilerParams(vmem_limit_bytes=24 * MIB),
    )(pos, queries, full, near_k, far_k, *tables)


def mix(pos, prob, total, full, near_v, far_v, tables):
    def body(pos_ref, prob_ref, total_ref, full_ref, near_ref, far_ref, slot, neighbour, first,
             out, cand):
        p = pl.program_id(0)

        @pl.when(p == 0)
        def _():
            _clear_rest(cand)

        _collect(p, pos_ref, slot, neighbour, first, full_ref, near_ref, far_ref, cand)
        for h in range(3):
            cols = slice(h * HD, h * HD + HD)
            mixed = jnp.dot(prob_ref[0, h], cand[:, cols], preferred_element_type=F32)
            out[:, cols] = (mixed / total_ref[:, cols]).astype(BF16)

    return pl.pallas_call(
        body,
        grid=(TPD,),
        out_shape=jax.ShapeDtypeStruct((TPD * TILE, 384), BF16),
        in_specs=[
            SM,
            pl.BlockSpec((1, 3, TILE, CAND), lambda p: (p, 0, 0, 0)),
            pl.BlockSpec((TILE, 384), lambda p: (p, 0)),
            VM,
            VM,
            VM,
        ]
        + [SM] * 3,
        out_specs=pl.BlockSpec((TILE, 384), lambda p: (p, 0)),
        scratch_shapes=[pltpu.VMEM((CAND, 384), BF16)],
        compiler_params=pltpu.CompilerParams(vmem_limit_bytes=24 * MIB),
    )(pos, prob, total, full, near_v, far_v, *tables)


def per_device(
    tokens,
    queries,
    w_key,
    w_value,
    tile_slot,
    neighbour_tile,
    slab_start,
    slab_length,
    window_low,
    window_high,
):
    fs = w_key.shape[0]
    ctx = lax.axis_index("ctx")
    tp = lax.axis_index("tp")
    pos = jnp.stack(
        [ctx >> 3, (ctx >> 1) & 3, ctx & 1, ctx, tp >> 2, tp & 3, jnp.int32(lax.axis_size("ctx"))]
    ).astype(jnp.int32)
    tables = (
        tile_slot.reshape(1, -1),
        neighbour_tile.T,
        slab_start.T,
        slab_length.T,
        window_low.T,
        window_high.T,
    )

    h = tokens.shape[1] // 2
    w = join(w_key, w_value, space=HBM)
    wc = send(w, dc=1)
    ya = send(tokens, dy=1)
    z1w = send(w, sz=1)
    yb = send(tokens, dy=-1)
    wc, tl, tr = lax.optimization_barrier((wc, tokens[:, :h], tokens[:, h:]))
    z1c = send(wc, sz=1)
    xw1 = send(w, sx=1)
    xc1 = send(wc, sx=1)
    z2 = send(z1w, sz=1)
    xw1, pos = lax.optimization_barrier((xw1, pos))
    xw2 = send(xw1, sx=1)
    z_l = send(tl, dzl=1)
    near = join(z1w, z1c, z2)
    xn1 = send(near, sx=1)
    far = send(near, dc=1)
    z_r = send(tr, dzl=1)
    xf1 = send(far, sx=1)
    yo_l = send(ya[:, :h], dy=1)
    yo_r = send(yb[:, h:], dy=-1)
    xn2 = send(xn1, sx=1)
    ua_l = send(z_l, dy=1)
    ub_l = send(z_l, dy=-1)
    uo_l = send(yo_l, dzl=1)
    uo_r = send(yo_r, dzl=1)
    ua_r = send(z_r, dy=1)
    ub_r = send(z_r, dy=-1)
    pieces = [
        (w, 0, False, 0, SAME),
        (wc, 0, False, 0, OTHER),
        (near, 0, False, 0, NEAR),
        (far, 0, False, 0, FAR),
    ]
    for p, xrel, signed, plan in (
        (xw1, 1, True, SAME),
        (xc1, 1, True, OTHER),
        (xw2, 2, False, SAME),
        (xn1, 1, True, NEAR),
        (xf1, 1, True, FAR),
        (xn2, 2, False, NEAR),
    ):
        pieces += [(p, xrel, signed, 0, plan), (send(p, dc=1), xrel, signed, 1, plan)]

    n = tokens.shape[0]
    toks = (tokens, ya, yb, yo_l, yo_r, z_l, z_r)
    at = ((0, 0), (n, 0), (2 * n, 0), (3 * n, 0), (3 * n, h), (4 * n, 0), (4 * n, h))
    kv1, w_all = project(pos, toks, at, 5 * n, pieces, fs)
    w_all = w_all.reshape(tokens.shape[1], 768)
    part = project_half((ua_l, ub_l, uo_l), w_all)
    rest = (ua_r, ub_r, uo_r)
    last = (
        kv1,
        ((0, 0), (0, -1), (0, 1), (0, 2), (1, 0)),
        ((1, -1), (1, 1), (1, 2)),
        tables[:3],
    )
    keys, near_k, far_k = project_last(0, pos, rest, w_all, part, *last)
    part = lax.optimization_barrier((part, far_k))[0]
    far_k = send(far_k, far=1)
    near_k = send(near_k, dc=1)
    values, near_v, far_v = project_last(1, pos, rest, w_all, part, *last)
    far_v = send(far_v, far=1)
    near_v = send(near_v, dc=1)
    prob, total = weigh(pos, queries, keys, near_k, far_k, tables)
    return mix(pos, prob, total, values, near_v, far_v, tables[:3])


def solution(mesh):
    in_specs = (
        P(("ctx", "tp"), None),
        P("ctx", "tp"),
        P("ctx", "tp"),
        P("ctx", "tp"),
        P(),
        P(),
        P(),
        P(),
        P(),
        P(),
    )
    out_specs = P("ctx", "tp")
    return jax.shard_map(
        per_device, mesh=mesh, in_specs=in_specs, out_specs=out_specs, check_vma=False
    )
```

```python
import math

import jax
import jax.numpy as jnp
from jax import lax
from jax.experimental import pallas as pl
from jax.experimental.pallas import tpu as pltpu
from jax.sharding import PartitionSpec as P


HD = 128
TILE = 256
NB = 6
SLAB = 64
TPD = 4
HALO = TPD * 2 * SLAB
WIN = 80
NX, NZH, NC, NZL, NY = 4, 4, 2, 2, 4
AXES = ("ctx", "tp")
BF16 = jnp.bfloat16
F32 = jnp.float32


def _index(x, zh, c, zl, y):
    return (((x % NX) * NZH + zh % NZH) * NC + c % NC) * (NZL * NY) + zl % NZL * NY + y % NY


def _moves(dx=0, dzh=0, dc=0, dzl=0, dy=0, sx=0, sz=0):
    pairs = []
    for x in range(NX):
        for zh in range(NZH):
            for c in range(NC):
                for zl in range(NZL):
                    for y in range(NY):
                        pairs.append(
                            (
                                _index(x, zh, c, zl, y),
                                _index(
                                    x + dx + sx * (1 - 2 * c),
                                    zh + dzh + sz * (1 - 2 * c),
                                    c + dc,
                                    zl + dzl,
                                    y + dy,
                                ),
                            )
                        )
    return pairs


def _far_moves():
    blocks = NX * NZH * NC
    tps = NZL * NY
    return [
        (b * tps + t, (b - 1 + 2 * (b % 2)) % blocks * tps + t)
        for b in range(blocks)
        for t in range(tps)
    ]


def send(a, **step):
    return lax.ppermute(a, AXES, _far_moves() if "far" in step else _moves(**step))


SAME = ((0, False, 0),)
OTHER = ((0, False, 1),)
NEAR = ((1, True, 0), (1, True, 1), (2, False, 0))
FAR = ((-1, True, 1), (-1, True, 0), (2, False, 1))


ANY = pl.BlockSpec(memory_space=pl.ANY)
HBM = pl.BlockSpec(memory_space=pltpu.HBM)
SM = pl.BlockSpec(memory_space=pltpu.SMEM)
VM = pl.BlockSpec(memory_space=pltpu.VMEM)
MIB = 1024 * 1024


def join(*parts, space=None):
    rows = [p.shape[0] for p in parts]

    def body(*refs):
        out, sems = refs[-2:]
        copies = []
        for i, ref in enumerate(refs[:-2]):
            copies.append(
                pltpu.make_async_copy(ref, out.at[pl.ds(sum(rows[:i]), rows[i]), :], sems.at[i])
            )
        for cp in copies:
            cp.start()
        for cp in copies:
            cp.wait()

    return pl.pallas_call(
        body,
        out_shape=jax.ShapeDtypeStruct((sum(rows), parts[0].shape[1]), parts[0].dtype),
        in_specs=[space or ANY] * len(parts),
        out_specs=ANY,
        scratch_shapes=[pltpu.SemaphoreType.DMA((len(parts),))],
        compiler_params=pltpu.CompilerParams(vmem_limit_bytes=MIB),
    )(*parts)


def project(pos, toks, tok_at, rows, pieces, fs):
    nt, np_ = len(toks), len(pieces)
    features = fs * NX * NZH * NC
    quarter = features // NX

    def body(*refs):
        pos_ref = refs[0]
        tok_refs = refs[1 : 1 + nt]
        piece_refs = refs[1 + nt : 1 + nt + np_]
        out, w_out, t_buf, w_buf, acc, t_sem, w_sem, o_sem = refs[1 + nt + np_ :]
        x, zh, c = pos_ref[0], pos_ref[1], pos_ref[2]
        steps = (0, 2 * c - 1, 1 - 2 * c, 2)
        at = [(x + step + NX) % NX for step in steps]
        waits = [[] for _ in steps]
        count = 0
        for group in range(NX):
            for ref, (_, xrel, signed, flip, plan) in zip(piece_refs, pieces):
                if (1 + flip if signed else xrel // 2 * 3) != group:
                    continue
                core = (c + flip) % NC
                sign = 2 * core - 1
                for i, (zrel, zsigned, other) in enumerate(plan):
                    zs = (zh + (sign * zrel if zsigned else zrel) + NZH) % NZH
                    place = pl.multiple_of((zs * NC + (core + other) % NC) * fs, 32)
                    for kv in range(2):
                        cp = pltpu.make_async_copy(
                            ref.at[pl.ds((2 * i + kv) * fs, fs), :],
                            w_buf.at[at[group], pl.ds(place, fs), pl.ds(kv * 384, 384)],
                            w_sem.at[count],
                        )
                        cp.start()
                        waits[group].append(cp)
                        count += 1
            if group == 0:
                for i, (ref, (r0, c0)) in enumerate(zip(tok_refs, tok_at)):
                    for k in range(ref.shape[1] // quarter):
                        cp = pltpu.make_async_copy(
                            ref.at[:, pl.ds(k * quarter, quarter)],
                            t_buf.at[c0 // quarter + k, pl.ds(r0, ref.shape[0]), :],
                            t_sem.at[i, k],
                        )
                        cp.start()
                        waits[0].append(cp)
        backs = []
        for q in range(NX):
            for cp in waits[q]:
                cp.wait()
            back = pltpu.make_async_copy(w_buf.at[at[q]], w_out.at[at[q]], o_sem.at[q])
            back.start()
            backs.append(back)
            part = jnp.dot(t_buf[at[q]], w_buf[at[q]], preferred_element_type=F32)
            if q == 0:
                acc[...] = part
            elif q < NX - 1:
                acc[...] += part
            else:
                out[...] = (acc[...] + part).astype(BF16)
        for back in backs:
            back.wait()

    n_copies = 2 * sum(len(p[4]) for p in pieces)
    return pl.pallas_call(
        body,
        out_shape=[
            jax.ShapeDtypeStruct((rows, 768), BF16),
            jax.ShapeDtypeStruct((NX, quarter, 768), BF16),
        ],
        in_specs=[SM] + [HBM] * (nt + np_),
        out_specs=[VM, ANY],
        scratch_shapes=[
            pltpu.VMEM((NX, rows, quarter), BF16),
            pltpu.VMEM((NX, quarter, 768), BF16),
            pltpu.VMEM((rows, 768), F32),
            pltpu.SemaphoreType.DMA((nt, NX)),
            pltpu.SemaphoreType.DMA((n_copies,)),
            pltpu.SemaphoreType.DMA((NX,)),
        ],
        compiler_params=pltpu.CompilerParams(vmem_limit_bytes=36 * MIB),
    )(pos, *toks, *[p[0] for p in pieces])


CHUNKS = 4


def _half_product(toks, w, row0, cols, t_buf, w_buf, t_sem, w_sem, unroll=False):
    n = toks[0].shape[0]
    step = toks[0].shape[1] // CHUNKS

    def copies(k):
        at = k * step if isinstance(k, int) else pl.multiple_of(k * step, 128)
        yield pltpu.make_async_copy(
            w.at[pl.ds(row0 + at, step), pl.ds(*cols)], w_buf.at[k], w_sem.at[k]
        )
        for i, ref in enumerate(toks):
            yield pltpu.make_async_copy(
                ref.at[:, pl.ds(at, step)], t_buf.at[k, pl.ds(i * n, n), :], t_sem.at[k, i]
            )

    for k in range(CHUNKS):
        for cp in copies(k):
            cp.start()

    def product(acc):
        def one(k, carry):
            for cp in copies(k):
                cp.wait()
            acc[...] += jnp.dot(t_buf[k], w_buf[k], preferred_element_type=F32)
            return carry

        if unroll:
            for k in range(CHUNKS):
                one(k, 0)
        else:
            lax.fori_loop(0, CHUNKS, one, 0)

    return product


def _half_scratch(rows, half, width, ntok):
    return [
        pltpu.VMEM((CHUNKS, rows, half // CHUNKS), BF16),
        pltpu.VMEM((CHUNKS, half // CHUNKS, width), BF16),
        pltpu.SemaphoreType.DMA((CHUNKS, ntok)),
        pltpu.SemaphoreType.DMA((CHUNKS,)),
    ]


def project_half(toks, w):
    rows = sum(t.shape[0] for t in toks)
    half = toks[0].shape[1]

    def body(t0, t1, t2, w_ref, acc, t_buf, w_buf, t_sem, w_sem):
        product = _half_product((t0, t1, t2), w_ref, 0, (0, 768), t_buf, w_buf, t_sem, w_sem)
        acc[...] = jnp.zeros_like(acc)
        product(acc)

    return pl.pallas_call(
        body,
        out_shape=jax.ShapeDtypeStruct((rows, 768), F32),
        in_specs=[ANY] * 4,
        out_specs=VM,
        scratch_shapes=_half_scratch(rows, half, 768, 3),
        compiler_params=pltpu.CompilerParams(vmem_limit_bytes=48 * MIB),
    )(*toks, w)


def _tile_at(slot_ref, block, p):
    tile = block * TPD
    for i in range(1, TPD):
        tile = jnp.where(slot_ref[0, block * TPD + i] == block * TPD + p, block * TPD + i, tile)
    return tile


def _aligned(start):
    return jnp.minimum(start // 16 * 16, TILE - WIN)


def project_last(side, pos, toks, w, acc_in, done, done_places, places, tables):
    n, half = toks[0].shape
    rows = n * len(toks)

    def body(pos_ref, t0, t1, t2, w_ref, acc_ref, done_ref, slot, neighbour, first,
             full, near, far, t_buf, w_buf, t_sem, w_sem, acc, wide, a_sem):
        block, zl, y, blocks = pos_ref[3], pos_ref[4], pos_ref[5], pos_ref[6]
        cols = (side * 384, 384)
        begin = pltpu.make_async_copy(acc_ref.at[:, pl.ds(*cols)], acc, a_sem)
        begin.start()
        product = _half_product(
            (t0, t1, t2), w_ref, half, cols, t_buf, w_buf, t_sem, w_sem, unroll=True
        )

        def row_of(place):
            dzl, dy = place
            return pl.multiple_of(((zl + dzl) % NZL * NY + (y + dy + NY) % NY) * n, n)

        for i, place in enumerate(done_places):
            part = done_ref[i * n : (i + 1) * n, side * 384 : side * 384 + 384]
            full[pl.ds(row_of(place), n), :] = part
            wide[pl.ds(row_of(place), n), :] = part.astype(F32)
        begin.wait()
        product(acc)
        for i, place in enumerate(places):
            part = acc[i * n : (i + 1) * n, :].astype(BF16)
            full[pl.ds(row_of(place), n), :] = part
            wide[pl.ds(row_of(place), n), :] = part.astype(F32)
        up = 1 - 2 * pos_ref[2]
        for out, step in ((far, -up), (near, up)):
            target = (block + step + blocks) % blocks

            def pick(p, carry, out=out, target=target):
                tile = _tile_at(slot, target, p)
                seen = jnp.int32(0)
                starts = [jnp.int32(0), jnp.int32(0)]
                for j in range(NB):
                    other = neighbour[j, tile]
                    hit = other // TPD == block
                    row = slot[0, other] % TPD * TILE + first[j, tile]
                    for o in range(2):
                        take = jnp.logical_and(hit, seen == o)
                        starts[o] = jnp.where(take, row, starts[o])
                    seen = seen + hit.astype(jnp.int32)
                for o in range(2):
                    al = pl.multiple_of(starts[o] // 8 * 8, 8)
                    rem = starts[o] - al
                    window = pltpu.roll(
                        wide[pl.ds(al, SLAB + 8), :], (SLAB + 8 - rem) % (SLAB + 8), 0
                    )
                    at = pl.multiple_of((p * 2 + o) * SLAB, SLAB)
                    out[pl.ds(at, SLAB), :] = window[:SLAB].astype(BF16)
                return carry

            lax.fori_loop(0, TPD, pick, 0)

    return pl.pallas_call(
        body,
        out_shape=[jax.ShapeDtypeStruct((TPD * TILE, 384), BF16)]
        + [jax.ShapeDtypeStruct((HALO, 384), BF16)] * 2,
        in_specs=[SM] + [ANY] * 5 + [VM] + [SM] * 3,
        out_specs=[VM] * 3,
        scratch_shapes=_half_scratch(rows, half, 384, 3)
        + [pltpu.VMEM((rows, 384), F32), pltpu.VMEM((TPD * TILE + 8, 384), F32)]
        + [pltpu.SemaphoreType.DMA],
        compiler_params=pltpu.CompilerParams(vmem_limit_bytes=48 * MIB),
    )(pos, *toks, w, acc_in, done, *tables)


CAND = 768


def _clear_rest(cand):
    cand[pl.ds(TILE + NB * WIN, CAND - TILE - NB * WIN), :] = jnp.zeros(
        (CAND - TILE - NB * WIN, 384), BF16
    )
    for j in range(NB):
        cand[pl.ds(TILE + j * WIN + SLAB, WIN - SLAB), :] = jnp.zeros((WIN - SLAB, 384), BF16)


def _collect(p, pos_ref, slot, neighbour, first, full_ref, near_ref, far_ref, cand):
    block, blocks = pos_ref[3], pos_ref[6]
    tile = _tile_at(slot, block, p)
    own = pl.multiple_of(p * TILE, TILE)
    cand[pl.ds(0, TILE), :] = full_ref[pl.ds(own, TILE), :]
    up = 1 - 2 * pos_ref[2]
    near_block = (block + up + blocks) % blocks
    far_block = (block - up + blocks) % blocks
    seen_near = jnp.int32(0)
    seen_far = jnp.int32(0)
    places = []
    for j in range(NB):
        other = neighbour[j, tile]
        at = other // TPD
        is_near = at == near_block
        is_far = at == far_block
        s = first[j, tile]
        al = _aligned(s)
        c0 = TILE + j * WIN
        begin = slot[0, other] % TPD * TILE + al
        away = jnp.logical_or(is_near, is_far)

        @pl.when(is_near)
        def _(c0=c0, seen=seen_near):
            row = pl.multiple_of((p * 2 + seen) * SLAB, SLAB)
            cand[pl.ds(c0, SLAB), :] = near_ref[pl.ds(row, SLAB), :]

        @pl.when(is_far)
        def _(c0=c0, seen=seen_far):
            row = pl.multiple_of((p * 2 + seen) * SLAB, SLAB)
            cand[pl.ds(c0, SLAB), :] = far_ref[pl.ds(row, SLAB), :]

        @pl.when(jnp.logical_not(away))
        def _(c0=c0, begin=begin):
            cand[pl.ds(c0, WIN), :] = full_ref[pl.ds(pl.multiple_of(begin, 16), WIN), :]

        places.append(c0 + jnp.where(away, 0, s - al))
        seen_near = seen_near + is_near.astype(jnp.int32)
        seen_far = seen_far + is_far.astype(jnp.int32)
    return tile, places


def weigh(pos, queries, full, near_k, far_k, tables):
    scale = 1.0 / math.sqrt(HD)

    def body(pos_ref, q_ref, full_ref, near_ref, far_ref, slot, neighbour, first, length,
             low, high, prob, total, cand):
        p = pl.program_id(0)

        @pl.when(p == 0)
        def _():
            _clear_rest(cand)

        tile, places = _collect(
            p, pos_ref, slot, neighbour, first, full_ref, near_ref, far_ref, cand
        )
        col = lax.broadcasted_iota(jnp.int32, (8, CAND), 1)
        lows = jnp.where(col < TILE, 0, TILE)
        highs = jnp.where(col < TILE, TILE, 0)
        for j in range(NB):
            valid = jnp.logical_and(col >= places[j], col < places[j] + length[j, tile])
            lows = jnp.where(valid, low[j, tile], lows)
            highs = jnp.where(valid, high[j, tile], highs)
        row = lax.broadcasted_iota(jnp.int32, (TILE, CAND - TILE), 0)
        allowed = jnp.logical_and(row >= lows[0:1, TILE:], row < highs[0:1, TILE:])
        for h in range(3):
            cols = slice(h * HD, h * HD + HD)
            scores = lax.dot_general(
                q_ref[:, cols],
                cand[:, cols],
                (((1,), (1,)), ((), ())),
                preferred_element_type=F32,
            ) * scale
            own = scores[:, :TILE]
            slabs = jnp.where(allowed, scores[:, TILE:], -jnp.inf)
            top = jnp.maximum(
                jnp.max(own, axis=-1, keepdims=True), jnp.max(slabs, axis=-1, keepdims=True)
            )
            own = jnp.exp(own - top)
            slabs = jnp.exp(slabs - top)
            total[:, cols] = jnp.broadcast_to(
                jnp.sum(own, axis=-1, keepdims=True) + jnp.sum(slabs, axis=-1, keepdims=True),
                (TILE, HD),
            )
            prob[0, h, :, :TILE] = own.astype(BF16)
            prob[0, h, :, TILE:] = slabs.astype(BF16)

    return pl.pallas_call(
        body,
        grid=(TPD,),
        out_shape=[
            jax.ShapeDtypeStruct((TPD, 3, TILE, CAND), BF16),
            jax.ShapeDtypeStruct((TPD * TILE, 384), F32),
        ],
        in_specs=[SM, pl.BlockSpec((TILE, 384), lambda p: (p, 0)), VM, VM, VM] + [SM] * 6,
        out_specs=[
            pl.BlockSpec((1, 3, TILE, CAND), lambda p: (p, 0, 0, 0)),
            pl.BlockSpec((TILE, 384), lambda p: (p, 0)),
        ],
        scratch_shapes=[pltpu.VMEM((CAND, 384), BF16)],
        compiler_params=pltpu.CompilerParams(vmem_limit_bytes=24 * MIB),
    )(pos, queries, full, near_k, far_k, *tables)


def mix(pos, prob, total, full, near_v, far_v, tables):
    def body(pos_ref, prob_ref, total_ref, full_ref, near_ref, far_ref, slot, neighbour, first,
             out, cand):
        p = pl.program_id(0)

        @pl.when(p == 0)
        def _():
            _clear_rest(cand)

        _collect(p, pos_ref, slot, neighbour, first, full_ref, near_ref, far_ref, cand)
        for h in range(3):
            cols = slice(h * HD, h * HD + HD)
            mixed = jnp.dot(prob_ref[0, h], cand[:, cols], preferred_element_type=F32)
            out[:, cols] = (mixed / total_ref[:, cols]).astype(BF16)

    return pl.pallas_call(
        body,
        grid=(TPD,),
        out_shape=jax.ShapeDtypeStruct((TPD * TILE, 384), BF16),
        in_specs=[
            SM,
            pl.BlockSpec((1, 3, TILE, CAND), lambda p: (p, 0, 0, 0)),
            pl.BlockSpec((TILE, 384), lambda p: (p, 0)),
            VM,
            VM,
            VM,
        ]
        + [SM] * 3,
        out_specs=pl.BlockSpec((TILE, 384), lambda p: (p, 0)),
        scratch_shapes=[pltpu.VMEM((CAND, 384), BF16)],
        compiler_params=pltpu.CompilerParams(vmem_limit_bytes=24 * MIB),
    )(pos, prob, total, full, near_v, far_v, *tables)


def per_device(
    tokens,
    queries,
    w_key,
    w_value,
    tile_slot,
    neighbour_tile,
    slab_start,
    slab_length,
    window_low,
    window_high,
):
    fs = w_key.shape[0]
    ctx = lax.axis_index("ctx")
    tp = lax.axis_index("tp")
    pos = jnp.stack(
        [ctx >> 3, (ctx >> 1) & 3, ctx & 1, ctx, tp >> 2, tp & 3, jnp.int32(lax.axis_size("ctx"))]
    ).astype(jnp.int32)
    tables = (
        tile_slot.reshape(1, -1),
        neighbour_tile.T,
        slab_start.T,
        slab_length.T,
        window_low.T,
        window_high.T,
    )

    h = tokens.shape[1] // 2
    w = join(w_key, w_value, space=HBM)
    wc = send(w, dc=1)
    ya = send(tokens, dy=1)
    z1w = send(w, sz=1)
    yb = send(tokens, dy=-1)
    wc, tl, tr = lax.optimization_barrier((wc, tokens[:, :h], tokens[:, h:]))
    z1c = send(wc, sz=1)
    xw1 = send(w, sx=1)
    xc1 = send(wc, sx=1)
    z2 = send(z1w, sz=1)
    xw1, pos = lax.optimization_barrier((xw1, pos))
    xw2 = send(xw1, sx=1)
    z_l = send(tl, dzl=1)
    near = join(z1w, z1c, z2)
    xn1 = send(near, sx=1)
    far = send(near, dc=1)
    z_r = send(tr, dzl=1)
    xf1 = send(far, sx=1)
    yo_l = send(ya[:, :h], dy=1)
    yo_r = send(yb[:, h:], dy=-1)
    xn2 = send(xn1, sx=1)
    ua_l = send(z_l, dy=1)
    ub_l = send(z_l, dy=-1)
    uo_l = send(yo_l, dzl=1)
    uo_r = send(yo_r, dzl=1)
    ua_r = send(z_r, dy=1)
    ub_r = send(z_r, dy=-1)
    pieces = [
        (w, 0, False, 0, SAME),
        (wc, 0, False, 0, OTHER),
        (near, 0, False, 0, NEAR),
        (far, 0, False, 0, FAR),
    ]
    for p, xrel, signed, plan in (
        (xw1, 1, True, SAME),
        (xc1, 1, True, OTHER),
        (xw2, 2, False, SAME),
        (xn1, 1, True, NEAR),
        (xf1, 1, True, FAR),
        (xn2, 2, False, NEAR),
    ):
        pieces += [(p, xrel, signed, 0, plan), (send(p, dc=1), xrel, signed, 1, plan)]

    n = tokens.shape[0]
    toks = (tokens, ya, yb, yo_l, yo_r, z_l, z_r)
    at = ((0, 0), (n, 0), (2 * n, 0), (3 * n, 0), (3 * n, h), (4 * n, 0), (4 * n, h))
    kv1, w_all = project(pos, toks, at, 5 * n, pieces, fs)
    w_all = w_all.reshape(tokens.shape[1], 768)
    part = project_half((ua_l, ub_l, uo_l), w_all)
    rest = (ua_r, ub_r, uo_r)
    last = (
        kv1,
        ((0, 0), (0, -1), (0, 1), (0, 2), (1, 0)),
        ((1, -1), (1, 1), (1, 2)),
        tables[:3],
    )
    keys, near_k, far_k = project_last(0, pos, rest, w_all, part, *last)
    part = lax.optimization_barrier((part, far_k))[0]
    far_k = send(far_k, far=1)
    near_k = send(near_k, dc=1)
    values, near_v, far_v = project_last(1, pos, rest, w_all, part, *last)
    far_v = send(far_v, far=1)
    near_v = send(near_v, dc=1)
    prob, total = weigh(pos, queries, keys, near_k, far_k, tables)
    return mix(pos, prob, total, values, near_v, far_v, tables[:3])


def solution(mesh):
    in_specs = (
        P(("ctx", "tp"), None),
        P("ctx", "tp"),
        P("ctx", "tp"),
        P("ctx", "tp"),
        P(),
        P(),
        P(),
        P(),
        P(),
        P(),
    )
    out_specs = P("ctx", "tp")
    return jax.shard_map(
        per_device, mesh=mesh, in_specs=in_specs, out_specs=out_specs, check_vma=False
    )
```

```python
import math

import jax
import jax.numpy as jnp
from jax import lax
from jax.experimental import pallas as pl
from jax.experimental.pallas import tpu as pltpu
from jax.sharding import PartitionSpec as P


HD = 128
TILE = 256
NB = 6
SLAB = 64
TPD = 4
HALO = TPD * 2 * SLAB
WIN = 80
NX, NZH, NC, NZL, NY = 4, 4, 2, 2, 4
AXES = ("ctx", "tp")
BF16 = jnp.bfloat16
F32 = jnp.float32


def _index(x, zh, c, zl, y):
    return (((x % NX) * NZH + zh % NZH) * NC + c % NC) * (NZL * NY) + zl % NZL * NY + y % NY


def _moves(dx=0, dzh=0, dc=0, dzl=0, dy=0, sx=0, sz=0):
    pairs = []
    for x in range(NX):
        for zh in range(NZH):
            for c in range(NC):
                for zl in range(NZL):
                    for y in range(NY):
                        pairs.append(
                            (
                                _index(x, zh, c, zl, y),
                                _index(
                                    x + dx + sx * (1 - 2 * c),
                                    zh + dzh + sz * (1 - 2 * c),
                                    c + dc,
                                    zl + dzl,
                                    y + dy,
                                ),
                            )
                        )
    return pairs


def _far_moves():
    blocks = NX * NZH * NC
    tps = NZL * NY
    return [
        (b * tps + t, (b - 1 + 2 * (b % 2)) % blocks * tps + t)
        for b in range(blocks)
        for t in range(tps)
    ]


def send(a, **step):
    return lax.ppermute(a, AXES, _far_moves() if "far" in step else _moves(**step))


SAME = ((0, False, 0),)
OTHER = ((0, False, 1),)
NEAR = ((1, True, 0), (1, True, 1), (2, False, 0))
FAR = ((-1, True, 1), (-1, True, 0), (2, False, 1))


ANY = pl.BlockSpec(memory_space=pl.ANY)
HBM = pl.BlockSpec(memory_space=pltpu.HBM)
SM = pl.BlockSpec(memory_space=pltpu.SMEM)
VM = pl.BlockSpec(memory_space=pltpu.VMEM)
MIB = 1024 * 1024


def join(*parts, space=None):
    rows = [p.shape[0] for p in parts]

    def body(*refs):
        out, sems = refs[-2:]
        copies = []
        for i, ref in enumerate(refs[:-2]):
            copies.append(
                pltpu.make_async_copy(ref, out.at[pl.ds(sum(rows[:i]), rows[i]), :], sems.at[i])
            )
        for cp in copies:
            cp.start()
        for cp in copies:
            cp.wait()

    return pl.pallas_call(
        body,
        out_shape=jax.ShapeDtypeStruct((sum(rows), parts[0].shape[1]), parts[0].dtype),
        in_specs=[space or ANY] * len(parts),
        out_specs=ANY,
        scratch_shapes=[pltpu.SemaphoreType.DMA((len(parts),))],
        compiler_params=pltpu.CompilerParams(vmem_limit_bytes=MIB),
    )(*parts)


def project(pos, toks, tok_at, rows, pieces, fs):
    nt, np_ = len(toks), len(pieces)
    features = fs * NX * NZH * NC
    quarter = features // NX

    def body(*refs):
        pos_ref = refs[0]
        tok_refs = refs[1 : 1 + nt]
        piece_refs = refs[1 + nt : 1 + nt + np_]
        out, w_out, t_buf, w_buf, acc, t_sem, w_sem, o_sem = refs[1 + nt + np_ :]
        x, zh, c = pos_ref[0], pos_ref[1], pos_ref[2]
        steps = (0, 2 * c - 1, 1 - 2 * c, 2)
        at = [(x + step + NX) % NX for step in steps]
        waits = [[] for _ in steps]
        count = 0
        for group in range(NX):
            for ref, (_, xrel, signed, flip, plan) in zip(piece_refs, pieces):
                if (1 + flip if signed else xrel // 2 * 3) != group:
                    continue
                core = (c + flip) % NC
                sign = 2 * core - 1
                for i, (zrel, zsigned, other) in enumerate(plan):
                    zs = (zh + (sign * zrel if zsigned else zrel) + NZH) % NZH
                    place = pl.multiple_of((zs * NC + (core + other) % NC) * fs, 32)
                    for kv in range(2):
                        cp = pltpu.make_async_copy(
                            ref.at[pl.ds((2 * i + kv) * fs, fs), :],
                            w_buf.at[at[group], pl.ds(place, fs), pl.ds(kv * 384, 384)],
                            w_sem.at[count],
                        )
                        cp.start()
                        waits[group].append(cp)
                        count += 1
            if group == 0:
                for i, (ref, (r0, c0)) in enumerate(zip(tok_refs, tok_at)):
                    for k in range(ref.shape[1] // quarter):
                        cp = pltpu.make_async_copy(
                            ref.at[:, pl.ds(k * quarter, quarter)],
                            t_buf.at[c0 // quarter + k, pl.ds(r0, ref.shape[0]), :],
                            t_sem.at[i, k],
                        )
                        cp.start()
                        waits[0].append(cp)
        backs = []
        for q in range(NX):
            for cp in waits[q]:
                cp.wait()
            back = pltpu.make_async_copy(w_buf.at[at[q]], w_out.at[at[q]], o_sem.at[q])
            back.start()
            backs.append(back)
            part = jnp.dot(t_buf[at[q]], w_buf[at[q]], preferred_element_type=F32)
            if q == 0:
                acc[...] = part
            elif q < NX - 1:
                acc[...] += part
            else:
                out[...] = (acc[...] + part).astype(BF16)
        for back in backs:
            back.wait()

    n_copies = 2 * sum(len(p[4]) for p in pieces)
    return pl.pallas_call(
        body,
        out_shape=[
            jax.ShapeDtypeStruct((rows, 768), BF16),
            jax.ShapeDtypeStruct((NX, quarter, 768), BF16),
        ],
        in_specs=[SM] + [HBM] * (nt + np_),
        out_specs=[VM, ANY],
        scratch_shapes=[
            pltpu.VMEM((NX, rows, quarter), BF16),
            pltpu.VMEM((NX, quarter, 768), BF16),
            pltpu.VMEM((rows, 768), F32),
            pltpu.SemaphoreType.DMA((nt, NX)),
            pltpu.SemaphoreType.DMA((n_copies,)),
            pltpu.SemaphoreType.DMA((NX,)),
        ],
        compiler_params=pltpu.CompilerParams(vmem_limit_bytes=36 * MIB),
    )(pos, *toks, *[p[0] for p in pieces])


CHUNKS = 2


def _half_product(toks, w, row0, cols, t_buf, w_buf, t_sem, w_sem, unroll=False):
    n = toks[0].shape[0]
    step = toks[0].shape[1] // CHUNKS

    def copies(k):
        at = k * step if isinstance(k, int) else pl.multiple_of(k * step, 128)
        yield pltpu.make_async_copy(
            w.at[pl.ds(row0 + at, step), pl.ds(*cols)], w_buf.at[k], w_sem.at[k]
        )
        for i, ref in enumerate(toks):
            yield pltpu.make_async_copy(
                ref.at[:, pl.ds(at, step)], t_buf.at[k, pl.ds(i * n, n), :], t_sem.at[k, i]
            )

    for k in range(CHUNKS):
        for cp in copies(k):
            cp.start()

    def product(acc):
        def one(k, carry):
            for cp in copies(k):
                cp.wait()
            acc[...] += jnp.dot(t_buf[k], w_buf[k], preferred_element_type=F32)
            return carry

        if unroll:
            for k in range(CHUNKS):
                one(k, 0)
        else:
            lax.fori_loop(0, CHUNKS, one, 0)

    return product


def _half_scratch(rows, half, width, ntok):
    return [
        pltpu.VMEM((CHUNKS, rows, half // CHUNKS), BF16),
        pltpu.VMEM((CHUNKS, half // CHUNKS, width), BF16),
        pltpu.SemaphoreType.DMA((CHUNKS, ntok)),
        pltpu.SemaphoreType.DMA((CHUNKS,)),
    ]


def project_half(toks, w):
    rows = sum(t.shape[0] for t in toks)
    half = toks[0].shape[1]

    def body(t0, t1, t2, w_ref, acc, t_buf, w_buf, t_sem, w_sem):
        product = _half_product((t0, t1, t2), w_ref, 0, (0, 768), t_buf, w_buf, t_sem, w_sem)
        acc[...] = jnp.zeros_like(acc)
        product(acc)

    return pl.pallas_call(
        body,
        out_shape=jax.ShapeDtypeStruct((rows, 768), F32),
        in_specs=[ANY] * 4,
        out_specs=VM,
        scratch_shapes=_half_scratch(rows, half, 768, 3),
        compiler_params=pltpu.CompilerParams(vmem_limit_bytes=48 * MIB),
    )(*toks, w)


def _tile_at(slot_ref, block, p):
    tile = block * TPD
    for i in range(1, TPD):
        tile = jnp.where(slot_ref[0, block * TPD + i] == block * TPD + p, block * TPD + i, tile)
    return tile


def _aligned(start):
    return jnp.minimum(start // 16 * 16, TILE - WIN)


def project_last(side, pos, toks, w, acc_in, done, done_places, places, tables):
    n, half = toks[0].shape
    rows = n * len(toks)

    def body(pos_ref, t0, t1, t2, w_ref, acc_ref, done_ref, slot, neighbour, first,
             full, near, far, t_buf, w_buf, t_sem, w_sem, acc, wide, a_sem, picks):
        block, zl, y, blocks = pos_ref[3], pos_ref[4], pos_ref[5], pos_ref[6]
        cols = (side * 384, 384)
        begin = pltpu.make_async_copy(acc_ref.at[:, pl.ds(*cols)], acc, a_sem)
        begin.start()
        product = _half_product(
            (t0, t1, t2), w_ref, half, cols, t_buf, w_buf, t_sem, w_sem, unroll=True
        )

        def row_of(place):
            dzl, dy = place
            return pl.multiple_of(((zl + dzl) % NZL * NY + (y + dy + NY) % NY) * n, n)

        for i, place in enumerate(done_places):
            part = done_ref[i * n : (i + 1) * n, side * 384 : side * 384 + 384]
            full[pl.ds(row_of(place), n), :] = part
            wide[pl.ds(row_of(place), n), :] = part.astype(F32)
        up = 1 - 2 * pos_ref[2]
        for d, step in enumerate((-up, up)):
            target = (block + step + blocks) % blocks

            def find(p, carry, d=d, target=target):
                tile = _tile_at(slot, target, p)
                seen = jnp.int32(0)
                starts = [jnp.int32(0), jnp.int32(0)]
                for j in range(NB):
                    other = neighbour[j, tile]
                    hit = other // TPD == block
                    row = slot[0, other] % TPD * TILE + first[j, tile]
                    for o in range(2):
                        take = jnp.logical_and(hit, seen == o)
                        starts[o] = jnp.where(take, row, starts[o])
                    seen = seen + hit.astype(jnp.int32)
                for o in range(2):
                    picks[d * TPD * 2 + p * 2 + o] = starts[o]
                return carry

            lax.fori_loop(0, TPD, find, 0)
        begin.wait()
        product(acc)
        for i, place in enumerate(places):
            part = acc[i * n : (i + 1) * n, :].astype(BF16)
            full[pl.ds(row_of(place), n), :] = part
            wide[pl.ds(row_of(place), n), :] = part.astype(F32)
        for d, out in enumerate((far, near)):

            def pick(i, carry, d=d, out=out):
                start = picks[d * TPD * 2 + i]
                al = pl.multiple_of(start // 8 * 8, 8)
                window = pltpu.roll(
                    wide[pl.ds(al, SLAB + 8), :], (SLAB + 8 - (start - al)) % (SLAB + 8), 0
                )
                at = pl.multiple_of(i * SLAB, SLAB)
                out[pl.ds(at, SLAB), :] = window[:SLAB].astype(BF16)
                return carry

            lax.fori_loop(0, TPD * 2, pick, 0)

    return pl.pallas_call(
        body,
        out_shape=[jax.ShapeDtypeStruct((TPD * TILE, 384), BF16)]
        + [jax.ShapeDtypeStruct((HALO, 384), BF16)] * 2,
        in_specs=[SM] + [ANY] * 5 + [VM] + [SM] * 3,
        out_specs=[VM] * 3,
        scratch_shapes=_half_scratch(rows, half, 384, 3)
        + [pltpu.VMEM((rows, 384), F32), pltpu.VMEM((TPD * TILE + 8, 384), F32)]
        + [pltpu.SemaphoreType.DMA, pltpu.SMEM((TPD * 4,), jnp.int32)],
        compiler_params=pltpu.CompilerParams(vmem_limit_bytes=48 * MIB),
    )(pos, *toks, w, acc_in, done, *tables)


CAND = 768


def _clear_rest(cand):
    cand[pl.ds(TILE + NB * WIN, CAND - TILE - NB * WIN), :] = jnp.zeros(
        (CAND - TILE - NB * WIN, 384), BF16
    )
    for j in range(NB):
        cand[pl.ds(TILE + j * WIN + SLAB, WIN - SLAB), :] = jnp.zeros((WIN - SLAB, 384), BF16)


def _collect(p, pos_ref, slot, neighbour, first, full_ref, near_ref, far_ref, cand):
    block, blocks = pos_ref[3], pos_ref[6]
    tile = _tile_at(slot, block, p)
    own = pl.multiple_of(p * TILE, TILE)
    cand[pl.ds(0, TILE), :] = full_ref[pl.ds(own, TILE), :]
    up = 1 - 2 * pos_ref[2]
    near_block = (block + up + blocks) % blocks
    far_block = (block - up + blocks) % blocks
    seen_near = jnp.int32(0)
    seen_far = jnp.int32(0)
    places = []
    for j in range(NB):
        other = neighbour[j, tile]
        at = other // TPD
        is_near = at == near_block
        is_far = at == far_block
        s = first[j, tile]
        al = _aligned(s)
        c0 = TILE + j * WIN
        begin = slot[0, other] % TPD * TILE + al
        away = jnp.logical_or(is_near, is_far)

        @pl.when(is_near)
        def _(c0=c0, seen=seen_near):
            row = pl.multiple_of((p * 2 + seen) * SLAB, SLAB)
            cand[pl.ds(c0, SLAB), :] = near_ref[pl.ds(row, SLAB), :]

        @pl.when(is_far)
        def _(c0=c0, seen=seen_far):
            row = pl.multiple_of((p * 2 + seen) * SLAB, SLAB)
            cand[pl.ds(c0, SLAB), :] = far_ref[pl.ds(row, SLAB), :]

        @pl.when(jnp.logical_not(away))
        def _(c0=c0, begin=begin):
            cand[pl.ds(c0, WIN), :] = full_ref[pl.ds(pl.multiple_of(begin, 16), WIN), :]

        places.append(c0 + jnp.where(away, 0, s - al))
        seen_near = seen_near + is_near.astype(jnp.int32)
        seen_far = seen_far + is_far.astype(jnp.int32)
    return tile, places


def weigh(pos, queries, full, near_k, far_k, tables):
    scale = 1.0 / math.sqrt(HD)

    def body(pos_ref, q_ref, full_ref, near_ref, far_ref, slot, neighbour, first, length,
             low, high, prob, total, cand):
        p = pl.program_id(0)

        @pl.when(p == 0)
        def _():
            _clear_rest(cand)

        tile, places = _collect(
            p, pos_ref, slot, neighbour, first, full_ref, near_ref, far_ref, cand
        )
        col = lax.broadcasted_iota(jnp.int32, (8, CAND), 1)
        lows = jnp.where(col < TILE, 0, TILE)
        highs = jnp.where(col < TILE, TILE, 0)
        for j in range(NB):
            valid = jnp.logical_and(col >= places[j], col < places[j] + length[j, tile])
            lows = jnp.where(valid, low[j, tile], lows)
            highs = jnp.where(valid, high[j, tile], highs)
        row = lax.broadcasted_iota(jnp.int32, (TILE, CAND - TILE), 0)
        allowed = jnp.logical_and(row >= lows[0:1, TILE:], row < highs[0:1, TILE:])
        for h in range(3):
            cols = slice(h * HD, h * HD + HD)
            scores = lax.dot_general(
                q_ref[:, cols],
                cand[:, cols],
                (((1,), (1,)), ((), ())),
                preferred_element_type=F32,
            ) * scale
            own = scores[:, :TILE]
            slabs = jnp.where(allowed, scores[:, TILE:], -jnp.inf)
            top = jnp.maximum(
                jnp.max(own, axis=-1, keepdims=True), jnp.max(slabs, axis=-1, keepdims=True)
            )
            own = jnp.exp(own - top)
            slabs = jnp.exp(slabs - top)
            total[:, cols] = jnp.broadcast_to(
                jnp.sum(own, axis=-1, keepdims=True) + jnp.sum(slabs, axis=-1, keepdims=True),
                (TILE, HD),
            )
            prob[0, h, :, :TILE] = own.astype(BF16)
            prob[0, h, :, TILE:] = slabs.astype(BF16)

    return pl.pallas_call(
        body,
        grid=(TPD,),
        out_shape=[
            jax.ShapeDtypeStruct((TPD, 3, TILE, CAND), BF16),
            jax.ShapeDtypeStruct((TPD * TILE, 384), F32),
        ],
        in_specs=[SM, pl.BlockSpec((TILE, 384), lambda p: (p, 0)), VM, VM, VM] + [SM] * 6,
        out_specs=[
            pl.BlockSpec((1, 3, TILE, CAND), lambda p: (p, 0, 0, 0)),
            pl.BlockSpec((TILE, 384), lambda p: (p, 0)),
        ],
        scratch_shapes=[pltpu.VMEM((CAND, 384), BF16)],
        compiler_params=pltpu.CompilerParams(vmem_limit_bytes=24 * MIB),
    )(pos, queries, full, near_k, far_k, *tables)


def mix(pos, prob, total, full, near_v, far_v, tables):
    def body(pos_ref, prob_ref, total_ref, full_ref, near_ref, far_ref, slot, neighbour, first,
             out, cand):
        p = pl.program_id(0)

        @pl.when(p == 0)
        def _():
            _clear_rest(cand)

        _collect(p, pos_ref, slot, neighbour, first, full_ref, near_ref, far_ref, cand)
        for h in range(3):
            cols = slice(h * HD, h * HD + HD)
            mixed = jnp.dot(prob_ref[0, h], cand[:, cols], preferred_element_type=F32)
            out[:, cols] = (mixed / total_ref[:, cols]).astype(BF16)

    return pl.pallas_call(
        body,
        grid=(TPD,),
        out_shape=jax.ShapeDtypeStruct((TPD * TILE, 384), BF16),
        in_specs=[
            SM,
            pl.BlockSpec((1, 3, TILE, CAND), lambda p: (p, 0, 0, 0)),
            pl.BlockSpec((TILE, 384), lambda p: (p, 0)),
            VM,
            VM,
            VM,
        ]
        + [SM] * 3,
        out_specs=pl.BlockSpec((TILE, 384), lambda p: (p, 0)),
        scratch_shapes=[pltpu.VMEM((CAND, 384), BF16)],
        compiler_params=pltpu.CompilerParams(vmem_limit_bytes=24 * MIB),
    )(pos, prob, total, full, near_v, far_v, *tables)


def per_device(
    tokens,
    queries,
    w_key,
    w_value,
    tile_slot,
    neighbour_tile,
    slab_start,
    slab_length,
    window_low,
    window_high,
):
    fs = w_key.shape[0]
    ctx = lax.axis_index("ctx")
    tp = lax.axis_index("tp")
    pos = jnp.stack(
        [ctx >> 3, (ctx >> 1) & 3, ctx & 1, ctx, tp >> 2, tp & 3, jnp.int32(lax.axis_size("ctx"))]
    ).astype(jnp.int32)
    tables = (
        tile_slot.reshape(1, -1),
        neighbour_tile.T,
        slab_start.T,
        slab_length.T,
        window_low.T,
        window_high.T,
    )

    h = tokens.shape[1] // 2
    w = join(w_key, w_value, space=HBM)
    wc = send(w, dc=1)
    ya = send(tokens, dy=1)
    z1w = send(w, sz=1)
    yb = send(tokens, dy=-1)
    wc, tl, tr = lax.optimization_barrier((wc, tokens[:, :h], tokens[:, h:]))
    z1c = send(wc, sz=1)
    xw1 = send(w, sx=1)
    xc1 = send(wc, sx=1)
    z2 = send(z1w, sz=1)
    xw1, pos = lax.optimization_barrier((xw1, pos))
    xw2 = send(xw1, sx=1)
    z_l = send(tl, dzl=1)
    near = join(z1w, z1c, z2)
    xn1 = send(near, sx=1)
    far = send(near, dc=1)
    z_r = send(tr, dzl=1)
    xf1 = send(far, sx=1)
    yo_l = send(ya[:, :h], dy=1)
    yo_r = send(yb[:, h:], dy=-1)
    xn2 = send(xn1, sx=1)
    ua_l = send(z_l, dy=1)
    ub_l = send(z_l, dy=-1)
    uo_l = send(yo_l, dzl=1)
    uo_r = send(yo_r, dzl=1)
    ua_r = send(z_r, dy=1)
    ub_r = send(z_r, dy=-1)
    pieces = [
        (w, 0, False, 0, SAME),
        (wc, 0, False, 0, OTHER),
        (near, 0, False, 0, NEAR),
        (far, 0, False, 0, FAR),
    ]
    for p, xrel, signed, plan in (
        (xw1, 1, True, SAME),
        (xc1, 1, True, OTHER),
        (xw2, 2, False, SAME),
        (xn1, 1, True, NEAR),
        (xf1, 1, True, FAR),
        (xn2, 2, False, NEAR),
    ):
        pieces += [(p, xrel, signed, 0, plan), (send(p, dc=1), xrel, signed, 1, plan)]

    n = tokens.shape[0]
    toks = (tokens, ya, yb, yo_l, yo_r, z_l, z_r)
    at = ((0, 0), (n, 0), (2 * n, 0), (3 * n, 0), (3 * n, h), (4 * n, 0), (4 * n, h))
    kv1, w_all = project(pos, toks, at, 5 * n, pieces, fs)
    w_all = w_all.reshape(tokens.shape[1], 768)
    part = project_half((ua_l, ub_l, uo_l), w_all)
    rest = (ua_r, ub_r, uo_r)
    last = (
        kv1,
        ((0, 0), (0, -1), (0, 1), (0, 2), (1, 0)),
        ((1, -1), (1, 1), (1, 2)),
        tables[:3],
    )
    keys, near_k, far_k = project_last(0, pos, rest, w_all, part, *last)
    part = lax.optimization_barrier((part, far_k))[0]
    far_k = send(far_k, far=1)
    near_k = send(near_k, dc=1)
    values, near_v, far_v = project_last(1, pos, rest, w_all, part, *last)
    far_v = send(far_v, far=1)
    near_v = send(near_v, dc=1)
    prob, total = weigh(pos, queries, keys, near_k, far_k, tables)
    return mix(pos, prob, total, values, near_v, far_v, tables[:3])


def solution(mesh):
    in_specs = (
        P(("ctx", "tp"), None),
        P("ctx", "tp"),
        P("ctx", "tp"),
        P("ctx", "tp"),
        P(),
        P(),
        P(),
        P(),
        P(),
        P(),
    )
    out_specs = P("ctx", "tp")
    return jax.shard_map(
        per_device, mesh=mesh, in_specs=in_specs, out_specs=out_specs, check_vma=False
    )
```

```python
import math

import jax
import jax.numpy as jnp
from jax import lax
from jax.experimental import pallas as pl
from jax.experimental.pallas import tpu as pltpu
from jax.sharding import PartitionSpec as P


HD = 128
TILE = 256
NB = 6
SLAB = 64
TPD = 4
HALO = TPD * 2 * SLAB
WIN = 80
NX, NZH, NC, NZL, NY = 4, 4, 2, 2, 4
AXES = ("ctx", "tp")
BF16 = jnp.bfloat16
F32 = jnp.float32


def _index(x, zh, c, zl, y):
    return (((x % NX) * NZH + zh % NZH) * NC + c % NC) * (NZL * NY) + zl % NZL * NY + y % NY


def _moves(dx=0, dzh=0, dc=0, dzl=0, dy=0, sx=0, sz=0):
    pairs = []
    for x in range(NX):
        for zh in range(NZH):
            for c in range(NC):
                for zl in range(NZL):
                    for y in range(NY):
                        pairs.append(
                            (
                                _index(x, zh, c, zl, y),
                                _index(
                                    x + dx + sx * (1 - 2 * c),
                                    zh + dzh + sz * (1 - 2 * c),
                                    c + dc,
                                    zl + dzl,
                                    y + dy,
                                ),
                            )
                        )
    return pairs


def _far_moves():
    blocks = NX * NZH * NC
    tps = NZL * NY
    return [
        (b * tps + t, (b - 1 + 2 * (b % 2)) % blocks * tps + t)
        for b in range(blocks)
        for t in range(tps)
    ]


def send(a, **step):
    return lax.ppermute(a, AXES, _far_moves() if "far" in step else _moves(**step))


SAME = ((0, False, 0),)
OTHER = ((0, False, 1),)
NEAR = ((1, True, 0), (1, True, 1), (2, False, 0))
FAR = ((-1, True, 1), (-1, True, 0), (2, False, 1))


ANY = pl.BlockSpec(memory_space=pl.ANY)
HBM = pl.BlockSpec(memory_space=pltpu.HBM)
SM = pl.BlockSpec(memory_space=pltpu.SMEM)
VM = pl.BlockSpec(memory_space=pltpu.VMEM)
MIB = 1024 * 1024


def join(*parts, space=None):
    rows = [p.shape[0] for p in parts]

    def body(*refs):
        out, sems = refs[-2:]
        copies = []
        for i, ref in enumerate(refs[:-2]):
            copies.append(
                pltpu.make_async_copy(ref, out.at[pl.ds(sum(rows[:i]), rows[i]), :], sems.at[i])
            )
        for cp in copies:
            cp.start()
        for cp in copies:
            cp.wait()

    return pl.pallas_call(
        body,
        out_shape=jax.ShapeDtypeStruct((sum(rows), parts[0].shape[1]), parts[0].dtype),
        in_specs=[space or ANY] * len(parts),
        out_specs=ANY,
        scratch_shapes=[pltpu.SemaphoreType.DMA((len(parts),))],
        compiler_params=pltpu.CompilerParams(vmem_limit_bytes=MIB),
    )(*parts)


def project(pos, toks, tok_at, rows, pieces, fs):
    nt, np_ = len(toks), len(pieces)
    features = fs * NX * NZH * NC
    quarter = features // NX

    def body(*refs):
        pos_ref = refs[0]
        tok_refs = refs[1 : 1 + nt]
        piece_refs = refs[1 + nt : 1 + nt + np_]
        out, w_out, t_buf, w_buf, acc, t_sem, w_sem, o_sem = refs[1 + nt + np_ :]
        x, zh, c = pos_ref[0], pos_ref[1], pos_ref[2]
        steps = (0, 2 * c - 1, 1 - 2 * c, 2)
        at = [(x + step + NX) % NX for step in steps]
        waits = [[] for _ in steps]
        count = 0
        for group in range(NX):
            for ref, (_, xrel, signed, flip, plan) in zip(piece_refs, pieces):
                if (1 + flip if signed else xrel // 2 * 3) != group:
                    continue
                core = (c + flip) % NC
                sign = 2 * core - 1
                for i, (zrel, zsigned, other) in enumerate(plan):
                    zs = (zh + (sign * zrel if zsigned else zrel) + NZH) % NZH
                    place = pl.multiple_of((zs * NC + (core + other) % NC) * fs, 32)
                    for kv in range(2):
                        cp = pltpu.make_async_copy(
                            ref.at[pl.ds((2 * i + kv) * fs, fs), :],
                            w_buf.at[at[group], pl.ds(place, fs), pl.ds(kv * 384, 384)],
                            w_sem.at[count],
                        )
                        cp.start()
                        waits[group].append(cp)
                        count += 1
            if group == 0:
                for i, (ref, (r0, c0)) in enumerate(zip(tok_refs, tok_at)):
                    for k in range(ref.shape[1] // quarter):
                        cp = pltpu.make_async_copy(
                            ref.at[:, pl.ds(k * quarter, quarter)],
                            t_buf.at[c0 // quarter + k, pl.ds(r0, ref.shape[0]), :],
                            t_sem.at[i, k],
                        )
                        cp.start()
                        waits[0].append(cp)
        backs = []
        for q in range(NX):
            for cp in waits[q]:
                cp.wait()
            back = pltpu.make_async_copy(w_buf.at[at[q]], w_out.at[at[q]], o_sem.at[q])
            back.start()
            backs.append(back)
            part = jnp.dot(t_buf[at[q]], w_buf[at[q]], preferred_element_type=F32)
            if q == 0:
                acc[...] = part
            elif q < NX - 1:
                acc[...] += part
            else:
                out[...] = (acc[...] + part).astype(BF16)
        for back in backs:
            back.wait()

    n_copies = 2 * sum(len(p[4]) for p in pieces)
    return pl.pallas_call(
        body,
        out_shape=[
            jax.ShapeDtypeStruct((rows, 768), BF16),
            jax.ShapeDtypeStruct((NX, quarter, 768), BF16),
        ],
        in_specs=[SM] + [HBM] * (nt + np_),
        out_specs=[VM, ANY],
        scratch_shapes=[
            pltpu.VMEM((NX, rows, quarter), BF16),
            pltpu.VMEM((NX, quarter, 768), BF16),
            pltpu.VMEM((rows, 768), F32),
            pltpu.SemaphoreType.DMA((nt, NX)),
            pltpu.SemaphoreType.DMA((n_copies,)),
            pltpu.SemaphoreType.DMA((NX,)),
        ],
        compiler_params=pltpu.CompilerParams(vmem_limit_bytes=36 * MIB),
    )(pos, *toks, *[p[0] for p in pieces])


CHUNKS = 2


def _half_product(toks, w, row0, cols, t_buf, w_buf, t_sem, w_sem, unroll=False):
    n = toks[0].shape[0]
    step = toks[0].shape[1] // CHUNKS

    def copies(k):
        at = k * step if isinstance(k, int) else pl.multiple_of(k * step, 128)
        yield pltpu.make_async_copy(
            w.at[pl.ds(row0 + at, step), pl.ds(*cols)], w_buf.at[k], w_sem.at[k]
        )
        for i, ref in enumerate(toks):
            yield pltpu.make_async_copy(
                ref.at[:, pl.ds(at, step)], t_buf.at[k, pl.ds(i * n, n), :], t_sem.at[k, i]
            )

    for k in range(CHUNKS):
        for cp in copies(k):
            cp.start()

    def product(acc):
        def one(k, carry):
            for cp in copies(k):
                cp.wait()
            acc[...] += jnp.dot(t_buf[k], w_buf[k], preferred_element_type=F32)
            return carry

        if unroll:
            for k in range(CHUNKS):
                one(k, 0)
        else:
            lax.fori_loop(0, CHUNKS, one, 0)

    return product


def _half_scratch(rows, half, width, ntok):
    return [
        pltpu.VMEM((CHUNKS, rows, half // CHUNKS), BF16),
        pltpu.VMEM((CHUNKS, half // CHUNKS, width), BF16),
        pltpu.SemaphoreType.DMA((CHUNKS, ntok)),
        pltpu.SemaphoreType.DMA((CHUNKS,)),
    ]


def project_half(toks, w):
    rows = sum(t.shape[0] for t in toks)
    half = toks[0].shape[1]

    def body(t0, t1, t2, w_ref, acc, t_buf, w_buf, t_sem, w_sem):
        product = _half_product((t0, t1, t2), w_ref, 0, (0, 768), t_buf, w_buf, t_sem, w_sem)
        acc[...] = jnp.zeros_like(acc)
        product(acc)

    return pl.pallas_call(
        body,
        out_shape=jax.ShapeDtypeStruct((rows, 768), F32),
        in_specs=[ANY] * 4,
        out_specs=VM,
        scratch_shapes=_half_scratch(rows, half, 768, 3),
        compiler_params=pltpu.CompilerParams(vmem_limit_bytes=48 * MIB),
    )(*toks, w)


def _tile_at(slot_ref, block, p):
    tile = block * TPD
    for i in range(1, TPD):
        tile = jnp.where(slot_ref[0, block * TPD + i] == block * TPD + p, block * TPD + i, tile)
    return tile


def _aligned(start):
    return jnp.minimum(start // 16 * 16, TILE - WIN)


def project_last(side, pos, toks, w, acc_in, done, done_places, places, tables):
    n, half = toks[0].shape
    rows = n * len(toks)

    def body(pos_ref, t0, t1, t2, w_ref, acc_ref, done_ref, slot, neighbour, first,
             full, near, far, t_buf, w_buf, t_sem, w_sem, acc, wide, a_sem, picks):
        block, zl, y, blocks = pos_ref[3], pos_ref[4], pos_ref[5], pos_ref[6]
        cols = (side * 384, 384)
        begin = pltpu.make_async_copy(acc_ref.at[:, pl.ds(*cols)], acc, a_sem)
        begin.start()
        product = _half_product(
            (t0, t1, t2), w_ref, half, cols, t_buf, w_buf, t_sem, w_sem, unroll=True
        )

        def row_of(place):
            dzl, dy = place
            return pl.multiple_of(((zl + dzl) % NZL * NY + (y + dy + NY) % NY) * n, n)

        for i, place in enumerate(done_places):
            part = done_ref[i * n : (i + 1) * n, side * 384 : side * 384 + 384]
            full[pl.ds(row_of(place), n), :] = part
            wide[pl.ds(row_of(place), n), :] = part.astype(F32)
        up = 1 - 2 * pos_ref[2]
        for d, step in enumerate((-up, up)):
            target = (block + step + blocks) % blocks

            def find(p, carry, d=d, target=target):
                tile = _tile_at(slot, target, p)
                seen = jnp.int32(0)
                starts = [jnp.int32(0), jnp.int32(0)]
                for j in range(NB):
                    other = neighbour[j, tile]
                    hit = other // TPD == block
                    row = slot[0, other] % TPD * TILE + first[j, tile]
                    for o in range(2):
                        take = jnp.logical_and(hit, seen == o)
                        starts[o] = jnp.where(take, row, starts[o])
                    seen = seen + hit.astype(jnp.int32)
                for o in range(2):
                    picks[d * TPD * 2 + p * 2 + o] = starts[o]
                return carry

            lax.fori_loop(0, TPD, find, 0)
        begin.wait()
        product(acc)
        for i, place in enumerate(places):
            part = acc[i * n : (i + 1) * n, :].astype(BF16)
            full[pl.ds(row_of(place), n), :] = part
            wide[pl.ds(row_of(place), n), :] = part.astype(F32)
        for d, out in enumerate((far, near)):

            def pick(i, carry, d=d, out=out):
                start = picks[d * TPD * 2 + i]
                al = pl.multiple_of(start // 8 * 8, 8)
                window = pltpu.roll(
                    wide[pl.ds(al, SLAB + 8), :], (SLAB + 8 - (start - al)) % (SLAB + 8), 0
                )
                at = pl.multiple_of(i * SLAB, SLAB)
                out[pl.ds(at, SLAB), :] = window[:SLAB].astype(BF16)
                return carry

            lax.fori_loop(0, TPD * 2, pick, 0)

    return pl.pallas_call(
        body,
        out_shape=[jax.ShapeDtypeStruct((TPD * TILE, 384), BF16)]
        + [jax.ShapeDtypeStruct((HALO, 384), BF16)] * 2,
        in_specs=[SM] + [ANY] * 5 + [VM] + [SM] * 3,
        out_specs=[VM] * 3,
        scratch_shapes=_half_scratch(rows, half, 384, 3)
        + [pltpu.VMEM((rows, 384), F32), pltpu.VMEM((TPD * TILE + 8, 384), F32)]
        + [pltpu.SemaphoreType.DMA, pltpu.SMEM((TPD * 4,), jnp.int32)],
        compiler_params=pltpu.CompilerParams(vmem_limit_bytes=48 * MIB),
    )(pos, *toks, w, acc_in, done, *tables)


CAND = 768


def _clear_rest(cand):
    cand[pl.ds(TILE + NB * WIN, CAND - TILE - NB * WIN), :] = jnp.zeros(
        (CAND - TILE - NB * WIN, 384), BF16
    )
    for j in range(NB):
        cand[pl.ds(TILE + j * WIN + SLAB, WIN - SLAB), :] = jnp.zeros((WIN - SLAB, 384), BF16)


def _collect(p, pos_ref, slot, neighbour, first, full_ref, near_ref, far_ref, cand):
    block, blocks = pos_ref[3], pos_ref[6]
    tile = _tile_at(slot, block, p)
    own = pl.multiple_of(p * TILE, TILE)
    cand[pl.ds(0, TILE), :] = full_ref[pl.ds(own, TILE), :]
    up = 1 - 2 * pos_ref[2]
    near_block = (block + up + blocks) % blocks
    far_block = (block - up + blocks) % blocks
    seen_near = jnp.int32(0)
    seen_far = jnp.int32(0)
    places = []
    for j in range(NB):
        other = neighbour[j, tile]
        at = other // TPD
        is_near = at == near_block
        is_far = at == far_block
        s = first[j, tile]
        al = _aligned(s)
        c0 = TILE + j * WIN
        begin = slot[0, other] % TPD * TILE + al
        away = jnp.logical_or(is_near, is_far)

        @pl.when(is_near)
        def _(c0=c0, seen=seen_near):
            row = pl.multiple_of((p * 2 + seen) * SLAB, SLAB)
            cand[pl.ds(c0, SLAB), :] = near_ref[pl.ds(row, SLAB), :]

        @pl.when(is_far)
        def _(c0=c0, seen=seen_far):
            row = pl.multiple_of((p * 2 + seen) * SLAB, SLAB)
            cand[pl.ds(c0, SLAB), :] = far_ref[pl.ds(row, SLAB), :]

        @pl.when(jnp.logical_not(away))
        def _(c0=c0, begin=begin):
            cand[pl.ds(c0, WIN), :] = full_ref[pl.ds(pl.multiple_of(begin, 16), WIN), :]

        places.append(c0 + jnp.where(away, 0, s - al))
        seen_near = seen_near + is_near.astype(jnp.int32)
        seen_far = seen_far + is_far.astype(jnp.int32)
    return tile, places


def weigh(pos, queries, full, near_k, far_k, tables):
    scale = 1.0 / math.sqrt(HD)

    def body(pos_ref, q_ref, full_ref, near_ref, far_ref, slot, neighbour, first, length,
             low, high, prob, total, cand):
        p = pl.program_id(0)

        @pl.when(p == 0)
        def _():
            _clear_rest(cand)

        tile, places = _collect(
            p, pos_ref, slot, neighbour, first, full_ref, near_ref, far_ref, cand
        )
        col = lax.broadcasted_iota(jnp.int32, (8, CAND), 1)
        lows = jnp.where(col < TILE, 0, TILE)
        highs = jnp.where(col < TILE, TILE, 0)
        for j in range(NB):
            valid = jnp.logical_and(col >= places[j], col < places[j] + length[j, tile])
            lows = jnp.where(valid, low[j, tile], lows)
            highs = jnp.where(valid, high[j, tile], highs)
        row = lax.broadcasted_iota(jnp.int32, (TILE, CAND - TILE), 0)
        allowed = jnp.logical_and(row >= lows[0:1, TILE:], row < highs[0:1, TILE:])
        for h in range(3):
            cols = slice(h * HD, h * HD + HD)
            scores = lax.dot_general(
                q_ref[:, cols],
                cand[:, cols],
                (((1,), (1,)), ((), ())),
                preferred_element_type=F32,
            ) * scale
            own = scores[:, :TILE]
            slabs = jnp.where(allowed, scores[:, TILE:], -jnp.inf)
            top = jnp.maximum(
                jnp.max(own, axis=-1, keepdims=True), jnp.max(slabs, axis=-1, keepdims=True)
            )
            own = jnp.exp(own - top)
            slabs = jnp.exp(slabs - top)
            total[pl.ds(pl.multiple_of(p * TILE, TILE), TILE), cols] = jnp.broadcast_to(
                jnp.sum(own, axis=-1, keepdims=True) + jnp.sum(slabs, axis=-1, keepdims=True),
                (TILE, HD),
            )
            prob[p, h, :, :TILE] = own.astype(BF16)
            prob[p, h, :, TILE:] = slabs.astype(BF16)

    return pl.pallas_call(
        body,
        grid=(TPD,),
        out_shape=[
            jax.ShapeDtypeStruct((TPD, 3, TILE, CAND), BF16),
            jax.ShapeDtypeStruct((TPD * TILE, 384), F32),
        ],
        in_specs=[SM, pl.BlockSpec((TILE, 384), lambda p: (p, 0)), VM, VM, VM] + [SM] * 6,
        out_specs=[VM, VM],
        scratch_shapes=[pltpu.VMEM((CAND, 384), BF16)],
        compiler_params=pltpu.CompilerParams(vmem_limit_bytes=24 * MIB),
    )(pos, queries, full, near_k, far_k, *tables)


def mix(pos, prob, total, full, near_v, far_v, tables):
    def body(pos_ref, prob_ref, total_ref, full_ref, near_ref, far_ref, slot, neighbour, first,
             out, cand):
        p = pl.program_id(0)

        @pl.when(p == 0)
        def _():
            _clear_rest(cand)

        _collect(p, pos_ref, slot, neighbour, first, full_ref, near_ref, far_ref, cand)
        for h in range(3):
            cols = slice(h * HD, h * HD + HD)
            mixed = jnp.dot(prob_ref[p, h], cand[:, cols], preferred_element_type=F32)
            rows = pl.ds(pl.multiple_of(p * TILE, TILE), TILE)
            out[:, cols] = (mixed / total_ref[rows, cols]).astype(BF16)

    return pl.pallas_call(
        body,
        grid=(TPD,),
        out_shape=jax.ShapeDtypeStruct((TPD * TILE, 384), BF16),
        in_specs=[
            SM,
            VM,
            VM,
            VM,
            VM,
            VM,
        ]
        + [SM] * 3,
        out_specs=pl.BlockSpec((TILE, 384), lambda p: (p, 0)),
        scratch_shapes=[pltpu.VMEM((CAND, 384), BF16)],
        compiler_params=pltpu.CompilerParams(vmem_limit_bytes=24 * MIB),
    )(pos, prob, total, full, near_v, far_v, *tables)


def per_device(
    tokens,
    queries,
    w_key,
    w_value,
    tile_slot,
    neighbour_tile,
    slab_start,
    slab_length,
    window_low,
    window_high,
):
    fs = w_key.shape[0]
    ctx = lax.axis_index("ctx")
    tp = lax.axis_index("tp")
    pos = jnp.stack(
        [ctx >> 3, (ctx >> 1) & 3, ctx & 1, ctx, tp >> 2, tp & 3, jnp.int32(lax.axis_size("ctx"))]
    ).astype(jnp.int32)
    tables = (
        tile_slot.reshape(1, -1),
        neighbour_tile.T,
        slab_start.T,
        slab_length.T,
        window_low.T,
        window_high.T,
    )

    h = tokens.shape[1] // 2
    w = join(w_key, w_value, space=HBM)
    wc = send(w, dc=1)
    ya = send(tokens, dy=1)
    z1w = send(w, sz=1)
    yb = send(tokens, dy=-1)
    wc, tl, tr = lax.optimization_barrier((wc, tokens[:, :h], tokens[:, h:]))
    z1c = send(wc, sz=1)
    xw1 = send(w, sx=1)
    xc1 = send(wc, sx=1)
    z2 = send(z1w, sz=1)
    xw1, pos = lax.optimization_barrier((xw1, pos))
    xw2 = send(xw1, sx=1)
    z_l = send(tl, dzl=1)
    near = join(z1w, z1c, z2)
    xn1 = send(near, sx=1)
    far = send(near, dc=1)
    z_r = send(tr, dzl=1)
    xf1 = send(far, sx=1)
    yo_l = send(ya[:, :h], dy=1)
    yo_r = send(yb[:, h:], dy=-1)
    xn2 = send(xn1, sx=1)
    ua_l = send(z_l, dy=1)
    ub_l = send(z_l, dy=-1)
    uo_l = send(yo_l, dzl=1)
    uo_r = send(yo_r, dzl=1)
    ua_r = send(z_r, dy=1)
    ub_r = send(z_r, dy=-1)
    pieces = [
        (w, 0, False, 0, SAME),
        (wc, 0, False, 0, OTHER),
        (near, 0, False, 0, NEAR),
        (far, 0, False, 0, FAR),
    ]
    for p, xrel, signed, plan in (
        (xw1, 1, True, SAME),
        (xc1, 1, True, OTHER),
        (xw2, 2, False, SAME),
        (xn1, 1, True, NEAR),
        (xf1, 1, True, FAR),
        (xn2, 2, False, NEAR),
    ):
        pieces += [(p, xrel, signed, 0, plan), (send(p, dc=1), xrel, signed, 1, plan)]

    n = tokens.shape[0]
    toks = (tokens, ya, yb, yo_l, yo_r, z_l, z_r)
    at = ((0, 0), (n, 0), (2 * n, 0), (3 * n, 0), (3 * n, h), (4 * n, 0), (4 * n, h))
    kv1, w_all = project(pos, toks, at, 5 * n, pieces, fs)
    w_all = w_all.reshape(tokens.shape[1], 768)
    part = project_half((ua_l, ub_l, uo_l), w_all)
    rest = (ua_r, ub_r, uo_r)
    last = (
        kv1,
        ((0, 0), (0, -1), (0, 1), (0, 2), (1, 0)),
        ((1, -1), (1, 1), (1, 2)),
        tables[:3],
    )
    keys, near_k, far_k = project_last(0, pos, rest, w_all, part, *last)
    part = lax.optimization_barrier((part, far_k))[0]
    far_k = send(far_k, far=1)
    near_k = send(near_k, dc=1)
    values, near_v, far_v = project_last(1, pos, rest, w_all, part, *last)
    far_v = send(far_v, far=1)
    near_v = send(near_v, dc=1)
    prob, total = weigh(pos, queries, keys, near_k, far_k, tables)
    return mix(pos, prob, total, values, near_v, far_v, tables[:3])


def solution(mesh):
    in_specs = (
        P(("ctx", "tp"), None),
        P("ctx", "tp"),
        P("ctx", "tp"),
        P("ctx", "tp"),
        P(),
        P(),
        P(),
        P(),
        P(),
        P(),
    )
    out_specs = P("ctx", "tp")
    return jax.shard_map(
        per_device, mesh=mesh, in_specs=in_specs, out_specs=out_specs, check_vma=False
    )
```

```python
import math

import jax
import jax.numpy as jnp
from jax import lax
from jax.experimental import pallas as pl
from jax.experimental.pallas import tpu as pltpu
from jax.sharding import PartitionSpec as P


HD = 128
TILE = 256
NB = 6
SLAB = 64
TPD = 4
HALO = TPD * 2 * SLAB
WIN = 80
NX, NZH, NC, NZL, NY = 4, 4, 2, 2, 4
AXES = ("ctx", "tp")
BF16 = jnp.bfloat16
F32 = jnp.float32


def _index(x, zh, c, zl, y):
    return (((x % NX) * NZH + zh % NZH) * NC + c % NC) * (NZL * NY) + zl % NZL * NY + y % NY


def _moves(dx=0, dzh=0, dc=0, dzl=0, dy=0, sx=0, sz=0):
    pairs = []
    for x in range(NX):
        for zh in range(NZH):
            for c in range(NC):
                for zl in range(NZL):
                    for y in range(NY):
                        pairs.append(
                            (
                                _index(x, zh, c, zl, y),
                                _index(
                                    x + dx + sx * (1 - 2 * c),
                                    zh + dzh + sz * (1 - 2 * c),
                                    c + dc,
                                    zl + dzl,
                                    y + dy,
                                ),
                            )
                        )
    return pairs


def _far_moves():
    blocks = NX * NZH * NC
    tps = NZL * NY
    return [
        (b * tps + t, (b - 1 + 2 * (b % 2)) % blocks * tps + t)
        for b in range(blocks)
        for t in range(tps)
    ]


def send(a, **step):
    return lax.ppermute(a, AXES, _far_moves() if "far" in step else _moves(**step))


SAME = ((0, False, 0),)
OTHER = ((0, False, 1),)
NEAR = ((1, True, 0), (1, True, 1), (2, False, 0))
FAR = ((-1, True, 1), (-1, True, 0), (2, False, 1))


ANY = pl.BlockSpec(memory_space=pl.ANY)
HBM = pl.BlockSpec(memory_space=pltpu.HBM)
SM = pl.BlockSpec(memory_space=pltpu.SMEM)
VM = pl.BlockSpec(memory_space=pltpu.VMEM)
MIB = 1024 * 1024


def join(*parts, space=None):
    rows = [p.shape[0] for p in parts]

    def body(*refs):
        out, sems = refs[-2:]
        copies = []
        for i, ref in enumerate(refs[:-2]):
            copies.append(
                pltpu.make_async_copy(ref, out.at[pl.ds(sum(rows[:i]), rows[i]), :], sems.at[i])
            )
        for cp in copies:
            cp.start()
        for cp in copies:
            cp.wait()

    return pl.pallas_call(
        body,
        out_shape=jax.ShapeDtypeStruct((sum(rows), parts[0].shape[1]), parts[0].dtype),
        in_specs=[space or ANY] * len(parts),
        out_specs=ANY,
        scratch_shapes=[pltpu.SemaphoreType.DMA((len(parts),))],
        compiler_params=pltpu.CompilerParams(vmem_limit_bytes=MIB),
    )(*parts)


def project(pos, toks, tok_at, rows, pieces, fs):
    nt, np_ = len(toks), len(pieces)
    features = fs * NX * NZH * NC
    quarter = features // NX

    def body(*refs):
        pos_ref = refs[0]
        tok_refs = refs[1 : 1 + nt]
        piece_refs = refs[1 + nt : 1 + nt + np_]
        out, w_out, t_buf, w_buf, acc, t_sem, w_sem, o_sem = refs[1 + nt + np_ :]
        x, zh, c = pos_ref[0], pos_ref[1], pos_ref[2]
        steps = (0, 2 * c - 1, 1 - 2 * c, 2)
        at = [(x + step + NX) % NX for step in steps]
        waits = [[] for _ in steps]
        count = 0
        for group in range(NX):
            for ref, (_, xrel, signed, flip, plan) in zip(piece_refs, pieces):
                if (1 + flip if signed else xrel // 2 * 3) != group:
                    continue
                core = (c + flip) % NC
                sign = 2 * core - 1
                for i, (zrel, zsigned, other) in enumerate(plan):
                    zs = (zh + (sign * zrel if zsigned else zrel) + NZH) % NZH
                    place = pl.multiple_of((zs * NC + (core + other) % NC) * fs, 32)
                    for kv in range(2):
                        cp = pltpu.make_async_copy(
                            ref.at[pl.ds((2 * i + kv) * fs, fs), :],
                            w_buf.at[at[group], pl.ds(place, fs), pl.ds(kv * 384, 384)],
                            w_sem.at[count],
                        )
                        cp.start()
                        waits[group].append(cp)
                        count += 1
            if group == 0:
                for i, (ref, (r0, c0)) in enumerate(zip(tok_refs, tok_at)):
                    for k in range(ref.shape[1] // quarter):
                        cp = pltpu.make_async_copy(
                            ref.at[:, pl.ds(k * quarter, quarter)],
                            t_buf.at[c0 // quarter + k, pl.ds(r0, ref.shape[0]), :],
                            t_sem.at[i, k],
                        )
                        cp.start()
                        waits[0].append(cp)
        backs = []
        for q in range(NX):
            for cp in waits[q]:
                cp.wait()
            back = pltpu.make_async_copy(w_buf.at[at[q]], w_out.at[at[q]], o_sem.at[q])
            back.start()
            backs.append(back)
            part = jnp.dot(t_buf[at[q]], w_buf[at[q]], preferred_element_type=F32)
            if q == 0:
                acc[...] = part
            elif q < NX - 1:
                acc[...] += part
            else:
                out[...] = (acc[...] + part).astype(BF16)
        for back in backs:
            back.wait()

    n_copies = 2 * sum(len(p[4]) for p in pieces)
    return pl.pallas_call(
        body,
        out_shape=[
            jax.ShapeDtypeStruct((rows, 768), BF16),
            jax.ShapeDtypeStruct((NX, quarter, 768), BF16),
        ],
        in_specs=[SM] + [HBM] * (nt + np_),
        out_specs=[VM, ANY],
        scratch_shapes=[
            pltpu.VMEM((NX, rows, quarter), BF16),
            pltpu.VMEM((NX, quarter, 768), BF16),
            pltpu.VMEM((rows, 768), F32),
            pltpu.SemaphoreType.DMA((nt, NX)),
            pltpu.SemaphoreType.DMA((n_copies,)),
            pltpu.SemaphoreType.DMA((NX,)),
        ],
        compiler_params=pltpu.CompilerParams(vmem_limit_bytes=36 * MIB),
    )(pos, *toks, *[p[0] for p in pieces])


CHUNKS = 2


def _half_product(toks, w, row0, cols, t_buf, w_buf, t_sem, w_sem, unroll=False):
    n = toks[0].shape[0]
    step = toks[0].shape[1] // CHUNKS

    def copies(k):
        at = k * step if isinstance(k, int) else pl.multiple_of(k * step, 128)
        yield pltpu.make_async_copy(
            w.at[pl.ds(row0 + at, step), pl.ds(*cols)], w_buf.at[k], w_sem.at[k]
        )
        for i, ref in enumerate(toks):
            yield pltpu.make_async_copy(
                ref.at[:, pl.ds(at, step)], t_buf.at[k, pl.ds(i * n, n), :], t_sem.at[k, i]
            )

    for k in range(CHUNKS):
        for cp in copies(k):
            cp.start()

    def product(acc):
        def one(k, carry):
            for cp in copies(k):
                cp.wait()
            acc[...] += jnp.dot(t_buf[k], w_buf[k], preferred_element_type=F32)
            return carry

        if unroll:
            for k in range(CHUNKS):
                one(k, 0)
        else:
            lax.fori_loop(0, CHUNKS, one, 0)

    return product


def _half_scratch(rows, half, width, ntok):
    return [
        pltpu.VMEM((CHUNKS, rows, half // CHUNKS), BF16),
        pltpu.VMEM((CHUNKS, half // CHUNKS, width), BF16),
        pltpu.SemaphoreType.DMA((CHUNKS, ntok)),
        pltpu.SemaphoreType.DMA((CHUNKS,)),
    ]


def project_half(toks, w):
    rows = sum(t.shape[0] for t in toks)
    half = toks[0].shape[1]

    def body(t0, t1, t2, w_ref, acc, t_buf, w_buf, t_sem, w_sem):
        product = _half_product((t0, t1, t2), w_ref, 0, (0, 768), t_buf, w_buf, t_sem, w_sem)
        acc[...] = jnp.zeros_like(acc)
        product(acc)

    return pl.pallas_call(
        body,
        out_shape=jax.ShapeDtypeStruct((rows, 768), F32),
        in_specs=[ANY] * 4,
        out_specs=VM,
        scratch_shapes=_half_scratch(rows, half, 768, 3),
        compiler_params=pltpu.CompilerParams(vmem_limit_bytes=48 * MIB),
    )(*toks, w)


def _tile_at(slot_ref, block, p):
    tile = block * TPD
    for i in range(1, TPD):
        tile = jnp.where(slot_ref[0, block * TPD + i] == block * TPD + p, block * TPD + i, tile)
    return tile


def _aligned(start):
    return jnp.minimum(start // 16 * 16, TILE - WIN)


def project_last(side, pos, toks, w, acc_in, done, done_places, places, tables):
    n, half = toks[0].shape
    rows = n * len(toks)

    def body(pos_ref, t0, t1, t2, w_ref, acc_ref, done_ref, slot, neighbour, first,
             full, near, far, t_buf, w_buf, t_sem, w_sem, acc, wide, a_sem, picks):
        block, zl, y, blocks = pos_ref[3], pos_ref[4], pos_ref[5], pos_ref[6]
        cols = (side * 384, 384)
        begin = pltpu.make_async_copy(acc_ref.at[:, pl.ds(*cols)], acc, a_sem)
        begin.start()
        product = _half_product(
            (t0, t1, t2), w_ref, half, cols, t_buf, w_buf, t_sem, w_sem, unroll=True
        )

        def row_of(place):
            dzl, dy = place
            return pl.multiple_of(((zl + dzl) % NZL * NY + (y + dy + NY) % NY) * n, n)

        for i, place in enumerate(done_places):
            part = done_ref[i * n : (i + 1) * n, side * 384 : side * 384 + 384]
            full[pl.ds(row_of(place), n), :] = part
            wide[pl.ds(row_of(place), n), :] = part.astype(F32)
        up = 1 - 2 * pos_ref[2]
        for d, step in enumerate((-up, up)):
            target = (block + step + blocks) % blocks

            def find(p, carry, d=d, target=target):
                tile = _tile_at(slot, target, p)
                seen = jnp.int32(0)
                starts = [jnp.int32(0), jnp.int32(0)]
                for j in range(NB):
                    other = neighbour[j, tile]
                    hit = other // TPD == block
                    row = slot[0, other] % TPD * TILE + first[j, tile]
                    for o in range(2):
                        take = jnp.logical_and(hit, seen == o)
                        starts[o] = jnp.where(take, row, starts[o])
                    seen = seen + hit.astype(jnp.int32)
                for o in range(2):
                    picks[d * TPD * 2 + p * 2 + o] = starts[o]
                return carry

            lax.fori_loop(0, TPD, find, 0)
        begin.wait()
        product(acc)
        for i, place in enumerate(places):
            part = acc[i * n : (i + 1) * n, :].astype(BF16)
            full[pl.ds(row_of(place), n), :] = part
            wide[pl.ds(row_of(place), n), :] = part.astype(F32)
        for d, out in enumerate((far, near)):

            def pick(i, carry, d=d, out=out):
                start = picks[d * TPD * 2 + i]
                al = pl.multiple_of(start // 8 * 8, 8)
                window = pltpu.roll(
                    wide[pl.ds(al, SLAB + 8), :], (SLAB + 8 - (start - al)) % (SLAB + 8), 0
                )
                at = pl.multiple_of(i * SLAB, SLAB)
                out[pl.ds(at, SLAB), :] = window[:SLAB].astype(BF16)
                return carry

            lax.fori_loop(0, TPD * 2, pick, 0)

    return pl.pallas_call(
        body,
        out_shape=[jax.ShapeDtypeStruct((TPD * TILE, 384), BF16)]
        + [jax.ShapeDtypeStruct((HALO, 384), BF16)] * 2,
        in_specs=[SM] + [ANY] * 5 + [VM] + [SM] * 3,
        out_specs=[VM] * 3,
        scratch_shapes=_half_scratch(rows, half, 384, 3)
        + [pltpu.VMEM((rows, 384), F32), pltpu.VMEM((TPD * TILE + 8, 384), F32)]
        + [pltpu.SemaphoreType.DMA, pltpu.SMEM((TPD * 4,), jnp.int32)],
        compiler_params=pltpu.CompilerParams(vmem_limit_bytes=48 * MIB),
    )(pos, *toks, w, acc_in, done, *tables)


CAND = 768


def _clear_rest(cand):
    cand[pl.ds(TILE + NB * WIN, CAND - TILE - NB * WIN), :] = jnp.zeros(
        (CAND - TILE - NB * WIN, 384), BF16
    )
    for j in range(NB):
        cand[pl.ds(TILE + j * WIN + SLAB, WIN - SLAB), :] = jnp.zeros((WIN - SLAB, 384), BF16)


def _collect(p, pos_ref, slot, neighbour, first, full_ref, near_ref, far_ref, cand):
    block, blocks = pos_ref[3], pos_ref[6]
    tile = _tile_at(slot, block, p)
    own = pl.multiple_of(p * TILE, TILE)
    cand[pl.ds(0, TILE), :] = full_ref[pl.ds(own, TILE), :]
    up = 1 - 2 * pos_ref[2]
    near_block = (block + up + blocks) % blocks
    far_block = (block - up + blocks) % blocks
    seen_near = jnp.int32(0)
    seen_far = jnp.int32(0)
    places = []
    for j in range(NB):
        other = neighbour[j, tile]
        at = other // TPD
        is_near = at == near_block
        is_far = at == far_block
        s = first[j, tile]
        al = _aligned(s)
        c0 = TILE + j * WIN
        begin = slot[0, other] % TPD * TILE + al
        away = jnp.logical_or(is_near, is_far)

        @pl.when(is_near)
        def _(c0=c0, seen=seen_near):
            row = pl.multiple_of((p * 2 + seen) * SLAB, SLAB)
            cand[pl.ds(c0, SLAB), :] = near_ref[pl.ds(row, SLAB), :]

        @pl.when(is_far)
        def _(c0=c0, seen=seen_far):
            row = pl.multiple_of((p * 2 + seen) * SLAB, SLAB)
            cand[pl.ds(c0, SLAB), :] = far_ref[pl.ds(row, SLAB), :]

        @pl.when(jnp.logical_not(away))
        def _(c0=c0, begin=begin):
            cand[pl.ds(c0, WIN), :] = full_ref[pl.ds(pl.multiple_of(begin, 16), WIN), :]

        places.append(c0 + jnp.where(away, 0, s - al))
        seen_near = seen_near + is_near.astype(jnp.int32)
        seen_far = seen_far + is_far.astype(jnp.int32)
    return tile, places


def weigh(pos, queries, full, near_k, far_k, tables):
    scale = 1.0 / math.sqrt(HD)

    def body(pos_ref, q_ref, full_ref, near_ref, far_ref, slot, neighbour, first, length,
             low, high, prob, total, cand):
        p = pl.program_id(0)

        @pl.when(p == 0)
        def _():
            _clear_rest(cand)

        tile, places = _collect(
            p, pos_ref, slot, neighbour, first, full_ref, near_ref, far_ref, cand
        )
        col = lax.broadcasted_iota(jnp.int32, (8, CAND), 1)
        lows = jnp.where(col < TILE, 0, TILE)
        highs = jnp.where(col < TILE, TILE, 0)
        for j in range(NB):
            valid = jnp.logical_and(col >= places[j], col < places[j] + length[j, tile])
            lows = jnp.where(valid, low[j, tile], lows)
            highs = jnp.where(valid, high[j, tile], highs)
        row = lax.broadcasted_iota(jnp.int32, (TILE, CAND - TILE), 0)
        allowed = jnp.logical_and(row >= lows[0:1, TILE:], row < highs[0:1, TILE:])
        raw = [
            lax.dot_general(
                q_ref[:, h * HD : h * HD + HD],
                cand[:, h * HD : h * HD + HD],
                (((1,), (1,)), ((), ())),
                preferred_element_type=F32,
            )
            for h in range(3)
        ]
        for h in range(3):
            cols = slice(h * HD, h * HD + HD)
            scores = raw[h] * scale
            own = scores[:, :TILE]
            slabs = jnp.where(allowed, scores[:, TILE:], -jnp.inf)
            top = jnp.maximum(
                jnp.max(own, axis=-1, keepdims=True), jnp.max(slabs, axis=-1, keepdims=True)
            )
            own = jnp.exp(own - top)
            slabs = jnp.exp(slabs - top)
            total[pl.ds(pl.multiple_of(p * TILE, TILE), TILE), cols] = jnp.broadcast_to(
                jnp.sum(own, axis=-1, keepdims=True) + jnp.sum(slabs, axis=-1, keepdims=True),
                (TILE, HD),
            )
            prob[p, h, :, :TILE] = own.astype(BF16)
            prob[p, h, :, TILE:] = slabs.astype(BF16)

    return pl.pallas_call(
        body,
        grid=(TPD,),
        out_shape=[
            jax.ShapeDtypeStruct((TPD, 3, TILE, CAND), BF16),
            jax.ShapeDtypeStruct((TPD * TILE, 384), F32),
        ],
        in_specs=[SM, pl.BlockSpec((TILE, 384), lambda p: (p, 0)), VM, VM, VM] + [SM] * 6,
        out_specs=[VM, VM],
        scratch_shapes=[pltpu.VMEM((CAND, 384), BF16)],
        compiler_params=pltpu.CompilerParams(vmem_limit_bytes=24 * MIB),
    )(pos, queries, full, near_k, far_k, *tables)


def mix(pos, prob, total, full, near_v, far_v, tables):
    def body(pos_ref, prob_ref, total_ref, full_ref, near_ref, far_ref, slot, neighbour, first,
             out, cand):
        p = pl.program_id(0)

        @pl.when(p == 0)
        def _():
            _clear_rest(cand)

        _collect(p, pos_ref, slot, neighbour, first, full_ref, near_ref, far_ref, cand)
        for h in range(3):
            cols = slice(h * HD, h * HD + HD)
            mixed = jnp.dot(prob_ref[p, h], cand[:, cols], preferred_element_type=F32)
            rows = pl.ds(pl.multiple_of(p * TILE, TILE), TILE)
            out[:, cols] = (mixed / total_ref[rows, cols]).astype(BF16)

    return pl.pallas_call(
        body,
        grid=(TPD,),
        out_shape=jax.ShapeDtypeStruct((TPD * TILE, 384), BF16),
        in_specs=[
            SM,
            VM,
            VM,
            VM,
            VM,
            VM,
        ]
        + [SM] * 3,
        out_specs=pl.BlockSpec((TILE, 384), lambda p: (p, 0)),
        scratch_shapes=[pltpu.VMEM((CAND, 384), BF16)],
        compiler_params=pltpu.CompilerParams(vmem_limit_bytes=24 * MIB),
    )(pos, prob, total, full, near_v, far_v, *tables)


def per_device(
    tokens,
    queries,
    w_key,
    w_value,
    tile_slot,
    neighbour_tile,
    slab_start,
    slab_length,
    window_low,
    window_high,
):
    fs = w_key.shape[0]
    ctx = lax.axis_index("ctx")
    tp = lax.axis_index("tp")
    pos = jnp.stack(
        [ctx >> 3, (ctx >> 1) & 3, ctx & 1, ctx, tp >> 2, tp & 3, jnp.int32(lax.axis_size("ctx"))]
    ).astype(jnp.int32)
    tables = (
        tile_slot.reshape(1, -1),
        neighbour_tile.T,
        slab_start.T,
        slab_length.T,
        window_low.T,
        window_high.T,
    )

    h = tokens.shape[1] // 2
    w = join(w_key, w_value, space=HBM)
    wc = send(w, dc=1)
    ya = send(tokens, dy=1)
    z1w = send(w, sz=1)
    yb = send(tokens, dy=-1)
    wc, tl, tr = lax.optimization_barrier((wc, tokens[:, :h], tokens[:, h:]))
    z1c = send(wc, sz=1)
    xw1 = send(w, sx=1)
    xc1 = send(wc, sx=1)
    z2 = send(z1w, sz=1)
    xw1, pos = lax.optimization_barrier((xw1, pos))
    xw2 = send(xw1, sx=1)
    z_l = send(tl, dzl=1)
    near = join(z1w, z1c, z2)
    xn1 = send(near, sx=1)
    far = send(near, dc=1)
    z_r = send(tr, dzl=1)
    xf1 = send(far, sx=1)
    yo_l = send(ya[:, :h], dy=1)
    yo_r = send(yb[:, h:], dy=-1)
    xn2 = send(xn1, sx=1)
    ua_l = send(z_l, dy=1)
    ub_l = send(z_l, dy=-1)
    uo_l = send(yo_l, dzl=1)
    uo_r = send(yo_r, dzl=1)
    ua_r = send(z_r, dy=1)
    ub_r = send(z_r, dy=-1)
    pieces = [
        (w, 0, False, 0, SAME),
        (wc, 0, False, 0, OTHER),
        (near, 0, False, 0, NEAR),
        (far, 0, False, 0, FAR),
    ]
    for p, xrel, signed, plan in (
        (xw1, 1, True, SAME),
        (xc1, 1, True, OTHER),
        (xw2, 2, False, SAME),
        (xn1, 1, True, NEAR),
        (xf1, 1, True, FAR),
        (xn2, 2, False, NEAR),
    ):
        pieces += [(p, xrel, signed, 0, plan), (send(p, dc=1), xrel, signed, 1, plan)]

    n = tokens.shape[0]
    toks = (tokens, ya, yb, yo_l, yo_r, z_l, z_r)
    at = ((0, 0), (n, 0), (2 * n, 0), (3 * n, 0), (3 * n, h), (4 * n, 0), (4 * n, h))
    kv1, w_all = project(pos, toks, at, 5 * n, pieces, fs)
    w_all = w_all.reshape(tokens.shape[1], 768)
    part = project_half((ua_l, ub_l, uo_l), w_all)
    rest = (ua_r, ub_r, uo_r)
    last = (
        kv1,
        ((0, 0), (0, -1), (0, 1), (0, 2), (1, 0)),
        ((1, -1), (1, 1), (1, 2)),
        tables[:3],
    )
    keys, near_k, far_k = project_last(0, pos, rest, w_all, part, *last)
    part = lax.optimization_barrier((part, far_k))[0]
    far_k = send(far_k, far=1)
    near_k = send(near_k, dc=1)
    values, near_v, far_v = project_last(1, pos, rest, w_all, part, *last)
    far_v = send(far_v, far=1)
    near_v = send(near_v, dc=1)
    prob, total = weigh(pos, queries, keys, near_k, far_k, tables)
    return mix(pos, prob, total, values, near_v, far_v, tables[:3])


def solution(mesh):
    in_specs = (
        P(("ctx", "tp"), None),
        P("ctx", "tp"),
        P("ctx", "tp"),
        P("ctx", "tp"),
        P(),
        P(),
        P(),
        P(),
        P(),
        P(),
    )
    out_specs = P("ctx", "tp")
    return jax.shard_map(
        per_device, mesh=mesh, in_specs=in_specs, out_specs=out_specs, check_vma=False
    )
```
